32 devices in a mesh: parts: 32 (over z, y, x, core).
Axes of the slice: x: 2, y: 2, z: 4, core: 2. Of those that a mesh axis runs over, the one named last changes fastest.
Arguments:
- basis: float32 [16, 32768], P(None, 'parts'), may hold values from -8000 to 8000, as said below
- k_tiles: float32 [256, 5, 128, 128], P('parts'), may hold values from -3 to 11, as said below
- m_tiles: float32 [256, 5, 128, 128], P('parts'), may hold values from -2 to 4, as said below
- tile_part: int32 [256, 5], P('parts'), may hold values from 0 to 31, as said below
- tile_slot: int32 [256, 5], P('parts'), may hold values from 0 to 7, as said below
- iface_rows: int32 [64], P('parts'), may hold values from 0 to 7
Outputs:
- corrections: float32 [16, 32768], P(None, 'parts')
- theta: float32 [16], replicated
The draws below stay inside these ranges and needn't reach their ends.
Inputs may be any that keep to these rules, and one draw needn't show every extreme that they name: `basis`: the rows form a full-rank set. `k_tiles`: block 0 of every row tile has a positive diagonal well above its other entries. `m_tiles`: block 0 of every row tile has a positive diagonal. `tile_part`: block 0 of a row tile lies in its own partition; every other block lies in its own partition, in the partition 1 away on either side, or in the partition 16 away, counted modulo the number of partitions. `tile_slot`: where the block lies in the own partition this is a row tile of it (for block 0 the row tile itself); elsewhere an interface slot below 2.
All inputs are finite; a program needn't handle non-finite values.
Results may differ from the reference program's by a relative error of at most 0.0003.
Values sent between devices are 32-bit elements; how exact they have to be, the bound alone decides.
No kernel may reach another device: no remote copies, remote signals or barrier semaphores. Data moves between devices by JAX's collectives and lax.ppermute only.
A program may use at most 64 MiB of HBM per device.

```python
import jax
import jax.numpy as jnp
from jax import lax

PAIRS = 16
TILE = 128
BLOCKS = 5
STEPS = 4
IFACE = 2
TILES_DEV = 8
STRIDE = 16
ROW_TILES = 256
ROWS = 32768
N_PARTS = 32


def draw_basis(key, part):
    keys = jax.random.split(key, 3)
    values = jax.random.truncated_normal(keys[0], -5.0, 5.0, (PAIRS, ROWS), jnp.float32)
    power = 1.0
    column_scale = jnp.exp(jax.random.uniform(keys[1], (PAIRS, 1), jnp.float32, 0.0, 2.3026))
    tile_scale = jnp.exp(jax.random.uniform(keys[2], (1, ROW_TILES), jnp.float32, 0.0, 2.3026))
    tile_scale = jnp.repeat(tile_scale, TILE, axis=1)
    place = (jnp.arange(ROWS, dtype=jnp.int32) // (TILES_DEV * TILE)).astype(jnp.float32)
    ramp = (3.0 ** (place / (N_PARTS - 1))) ** power
    return values * column_scale * tile_scale * ramp[None, :]


def operator_like(key, ratio, lowest, highest):
    keys = jax.random.split(key, 2)
    spread = ratio / (BLOCKS * TILE) ** 0.5
    shape = (ROW_TILES, BLOCKS, TILE, TILE)
    entries = jax.random.truncated_normal(keys[0], -5.0, 5.0, shape, jnp.float32) * spread
    diagonal = jax.random.uniform(keys[1], (ROW_TILES, TILE), jnp.float32, lowest, highest)
    eye = jnp.eye(TILE, dtype=jnp.float32)
    return entries.at[:, 0].add(diagonal[:, :, None] * eye[None])


def draw_k_tiles(key, part):
    return operator_like(jax.random.fold_in(key, 11), 3.0, 4.0, 8.0)


def draw_m_tiles(key, part):
    return operator_like(jax.random.fold_in(key, 13), 0.75, 1.0, 2.0)


def tile_pattern(key):
    keys = jax.random.split(jax.random.fold_in(key, 7), 4)
    shape = (ROW_TILES, BLOCKS)
    owner = (jnp.arange(ROW_TILES, dtype=jnp.int32) // TILES_DEV)[:, None]
    own_tile = (jnp.arange(ROW_TILES, dtype=jnp.int32) % TILES_DEV)[:, None]
    first = jnp.arange(BLOCKS, dtype=jnp.int32)[None, :] == 0
    coin = jax.random.randint(keys[0], shape, 0, 2) == 1
    remote = jnp.logical_and(coin, jnp.logical_not(first))
    direction = jax.random.randint(keys[1], shape, 0, 4)
    offsets = jnp.where(direction == 0, 1, jnp.where(direction == 1, -1, jnp.where(direction == 2, STRIDE, -STRIDE)))
    neighbour = (owner + offsets + N_PARTS) % N_PARTS
    local_slot = jax.random.randint(keys[2], shape, 0, TILES_DEV)
    iface_slot = jax.random.randint(keys[3], shape, 0, IFACE)
    parts_of = jnp.where(remote, neighbour, owner + 0 * neighbour)
    slots = jnp.where(remote, iface_slot, jnp.where(first, own_tile + 0 * local_slot, local_slot))
    return (parts_of.astype(jnp.int32), slots.astype(jnp.int32))


def draw_tile_part(key, part):
    return tile_pattern(key)[0]


def draw_tile_slot(key, part):
    return tile_pattern(key)[1]


def with_ends(result, stream_key, least, largest):
    longest = result.shape.index(max(result.shape))
    spots = []
    for shift in (0, 1):
        where = [jax.random.randint(jax.random.fold_in(stream_key, axis), (), 0, length) for axis, length in enumerate(result.shape)]
        where[longest] = (where[longest] + shift) % result.shape[longest]
        spots.append(tuple(where))
    return result.at[spots[0]].set(least).at[spots[1]].set(largest)


def setup_inputs(seed: int = 0) -> dict:
    key_list = jax.random.split(jax.random.key(seed), 7)
    basis = draw_basis(jax.random.fold_in(key_list[6], 71), 0)
    k_tiles = draw_k_tiles(jax.random.fold_in(key_list[6], 71), 0)
    m_tiles = draw_m_tiles(jax.random.fold_in(key_list[6], 71), 0)
    tile_part = draw_tile_part(jax.random.fold_in(key_list[6], 71), 0)
    tile_slot = draw_tile_slot(jax.random.fold_in(key_list[6], 71), 0)
    iface_rows = with_ends(jax.random.randint(key_list[5], (N_PARTS * IFACE,), 0, TILES_DEV), jax.random.fold_in(key_list[5], 1), 0, TILES_DEV - 1).astype(jnp.int32)
    return {"basis": basis, "k_tiles": k_tiles, "m_tiles": m_tiles, "tile_part": tile_part, "tile_slot": tile_slot, "iface_rows": iface_rows}


relax = 0.4

def product(left, right):
    return jnp.dot(left.astype(jnp.float32), right.astype(jnp.float32), precision=lax.Precision.HIGHEST, preferred_element_type=jnp.float32)

def inverse_lower(chol):
    eye = jnp.eye(chol.shape[0], dtype=chol.dtype)
    return jax.scipy.linalg.solve_triangular(chol, eye, lower=True)

def apply_pair(vectors, k_tiles, m_tiles, columns):
    blocks = vectors.reshape(PAIRS, ROW_TILES, TILE)
    picked = jnp.take(blocks, columns, axis=1)
    stiff = jnp.einsum('ptbc,tbrc->ptr', picked, k_tiles, precision=lax.Precision.HIGHEST)
    mass = jnp.einsum('ptbc,tbrc->ptr', picked, m_tiles, precision=lax.Precision.HIGHEST)
    return (stiff.reshape(PAIRS, ROWS), mass.reshape(PAIRS, ROWS))

def reference(basis, k_tiles, m_tiles, tile_part, tile_slot, iface_rows):
    owner = (jnp.arange(ROW_TILES, dtype=jnp.int32) // TILES_DEV)[:, None]
    lookup = jnp.clip(tile_part * IFACE + tile_slot, 0, N_PARTS * IFACE - 1).astype(jnp.int32)
    remote_tile = jnp.take(iface_rows, lookup)
    columns = (tile_part * TILES_DEV + jnp.where(tile_part == owner, tile_slot, remote_tile)).astype(jnp.int32)
    gram = product(basis, basis.T) / ROWS
    inv_v = inverse_lower(jnp.linalg.cholesky(gram))
    ortho = product(inv_v, basis)
    k_ortho, m_ortho = apply_pair(ortho, k_tiles, m_tiles, columns)
    mass_gram = product(m_ortho, m_ortho.T) / ROWS
    stiff_cross = product(m_ortho, k_ortho.T) / ROWS
    chol_b = jnp.linalg.cholesky(mass_gram)
    inv_b = inverse_lower(chol_b)
    test_basis = product(inv_b, m_ortho)
    theta = jnp.diagonal(product(inv_b, stiff_cross)) / jnp.diagonal(chol_b)
    resid = k_ortho - theta[:, None] * m_ortho
    diag_k = jnp.diagonal(k_tiles[:, 0], axis1=1, axis2=2).reshape(ROWS)
    correct = -relax * resid / diag_k
    for step in range(STEPS):
        right = product(correct, ortho.T) / ROWS
        moved = correct - product(right, ortho)
        k_moved, m_moved = apply_pair(moved, k_tiles, m_tiles, columns)
        image = k_moved - theta[:, None] * m_moved
        left = product(image, test_basis.T) / ROWS
        image = image - product(left, test_basis)
        correct = correct - relax * (resid + image) / diag_k
    final = product(correct, ortho.T) / ROWS
    correct = correct - product(final, ortho)
    return (correct, theta)
```

```python
import jax
import jax.numpy as jnp
from jax import lax
from jax.experimental import pallas as pl
from jax.experimental.pallas import tpu as pltpu
from jax.sharding import PartitionSpec as P

relax = 0.4

F32 = jnp.float32
BF16 = jnp.bfloat16
VM = pl.BlockSpec(memory_space=pltpu.VMEM)
SM = pl.BlockSpec(memory_space=pltpu.SMEM)
MAT = 128


def call(kernel, name, outs, specs, scratch=()):
    return pl.pallas_call(
        kernel,
        name=name,
        in_specs=specs,
        out_specs=[VM] * len(outs),
        out_shape=[jax.ShapeDtypeStruct(shape, dtype) for shape, dtype in outs],
        scratch_shapes=list(scratch),
        compiler_params=pltpu.CompilerParams(vmem_limit_bytes=24 << 20),
    )


def mm(left, right):
    return jnp.dot(left, right, precision=lax.Precision.HIGHEST, preferred_element_type=F32)


def nt(left, right):
    return lax.dot_general(
        left, right, (((1,), (1,)), ((), ())), precision=lax.Precision.HIGHEST, preferred_element_type=F32
    )


def split(value):
    high = value.astype(BF16)
    return high, (value - high.astype(F32)).astype(BF16)


def rows(parts):
    return jnp.concatenate(parts, axis=0)


def lanes(parts):
    return jnp.concatenate(parts, axis=1)


def halo_lanes(refs, first, last):
    return lanes([ref[slot, first:last] for ref in refs for slot in range(ref.shape[0])])


def put_sources(xs, at, value):
    n, width = value.shape[0], xs.shape[2]
    for t in range(value.shape[1] // width):
        high, low = split(value[:, t * width : (t + 1) * width])
        xs[at + t, :n] = high
        xs[at + t, n:] = low


def apply_pair(xs, cols, w_high, w_low, k_out, m_out):
    tiles, blocks = cols.shape
    width = xs.shape[2]
    n = xs.shape[1] // 2
    for i in range(tiles):
        lhs = lanes([xs[cols[i, b]] for b in range(blocks)])
        dims = (((1,), (1,)), ((), ()))
        both = lax.dot_general(lhs, w_high[i], dims, preferred_element_type=F32)
        low = lax.dot_general(lhs[:n], w_low[i], dims, preferred_element_type=F32)
        result = both[:n] + both[n:] + low
        k_out[:, i * width : (i + 1) * width] = result[:, :width]
        m_out[:, i * width : (i + 1) * width] = result[:, width:]


def send_tiles(iface, outgoing, at, ref):
    width = outgoing.shape[2]
    n = ref.shape[0]
    for slot in range(outgoing.shape[0]):
        start = pl.multiple_of(iface[slot] * width, width)
        outgoing[slot, at : at + n] = ref[:, pl.ds(start, width)]


def lane_row(shape):
    return lax.broadcasted_iota(jnp.int32, shape, 1), lax.broadcasted_iota(jnp.int32, shape, 0)


def blocks_of(summed, n):
    square = rows([summed, jnp.zeros((MAT - n, MAT), F32)])
    turned = square.T
    return [turned[k * n : (k + 1) * n] for k in range(MAT // n)]


def inverse_chols(grams):
    n = grams[0].shape[0]
    lane, row = lane_row(grams[0].shape)
    states = [g + jnp.where(lane == row + n, 1.0, 0.0) for g in grams]
    for k in range(n - 1):
        for index, a in enumerate(states):
            pivot_row = a[k : k + 1, :]
            factor = a[:, k : k + 1] * (1.0 / a[k : k + 1, k : k + 1])
            states[index] = a - jnp.where(row > k, factor, 0.0) * pivot_row
    out = []
    for a in states:
        pivots = jnp.sum(jnp.where(lane == row, a, 0.0), axis=1, keepdims=True)
        moved = pltpu.roll(a, MAT - n, 1)
        out.append(jnp.where(lane < n, moved, 0.0) * lax.rsqrt(pivots))
    return out


def diagonal(a):
    lane, row = lane_row(a.shape)
    return jnp.sum(jnp.where(lane == row, a, 0.0), axis=1, keepdims=True)


def k_first(iface, basis, outgoing):
    send_tiles(iface, outgoing, 0, basis)


def k_prep(k, m, w_high, w_low, inv_d):
    tiles, blocks, width, _ = k.shape
    row = lax.broadcasted_iota(jnp.int32, (width, width), 0)
    lane = lax.broadcasted_iota(jnp.int32, (width, width), 1)
    for i in range(tiles):
        for b in range(blocks):
            high, low = split(k[i, b])
            w_high[i, :width, b * width : (b + 1) * width] = high
            w_low[i, :width, b * width : (b + 1) * width] = low
            high, low = split(m[i, b])
            w_high[i, width:, b * width : (b + 1) * width] = high
            w_low[i, width:, b * width : (b + 1) * width] = low
        diag = jnp.sum(jnp.where(row == lane, k[i, 0], 0.0), axis=0, keepdims=True)
        inv_d[:, i * width : (i + 1) * width] = 1.0 / diag


def fill_blocks(out, value):
    for device in range(out.shape[0]):
        out[device] = value


def total(ref):
    value = ref[0]
    for device in range(1, ref.shape[0]):
        value = value + ref[device]
    return value


def fold(value):
    half = value.shape[0] // 2
    return value[:half] + pltpu.roll(value[half:], MAT // 2, 1)


def unfold(value):
    lane, _ = lane_row(value.shape)
    keep = lane < MAT // 2
    return rows([jnp.where(keep, value, 0.0), jnp.where(keep, pltpu.roll(value, MAT // 2, 1), 0.0)])


def make_kernels(n, scale):
    def k_a(cols, iface, basis, h_a, h_b, h_f, w_high, w_low, inv_d, kb, mb, u, outgoing, grams, xs):
        put_sources(xs, 0, basis[...])
        put_sources(xs, basis.shape[1] // xs.shape[2], halo_lanes((h_a, h_b, h_f), 0, n))
        apply_pair(xs, cols, w_high, w_low, kb, mb)
        d = inv_d[...]
        u[:n] = kb[...] * d
        u[n:] = mb[...] * d
        send_tiles(iface, outgoing, 0, u)
        right = rows([basis[...], u[...], mb[...], kb[...], jnp.zeros((MAT - 5 * n, basis.shape[1]), F32)])
        both = nt(rows([basis[...], mb[...]]), right) * scale
        lane, _ = lane_row((n, MAT))
        fill_blocks(grams, jnp.where(lane < 3 * n, both[:n], both[n:]))

    def k_b(
        cols, iface, red, basis, kb, mb, u, h_a, h_b, h_f, w_high, w_low, inv_d,
        p_out, image_out, v_out, t_out, ko_out, mo_out, c0_out, words, words_halo, kf_out, small, outgoing,
        theta_out, xs, res,
    ):
        g_bb, g_u1b, g_u2b, g_mm, g_km = blocks_of(total(red), n)[:5]
        inv_v, inv_c = inverse_chols([g_bb, g_mm])
        lv, lc = inv_v[:, :n], inv_c[:, :n]
        cross = nt(mm(lv, g_km[:, :n]), lc)
        mass = nt(mm(lv, g_mm[:, :n]), lc)
        theta = diagonal(cross) * diagonal(inv_c) / diagonal(inv_v)
        e1 = nt(mm(lv, g_u1b[:, :n]), lv)
        e2 = nt(mm(lv, g_u2b[:, :n]), lv)
        ef = nt(mm(lc, g_u2b[:, :n]), lv)
        right = -relax * (e1 - theta * e2)
        pad = jnp.zeros((n, MAT - n), F32)
        for k, value in enumerate((cross, mass, e1, e2, ef)):
            small[k * n : (k + 1) * n] = lanes([value, pad])
        small[5 * n : 6 * n] = jnp.broadcast_to(theta, (n, MAT))
        lane, row = lane_row((n, MAT))
        theta_out[...] = jnp.sum(jnp.where(lane == row, theta, 0.0), axis=0, keepdims=True)[:, :n]
        local = basis.shape[1]
        tiles = local // xs.shape[2]
        u1 = lanes([u[:n], halo_lanes((h_a, h_b, h_f), 0, n)])
        u2 = lanes([u[n:], halo_lanes((h_a, h_b, h_f), n, 2 * n)])
        g1 = mm(lv, u1)
        both = mm(rows([lv, lc]), u2)
        g2, f1 = both[:n], both[n:]
        c0 = -relax * (g1 - theta * g2)
        put_sources(xs, 0, rows([c0, f1]))
        apply_pair(xs, cols, w_high, w_low, res.at[0], res.at[1])
        for k, value in ((0, f1), (3, g1), (4, g2)):
            words[k * n : (k + 1) * n] = value[:, :local]
        for k, value in ((0, f1), (1, g1), (2, g2)):
            words_halo[k * n : (k + 1) * n] = value[:, local:]
        c0_out[...] = c0[:, :local]
        ko = mm(lv, kb[...])
        both = mm(rows([lv, lc]), mb[...])
        mo = both[:n]
        t_out[...] = both[n:]
        ko_out[...] = ko
        mo_out[...] = mo
        v_out[...] = mm(lv, basis[...])
        d = inv_d[...]
        image = res[0, :n] - theta * res[1, :n] - mm(lanes([right, -theta * right]), rows([ko, mo]))
        image_out[...] = image
        kf_out[:n] = res[0, n:]
        kf_out[n:] = res[1, n:]
        words[n : 2 * n] = res[0, n:] * d
        words[2 * n : 3 * n] = res[1, n:] * d
        p_out[...] = 2.0 * c0[:, :local] - relax * d * image
        send_tiles(iface, outgoing, 0, p_out)
        send_tiles(iface, outgoing, n, words.at[n : 3 * n])

    def half(cols, p, halo, small, c0, w_high, w_low, inv_d, xs, res):
        put_sources(xs, 0, p)
        put_sources(xs, p.shape[1] // xs.shape[2], halo)
        apply_pair(xs, cols, w_high, w_low, res.at[0], res.at[1])
        theta = small[5 * n : 6 * n, :1]
        image = res[0] - theta * res[1]
        return image, p + c0[...] - relax * inv_d[...] * image

    def k_c(
        cols, iface, p, h_a, h_b, h_f, image0, v, t, c0, words, kf, small, w_high, w_low, inv_d,
        p_out, outgoing, grams, xs, res,
    ):
        image, fresh = half(
            cols, p[...], halo_lanes((h_a, h_b, h_f), 0, n), small, c0, w_high, w_low, inv_d, xs, res
        )
        p_out[...] = fresh
        send_tiles(iface, outgoing, 0, p_out)
        right = rows([image0[...], kf[...], image, p[...], words[n : 3 * n], fresh])
        both = nt(rows([t[...], v[...]]), right) * scale
        lane, _ = lane_row((n, MAT))
        fill_blocks(grams, jnp.where(lane < 4 * n, both[:n], both[n:]))

    def solve(small, g_left, g_kf, g_mf, g_a, g_p, g_h1, g_h2, g_fresh):
        cross, mass, e1, e2, ef = (small[k * n : (k + 1) * n, :n] for k in range(5))
        theta = small[5 * n : 6 * n, :1]
        right = g_p + relax * mm(g_left, ef)
        left = (
            g_a
            + mm(lanes([relax * g_left, -relax * theta * g_left]), rows([g_kf, g_mf]))
            + mm(lanes([-right, theta * right]), rows([cross, mass]))
        )
        coef = lanes(
            [
                relax * (g_left + left),
                -relax * relax * g_left,
                relax * relax * theta * g_left,
                relax * right,
                -relax * theta * right,
            ]
        )
        after = g_fresh + mm(coef, rows([ef, g_h1, g_h2, e1, e2]))
        return coef, after

    def k_d(
        cols, iface, red, p, h_a, h_b, h_f, q_a, q_b, q_f, ko, mo, c0, words, words_halo, small,
        w_high, w_low, inv_d, p_out, image_out, words_grams, outgoing, xs, res,
    ):
        g = [value[:, :n] for value in blocks_of(total(red), n)]
        g_left, g_kf, g_mf, g_a, g_p, g_h1, g_h2, g_fresh = g
        pad = jnp.zeros((n, MAT - n), F32)
        for k, value in enumerate((g_kf, g_mf, g_h1, g_h2)):
            words_grams[k * n : (k + 1) * n] = lanes([value, pad])
        coef, right = solve(small, *g)
        theta = small[5 * n : 6 * n, :1]
        local = p.shape[1]
        c_local = p[...] + mm(coef, words[...])
        around = rows([words_halo[:n], halo_lanes((q_a, q_b, q_f), n, 3 * n), words_halo[n:]])
        c_halo = halo_lanes((h_a, h_b, h_f), 0, n) + mm(coef, around)
        put_sources(xs, 0, c_local)
        put_sources(xs, local // xs.shape[2], c_halo)
        apply_pair(xs, cols, w_high, w_low, res.at[0], res.at[1])
        image = res[0] - theta * res[1] - mm(lanes([right, -theta * right]), rows([ko[...], mo[...]]))
        image_out[...] = image
        p_out[...] = c_local + c0[...] - relax * inv_d[...] * image
        send_tiles(iface, outgoing, 0, p_out)

    def k_e(
        cols, p, h_a, h_b, h_f, image2, v, t, c0, small, w_high, w_low, inv_d, p_out, grams, xs, res
    ):
        image, fresh = half(
            cols, p[...], halo_lanes((h_a, h_b, h_f), 0, n), small, c0, w_high, w_low, inv_d, xs, res
        )
        p_out[...] = fresh
        right = rows([image2[...], image, p[...], fresh, jnp.zeros((MAT - 4 * n, p.shape[1]), F32)])
        both = nt(rows([t[...], v[...]]), right) * scale
        lane, _ = lane_row((n, MAT))
        fill_blocks(grams, fold(jnp.where(lane < 2 * n, both[:n], both[n:])))

    def k_f(red, p, v, words, small, words_grams, out):
        g_left, g_a, g_p, g_fresh = (value[:, :n] for value in blocks_of(unfold(total(red)), n)[:4])
        g_kf, g_mf, g_h1, g_h2 = (words_grams[k * n : (k + 1) * n, :n] for k in range(4))
        coef, right = solve(small, g_left, g_kf, g_mf, g_a, g_p, g_h1, g_h2, g_fresh)
        out[...] = p[...] + mm(lanes([coef, -right]), rows([words[...], v[...]]))

    return k_a, k_b, k_c, k_d, k_e, k_f


def shards(basis, k_tiles, m_tiles, tile_part, tile_slot, iface):
    n, local = basis.shape
    tiles, blocks, width, _ = k_tiles.shape
    count = iface.shape[0]
    parts = lax.axis_size("parts")
    me = lax.axis_index("parts")
    half_way = parts // 2
    scale = 1.0 / (local * parts)
    chip = [(source, source ^ 1) for source in range(parts)]
    other = [(source, (source + 1 if source % 2 else source - 1) % parts) for source in range(parts)]
    far = [(source, (source + half_way) % parts) for source in range(parts)]

    remote = jnp.where(
        tile_part == me ^ 1, 0, jnp.where(tile_part == (me + half_way) % parts, 2 * count, count)
    )
    cols = jnp.where(tile_part == me, tile_slot, tiles + remote + tile_slot)

    def halo(outgoing):
        return [lax.ppermute(outgoing, "parts", pairs) for pairs in (chip, other, far)]

    def reduced(blocks_out):
        return lax.all_to_all(blocks_out, "parts", 0, 0, tiled=True)

    k_a, k_b, k_c, k_d, k_e, k_f = make_kernels(n, scale)
    sources = tiles + 3 * count
    xs = lambda m: pltpu.VMEM((sources, 2 * m, width), BF16)
    vec = ((n, local), F32)
    out = lambda m: ((count, m, width), F32)
    grams16 = ((parts, n, MAT), F32)
    grams8 = ((parts, n // 2, MAT), F32)

    (outgoing,) = call(k_first, "first", [out(n)], [SM, VM])(iface, basis)
    h0 = halo(outgoing)
    w_high, w_low, inv_d = call(
        k_prep,
        "prep",
        [((tiles, 2 * width, blocks * width), BF16)] * 2 + [((1, local), F32)],
        [VM, VM],
    )(k_tiles, m_tiles)
    w = (w_high, w_low, inv_d)
    kb, mb, u, outgoing, grams = call(
        k_a, "level0", [vec, vec, ((2 * n, local), F32), out(2 * n), grams16], [SM, SM] + [VM] * 7, [xs(n)]
    )(cols, iface, basis, *h0, *w)
    red = reduced(grams)
    h1 = halo(outgoing)
    p1, image0, v, t, ko, mo, c0, words, words_halo, kf, small, outgoing, theta = call(
        k_b,
        "level1",
        [vec] * 7
        + [((5 * n, local), F32), ((3 * n, 3 * count * width), F32), ((2 * n, local), F32)]
        + [((6 * n, MAT), F32), out(3 * n), ((1, n), F32)],
        [SM, SM] + [VM] * 11,
        [xs(2 * n), pltpu.VMEM((2, 2 * n, local), F32)],
    )(cols, iface, red, basis, kb, mb, u, *h1, *w)
    h2 = halo(outgoing)
    res = pltpu.VMEM((2, n, local), F32)
    p2, outgoing, grams = call(k_c, "level2", [vec, out(n), grams16], [SM, SM] + [VM] * 14, [xs(n), res])(
        cols, iface, p1, *h2, image0, v, t, c0, words, kf, small, *w
    )
    red = reduced(grams)
    h3 = halo(outgoing)
    p3, image2, words_grams, outgoing = call(
        k_d, "level3", [vec, vec, ((4 * n, MAT), F32), out(n)], [SM, SM] + [VM] * 17, [xs(n), res]
    )(cols, iface, red, p2, *h3, *h2, ko, mo, c0, words, words_halo, small, *w)
    h4 = halo(outgoing)
    p4, grams = call(k_e, "level4", [vec, grams8], [SM] + [VM] * 12, [xs(n), res])(
        cols, p3, *h4, image2, v, t, c0, small, *w
    )
    red = reduced(grams)
    (correct,) = call(k_f, "last", [vec], [VM] * 6)(red, p4, v, words, small, words_grams)
    return (correct, theta.reshape(-1))


def solution(mesh):
    placed = (
        P(None, "parts"),
        P("parts", None, None, None),
        P("parts", None, None, None),
        P("parts", None),
        P("parts", None),
        P("parts"),
    )
    return jax.shard_map(
        shards, mesh=mesh, in_specs=placed, out_specs=(P(None, "parts"), P()), check_vma=False
    )
```

```python
import jax
import jax.numpy as jnp
from jax import lax
from jax.experimental import pallas as pl
from jax.experimental.pallas import tpu as pltpu
from jax.sharding import PartitionSpec as P

relax = 0.4

F32 = jnp.float32
BF16 = jnp.bfloat16
VM = pl.BlockSpec(memory_space=pltpu.VMEM)
SM = pl.BlockSpec(memory_space=pltpu.SMEM)
HBM = pl.BlockSpec(memory_space=pltpu.MemorySpace.HBM)
MAT = 128


def call(kernel, outs, specs, scratch=()):
    return pl.pallas_call(
        kernel,
        in_specs=specs,
        out_specs=[VM] * len(outs),
        out_shape=[jax.ShapeDtypeStruct(shape, dtype) for shape, dtype in outs],
        scratch_shapes=list(scratch),
        compiler_params=pltpu.CompilerParams(vmem_limit_bytes=24 << 20),
    )


def in_hbm(value):
    return pltpu.with_memory_space_constraint(value, pltpu.MemorySpace.HBM)


def mm(left, right):
    return jnp.dot(left, right, precision=lax.Precision.HIGHEST, preferred_element_type=F32)


def nt(left, right):
    return lax.dot_general(
        left, right, (((1,), (1,)), ((), ())), precision=lax.Precision.HIGHEST, preferred_element_type=F32
    )


def split(value):
    high = value.astype(BF16)
    return high, (value - high.astype(F32)).astype(BF16)


def rows(parts):
    return jnp.concatenate(parts, axis=0)


def lanes(parts):
    return jnp.concatenate(parts, axis=1)


def halo_lanes(refs, first, last):
    return lanes([ref[slot, first:last] for ref in refs for slot in range(ref.shape[0])])


def put_sources(xs, at, value):
    n, width = value.shape[0], xs.shape[2]
    for t in range(value.shape[1] // width):
        high, low = split(value[:, t * width : (t + 1) * width])
        xs[at + t, :n] = high
        xs[at + t, n:] = low


def apply_pair(xs, cols, w_high, w_low, k_out, m_out):
    tiles, blocks = cols.shape
    width = xs.shape[2]
    n = xs.shape[1] // 2
    for i in range(tiles):
        lhs = lanes([xs[cols[i, b]] for b in range(blocks)])
        both = jnp.dot(lhs, w_high[i], preferred_element_type=F32)
        low = jnp.dot(lhs[:n], w_low[i], preferred_element_type=F32)
        result = both[:n] + both[n:] + low
        k_out[:, i * width : (i + 1) * width] = result[:, :width]
        m_out[:, i * width : (i + 1) * width] = result[:, width:]


def send_tiles(iface, outgoing, at, ref):
    width = outgoing.shape[2]
    n = ref.shape[0]
    for slot in range(outgoing.shape[0]):
        start = pl.multiple_of(iface[slot] * width, width)
        outgoing[slot, at : at + n] = ref[:, pl.ds(start, width)]


def lane_row(shape):
    return lax.broadcasted_iota(jnp.int32, shape, 1), lax.broadcasted_iota(jnp.int32, shape, 0)


def blocks_of(summed, n):
    square = rows([summed, jnp.zeros((MAT - n, MAT), F32)])
    turned = square.T
    return [turned[k * n : (k + 1) * n] for k in range(MAT // n)]


def inverse_chols(grams):
    n = grams[0].shape[0]
    lane, row = lane_row(grams[0].shape)
    states = [g + jnp.where(lane == row + n, 1.0, 0.0) for g in grams]
    for k in range(n - 1):
        for index, a in enumerate(states):
            pivot_row = a[k : k + 1, :]
            factor = a[:, k : k + 1] * (1.0 / a[k : k + 1, k : k + 1])
            states[index] = a - jnp.where(row > k, factor, 0.0) * pivot_row
    out = []
    for a in states:
        pivots = jnp.sum(jnp.where(lane == row, a, 0.0), axis=1, keepdims=True)
        moved = pltpu.roll(a, MAT - n, 1)
        out.append(jnp.where(lane < n, moved, 0.0) * lax.rsqrt(pivots))
    return out


def diagonal(a):
    lane, row = lane_row(a.shape)
    return jnp.sum(jnp.where(lane == row, a, 0.0), axis=1, keepdims=True)


def k_first(iface_hbm, basis, outgoing, iface, sems):
    copy = pltpu.make_async_copy(iface_hbm, iface, sems.at[0])
    copy.start()
    copy.wait()
    width = outgoing.shape[2]
    copies = []
    for slot in range(outgoing.shape[0]):
        start = pl.multiple_of(iface[slot] * width, width)
        copy = pltpu.make_async_copy(basis.at[:, pl.ds(start, width)], outgoing.at[slot], sems.at[slot])
        copy.start()
        copies.append(copy)
    for copy in copies:
        copy.wait()


def make_prep(count):
    def k_prep(part_hbm, slot_hbm, k_hbm, m_hbm, w_high, w_low, inv_d, cols, k, m, part_in, slot_in, sems):
        tiles, blocks, width, _ = k.shape
        pattern = [
            pltpu.make_async_copy(source, target, sems.at[which, tiles])
            for which, (source, target) in enumerate(((part_hbm, part_in), (slot_hbm, slot_in)))
        ]
        for copy in pattern:
            copy.start()
        copies = []
        for i in range(tiles):
            pair = [
                pltpu.make_async_copy(source.at[i], target.at[i], sems.at[which, i])
                for which, (source, target) in enumerate(((k_hbm, k), (m_hbm, m)))
            ]
            for copy in pair:
                copy.start()
            copies.append(pair)
        parts = lax.axis_size("parts")
        me = lax.axis_index("parts")
        for copy in pattern:
            copy.wait()
        part, slot = part_in[...], slot_in[...]
        remote = jnp.where(part == me ^ 1, 0, jnp.where(part == (me + parts // 2) % parts, count, 2 * count))
        cols[...] = jnp.where(part == me, slot, tiles + remote + slot)
        row = lax.broadcasted_iota(jnp.int32, (width, width), 0)
        lane = lax.broadcasted_iota(jnp.int32, (width, width), 1)
        for i in range(tiles):
            for which, source in enumerate((k, m)):
                copies[i][which].wait()
                for b in range(blocks):
                    high, low = split(source[i, b].T)
                    w_high[i, b * width : (b + 1) * width, which * width : (which + 1) * width] = high
                    w_low[i, b * width : (b + 1) * width, which * width : (which + 1) * width] = low
            diag = jnp.sum(jnp.where(row == lane, k[i, 0], 0.0), axis=0, keepdims=True)
            inv_d[:, i * width : (i + 1) * width] = 1.0 / diag

    return k_prep


def fill_blocks(out, value):
    for device in range(out.shape[0]):
        out[device] = value


def total(ref):
    value = ref[0]
    for device in range(1, ref.shape[0]):
        value = value + ref[device]
    return value


def fold(value):
    half = value.shape[0] // 2
    return value[:half] + pltpu.roll(value[half:], MAT // 2, 1)


def unfold(value):
    lane, _ = lane_row(value.shape)
    keep = lane < MAT // 2
    return rows([jnp.where(keep, value, 0.0), jnp.where(keep, pltpu.roll(value, MAT // 2, 1), 0.0)])


def make_kernels(n, scale):
    def put_small(ref, k, value):
        ref[k * n : (k + 1) * n] = jnp.broadcast_to(value, (n, MAT)) if value.shape[1] == 1 else lanes(
            [value, jnp.zeros((n, MAT - n), F32)]
        )

    def get_small(ref, k):
        return ref[k * n : (k + 1) * n, :n]

    def k_a(cols, iface, basis, h_a, h_f, h_b, w_high, w_low, inv_d, kb, mb, u, outgoing, grams, xs):
        put_sources(xs, 0, basis[...])
        put_sources(xs, basis.shape[1] // xs.shape[2], halo_lanes((h_a, h_f, h_b), 0, n))
        apply_pair(xs, cols, w_high, w_low, kb, mb)
        d = inv_d[...]
        u[:n] = kb[...] * d
        u[n:] = mb[...] * d
        send_tiles(iface, outgoing, 0, u)
        right = rows([basis[...], u[...], mb[...], kb[...], jnp.zeros((MAT - 5 * n, basis.shape[1]), F32)])
        both = nt(rows([basis[...], mb[...]]), right) * scale
        lane, _ = lane_row((n, MAT))
        fill_blocks(grams, jnp.where(lane < 3 * n, both[:n], both[n:]))

    def k_b0(red, basis, kb, mb, u, v_out, t_out, ko_out, mo_out, c0_out, words, small, theta_out):
        g_bb, g_u1b, g_u2b, g_mm, g_km = blocks_of(total(red), n)[:5]
        inv_v, inv_c = inverse_chols([g_bb, g_mm])
        lv, lc = inv_v[:, :n], inv_c[:, :n]
        cross = nt(mm(lv, g_km[:, :n]), lc)
        theta = diagonal(cross) * diagonal(inv_c) / diagonal(inv_v)
        g1 = mm(lv, u[:n])
        both = mm(rows([lv, lc]), u[n:])
        g2, f1 = both[:n], both[n:]
        for k, value in ((0, f1), (3, g1), (4, g2)):
            words[k * n : (k + 1) * n] = value
        c0_out[...] = -relax * (g1 - theta * g2)
        ko_out[...] = mm(lv, kb[...])
        both = mm(rows([lv, lc]), mb[...])
        mo_out[...] = both[:n]
        t_out[...] = both[n:]
        v_out[...] = mm(lv, basis[...])
        mass = nt(mm(lv, g_mm[:, :n]), lc)
        e1 = nt(mm(lv, g_u1b[:, :n]), lv)
        e2 = nt(mm(lv, g_u2b[:, :n]), lv)
        ef = nt(mm(lc, g_u2b[:, :n]), lv)
        right = -relax * (e1 - theta * e2)
        for k, value in enumerate((cross, mass, e1, e2, ef, theta, lv, lc, right)):
            put_small(small, k, value)
        lane, row = lane_row((n, MAT))
        theta_out[...] = jnp.sum(jnp.where(lane == row, theta, 0.0), axis=0, keepdims=True)[:, :n]

    def k_b1(
        cols, iface, h_a, h_f, h_b, w_high, w_low, inv_d, ko, mo, c0, words_in, small,
        p_out, image_out, words, words_halo, kf_out, outgoing, xs, res,
    ):
        lv, lc, right = (get_small(small, k) for k in (6, 7, 8))
        theta = small[5 * n : 6 * n, :1]
        g1 = mm(lv, halo_lanes((h_a, h_f, h_b), 0, n))
        both = mm(rows([lv, lc]), halo_lanes((h_a, h_f, h_b), n, 2 * n))
        g2, f1 = both[:n], both[n:]
        put_sources(xs, 0, rows([c0[...], words_in[:n]]))
        put_sources(xs, c0.shape[1] // xs.shape[2], rows([-relax * (g1 - theta * g2), f1]))
        apply_pair(xs, cols, w_high, w_low, res.at[0], res.at[1])
        for k, value in ((0, f1), (1, g1), (2, g2)):
            words_halo[k * n : (k + 1) * n] = value
        d = inv_d[...]
        image = res[0, :n] - theta * res[1, :n] - mm(lanes([right, -theta * right]), rows([ko[...], mo[...]]))
        image_out[...] = image
        kf_out[:n] = res[0, n:]
        kf_out[n:] = res[1, n:]
        words[:n] = words_in[:n]
        words[n : 2 * n] = res[0, n:] * d
        words[2 * n : 3 * n] = res[1, n:] * d
        words[3 * n :] = words_in[3 * n :]
        p_out[...] = 2.0 * c0[...] - relax * d * image
        send_tiles(iface, outgoing, 0, p_out)
        send_tiles(iface, outgoing, n, words.at[n : 3 * n])

    def half(cols, p, halo, small, c0, w_high, w_low, inv_d, xs, res):
        put_sources(xs, 0, p)
        put_sources(xs, p.shape[1] // xs.shape[2], halo)
        apply_pair(xs, cols, w_high, w_low, res.at[0], res.at[1])
        theta = small[5 * n : 6 * n, :1]
        image = res[0] - theta * res[1]
        return image, p + c0[...] - relax * inv_d[...] * image

    def k_c(
        cols, iface, p, h_a, h_f, h_b, image0, v, t, c0, words, kf, small, w_high, w_low, inv_d,
        p_out, outgoing, grams, xs, res,
    ):
        image, fresh = half(
            cols, p[...], halo_lanes((h_a, h_f, h_b), 0, n), small, c0, w_high, w_low, inv_d, xs, res
        )
        p_out[...] = fresh
        send_tiles(iface, outgoing, 0, p_out)
        right = rows([image0[...], kf[...], image, p[...], words[n : 3 * n], fresh])
        both = nt(rows([t[...], v[...]]), right) * scale
        lane, _ = lane_row((n, MAT))
        fill_blocks(grams, jnp.where(lane < 4 * n, both[:n], both[n:]))

    def solve(small, g_left, g_kf, g_mf, g_a, g_p, g_h1, g_h2, g_fresh):
        cross, mass, e1, e2, ef = (get_small(small, k) for k in range(5))
        theta = small[5 * n : 6 * n, :1]
        right = g_p + relax * mm(g_left, ef)
        left = (
            g_a
            + mm(lanes([relax * g_left, -relax * theta * g_left]), rows([g_kf, g_mf]))
            + mm(lanes([-right, theta * right]), rows([cross, mass]))
        )
        coef = lanes(
            [
                relax * (g_left + left),
                -relax * relax * g_left,
                relax * relax * theta * g_left,
                relax * right,
                -relax * theta * right,
            ]
        )
        after = g_fresh + mm(coef, rows([ef, g_h1, g_h2, e1, e2]))
        return coef, after

    def k_d0(red, p, words, small, c_out, words_grams, coefs):
        g = [value[:, :n] for value in blocks_of(total(red), n)]
        coef, right = solve(small, *g)
        for k, index in enumerate((1, 2, 5, 6)):
            put_small(words_grams, k, g[index])
        coefs[:n] = lanes([coef, jnp.zeros((n, MAT - 5 * n), F32)])
        put_small(coefs, 1, right)
        c_out[...] = p[...] + mm(coef, words[...])

    def k_d1(
        cols, iface, c_local, coefs, h_a, h_f, h_b, q_a, q_f, q_b, ko, mo, c0, words_halo, small,
        w_high, w_low, inv_d, p_out, image_out, outgoing, xs, res,
    ):
        coef, right = coefs[:n, : 5 * n], get_small(coefs, 1)
        theta = small[5 * n : 6 * n, :1]
        around = rows([words_halo[:n], halo_lanes((q_a, q_f, q_b), n, 3 * n), words_halo[n:]])
        c_halo = halo_lanes((h_a, h_f, h_b), 0, n) + mm(coef, around)
        put_sources(xs, 0, c_local[...])
        put_sources(xs, c_local.shape[1] // xs.shape[2], c_halo)
        apply_pair(xs, cols, w_high, w_low, res.at[0], res.at[1])
        image = res[0] - theta * res[1] - mm(lanes([right, -theta * right]), rows([ko[...], mo[...]]))
        image_out[...] = image
        p_out[...] = c_local[...] + c0[...] - relax * inv_d[...] * image
        send_tiles(iface, outgoing, 0, p_out)

    def k_e(
        cols, p, h_a, h_f, h_b, image2, v, t, c0, small, w_high, w_low, inv_d, p_out, grams, xs, res
    ):
        image, fresh = half(
            cols, p[...], halo_lanes((h_a, h_f, h_b), 0, n), small, c0, w_high, w_low, inv_d, xs, res
        )
        p_out[...] = fresh
        right = rows([image2[...], image, p[...], fresh, jnp.zeros((MAT - 4 * n, p.shape[1]), F32)])
        both = nt(rows([t[...], v[...]]), right) * scale
        lane, _ = lane_row((n, MAT))
        fill_blocks(grams, fold(jnp.where(lane < 2 * n, both[:n], both[n:])))

    def k_f(red, p, v, words, small, words_grams, out):
        g_left, g_a, g_p, g_fresh = (value[:, :n] for value in blocks_of(unfold(total(red)), n)[:4])
        g_kf, g_mf, g_h1, g_h2 = (get_small(words_grams, k) for k in range(4))
        coef, right = solve(small, g_left, g_kf, g_mf, g_a, g_p, g_h1, g_h2, g_fresh)
        out[...] = p[...] + mm(lanes([coef, -right]), rows([words[...], v[...]]))

    return k_a, k_b0, k_b1, k_c, k_d0, k_d1, k_e, k_f


def ordered(first, second):
    return lax.optimization_barrier((first, second))


def shards(basis, k_tiles, m_tiles, tile_part, tile_slot, iface):
    n, local = basis.shape
    tiles, blocks, width, _ = k_tiles.shape
    count = iface.shape[0]
    parts = lax.axis_size("parts")
    half_way = parts // 2
    scale = 1.0 / (local * parts)
    chip = [(source, source ^ 1) for source in range(parts)]
    other = [(source, (source + 1 if source % 2 else source - 1) % parts) for source in range(parts)]
    far = [(source, (source + half_way) % parts) for source in range(parts)]

    def halo(outgoing):
        return [lax.ppermute(outgoing, "parts", pairs) for pairs in (chip, far, other)]

    def reduced(blocks_out):
        return lax.all_to_all(blocks_out, "parts", 0, 0, tiled=True)

    k_a, k_b0, k_b1, k_c, k_d0, k_d1, k_e, k_f = make_kernels(n, scale)
    sources = tiles + 3 * count
    xs = lambda m: pltpu.VMEM((sources, 2 * m, width), BF16)
    vec = ((n, local), F32)
    vecs = lambda m: ((m * n, local), F32)
    mats = lambda m: ((m * n, MAT), F32)
    out = lambda m: ((count, m, width), F32)
    grams16 = ((parts, n, MAT), F32)
    grams8 = ((parts, n // 2, MAT), F32)
    res = pltpu.VMEM((2, n, local), F32)

    (outgoing,) = call(
        k_first, [out(n)], [HBM, HBM], [pltpu.SMEM((count,), jnp.int32), pltpu.SemaphoreType.DMA((count,))]
    )(in_hbm(iface), in_hbm(basis))
    h0 = halo(outgoing)
    w_high, w_low, inv_d, cols = call(
        make_prep(count),
        [((tiles, blocks * width, 2 * width), BF16)] * 2 + [((1, local), F32), ((tiles, blocks), jnp.int32)],
        [HBM] * 4,
        [pltpu.VMEM(k_tiles.shape, F32)] * 2
        + [pltpu.VMEM((tiles, blocks), jnp.int32)] * 2
        + [pltpu.SemaphoreType.DMA((2, tiles + 1))],
    )(*(in_hbm(value) for value in (tile_part, tile_slot, k_tiles, m_tiles)))
    w = (w_high, w_low, inv_d)
    kb, mb, u, outgoing, grams = call(
        k_a, [vec, vec, vecs(2), out(2 * n), grams16], [SM, SM] + [VM] * 7, [xs(n)]
    )(cols, iface, basis, *h0, *w)
    red, outgoing = ordered(reduced(grams), outgoing)
    h1 = halo(outgoing)
    v, t, ko, mo, c0, words, small, theta = call(
        k_b0, [vec] * 5 + [vecs(5), mats(9), ((1, n), F32)], [VM] * 5
    )(red, basis, kb, mb, u)
    p1, image0, words, words_halo, kf, outgoing = call(
        k_b1,
        [vec, vec, vecs(5), ((3 * n, 3 * count * width), F32), vecs(2), out(3 * n)],
        [SM, SM] + [VM] * 11,
        [xs(2 * n), pltpu.VMEM((2, 2 * n, local), F32)],
    )(cols, iface, *h1, *w, ko, mo, c0, words, small)
    h2 = halo(outgoing)
    p2, outgoing, grams = call(k_c, [vec, out(n), grams16], [SM, SM] + [VM] * 14, [xs(n), res])(
        cols, iface, p1, *h2, image0, v, t, c0, words, kf, small, *w
    )
    red, outgoing = ordered(reduced(grams), outgoing)
    h3 = halo(outgoing)
    c2, words_grams, coefs = call(k_d0, [vec, mats(4), mats(2)], [VM] * 4)(red, p2, words, small)
    p3, image2, outgoing = call(k_d1, [vec, vec, out(n)], [SM, SM] + [VM] * 16, [xs(n), res])(
        cols, iface, c2, coefs, *h3, *h2, ko, mo, c0, words_halo, small, *w
    )
    h4 = halo(outgoing)
    p4, grams = call(k_e, [vec, grams8], [SM] + [VM] * 12, [xs(n), res])(cols, p3, *h4, image2, v, t, c0, small, *w)
    red = reduced(grams)
    (correct,) = call(k_f, [vec], [VM] * 6)(red, p4, v, words, small, words_grams)
    return (correct, theta.reshape(-1))


def solution(mesh):
    placed = (
        P(None, "parts"),
        P("parts", None, None, None),
        P("parts", None, None, None),
        P("parts", None),
        P("parts", None),
        P("parts"),
    )
    return jax.shard_map(
        shards, mesh=mesh, in_specs=placed, out_specs=(P(None, "parts"), P()), check_vma=False
    )
```

```python
import jax
import jax.numpy as jnp
from jax import lax
from jax.experimental import pallas as pl
from jax.experimental.pallas import tpu as pltpu
from jax.sharding import PartitionSpec as P


relax = 0.4

F32 = jnp.float32
BF16 = jnp.bfloat16
VM = pl.BlockSpec(memory_space=pltpu.VMEM)
SM = pl.BlockSpec(memory_space=pltpu.SMEM)
HBM = pl.BlockSpec(memory_space=pltpu.MemorySpace.HBM)
MAT = 128


def call(kernel, outs, specs, scratch=()):
    return pl.pallas_call(
        kernel,
        in_specs=specs,
        out_specs=[VM] * len(outs),
        out_shape=[jax.ShapeDtypeStruct(shape, dtype) for shape, dtype in outs],
        scratch_shapes=list(scratch),
        compiler_params=pltpu.CompilerParams(vmem_limit_bytes=24 << 20),
    )


def in_hbm(value):
    return pltpu.with_memory_space_constraint(value, pltpu.MemorySpace.HBM)


def mm(left, right):
    return jnp.dot(left, right, precision=lax.Precision.HIGHEST, preferred_element_type=F32)


def nt(left, right):
    return lax.dot_general(
        left, right, (((1,), (1,)), ((), ())), precision=lax.Precision.HIGHEST, preferred_element_type=F32
    )


def split(value):
    high = value.astype(BF16)
    return high, (value - high.astype(F32)).astype(BF16)


def mm3(left, right):
    lh, ll = split(left)
    rh, rl = split(right)
    n = left.shape[0]
    both = jnp.dot(jnp.concatenate([lh, ll], axis=0), rh, preferred_element_type=F32)
    return both[:n] + both[n:] + jnp.dot(lh, rl, preferred_element_type=F32)


def nt3(high, low, right):
    dims = (((1,), (1,)), ((), ()))
    rh, rl = split(right)
    n = high.shape[0]
    both = lax.dot_general(jnp.concatenate([high, low], axis=0), rh, dims, preferred_element_type=F32)
    return both[:n] + both[n:] + lax.dot_general(high, rl, dims, preferred_element_type=F32)


def rows(parts):
    return jnp.concatenate(parts, axis=0)


def lanes(parts):
    return jnp.concatenate(parts, axis=1)


def halo_lanes(refs, first, last):
    return lanes([ref[slot, first:last] for ref in refs for slot in range(ref.shape[0])])


def put_sources(xs, at, value):
    n, width = value.shape[0], xs.shape[2]
    for t in range(value.shape[1] // width):
        high, low = split(value[:, t * width : (t + 1) * width])
        xs[at + t, :n] = high
        xs[at + t, n:] = low


def apply_pair(xs, cols, w_high, w_low, k_out, m_out):
    tiles, blocks = cols.shape
    width = xs.shape[2]
    n = xs.shape[1] // 2
    for i in range(tiles):
        lhs = lanes([xs[cols[i, b]] for b in range(blocks)])
        both = jnp.dot(lhs, w_high[i], preferred_element_type=F32)
        low = jnp.dot(lhs[:n], w_low[i], preferred_element_type=F32)
        result = both[:n] + both[n:] + low
        k_out[:, i * width : (i + 1) * width] = result[:, :width]
        m_out[:, i * width : (i + 1) * width] = result[:, width:]


def send_tiles(iface, outgoing, at, ref):
    width = outgoing.shape[2]
    n = ref.shape[0]
    for slot in range(outgoing.shape[0]):
        start = pl.multiple_of(iface[slot] * width, width)
        outgoing[slot, at : at + n] = ref[:, pl.ds(start, width)]


def lane_row(shape):
    return lax.broadcasted_iota(jnp.int32, shape, 1), lax.broadcasted_iota(jnp.int32, shape, 0)


def blocks_of(summed, n):
    square = rows([summed, jnp.zeros((MAT - n, MAT), F32)])
    turned = square.T
    return [turned[k * n : (k + 1) * n] for k in range(MAT // n)]


def inverse_chols(first, second):
    n = first.shape[0]
    shape = first.shape
    lane, row = lane_row(shape)
    half = MAT // 2
    columns = [
        jnp.where(
            lane < half,
            jnp.broadcast_to(first[:, j : j + 1], shape),
            jnp.broadcast_to(second[:, j : j + 1], shape),
        )
        for j in range(n)
    ]
    inverse = jnp.where(lane % half == row, 1.0, 0.0)
    pivots = jnp.ones(shape, F32)
    for k in range(n):
        pivot = columns[k][k : k + 1, :]
        pivots = jnp.where(row == k, pivot, pivots)
        if k == n - 1:
            break
        factor = jnp.where(row > k, columns[k], 0.0) * (1.0 / pivot)
        for j in range(k + 1, n):
            columns[j] = columns[j] - factor * columns[j][k : k + 1, :]
        inverse = inverse - factor * inverse[k : k + 1, :]
    inverse = inverse * lax.rsqrt(pivots)
    return [jnp.where(lane < n, value, 0.0) for value in (inverse, pltpu.roll(inverse, half, 1))]


def diagonal(a):
    lane, row = lane_row(a.shape)
    return jnp.sum(jnp.where(lane == row, a, 0.0), axis=1, keepdims=True)


def k_first(iface_hbm, basis, outgoing, iface, sems):
    copy = pltpu.make_async_copy(iface_hbm, iface, sems.at[0])
    copy.start()
    copy.wait()
    width = outgoing.shape[2]
    copies = []
    for slot in range(outgoing.shape[0]):
        start = pl.multiple_of(iface[slot] * width, width)
        copy = pltpu.make_async_copy(basis.at[:, pl.ds(start, width)], outgoing.at[slot], sems.at[slot])
        copy.start()
        copies.append(copy)
    for copy in copies:
        copy.wait()


def make_prep(count):
    def k_prep(part_hbm, slot_hbm, k_hbm, m_hbm, w_high, w_low, inv_d, cols, k, m, part_in, slot_in, sems):
        tiles, blocks, width, _ = k.shape
        pattern = [
            pltpu.make_async_copy(source, target, sems.at[which, tiles])
            for which, (source, target) in enumerate(((part_hbm, part_in), (slot_hbm, slot_in)))
        ]
        for copy in pattern:
            copy.start()
        copies = []
        for i in range(tiles):
            pair = [
                pltpu.make_async_copy(source.at[i], target.at[i], sems.at[which, i])
                for which, (source, target) in enumerate(((k_hbm, k), (m_hbm, m)))
            ]
            for copy in pair:
                copy.start()
            copies.append(pair)
        parts = lax.axis_size("parts")
        me = lax.axis_index("parts")
        for copy in pattern:
            copy.wait()
        part, slot = part_in[...], slot_in[...]
        remote = jnp.where(part == me ^ 1, 0, jnp.where(part == (me + parts // 2) % parts, count, 2 * count))
        cols[...] = jnp.where(part == me, slot, tiles + remote + slot)
        row = lax.broadcasted_iota(jnp.int32, (width, width), 0)
        lane = lax.broadcasted_iota(jnp.int32, (width, width), 1)
        for i in range(tiles):
            for which, source in enumerate((k, m)):
                copies[i][which].wait()
                for b in range(blocks):
                    high, low = split(source[i, b].T)
                    w_high[i, b * width : (b + 1) * width, which * width : (which + 1) * width] = high
                    w_low[i, b * width : (b + 1) * width, which * width : (which + 1) * width] = low
            diag = jnp.sum(jnp.where(row == lane, k[i, 0], 0.0), axis=0, keepdims=True)
            inv_d[:, i * width : (i + 1) * width] = 1.0 / diag

    return k_prep


def fill_blocks(out, value):
    for device in range(out.shape[0]):
        out[device] = value


def total(ref):
    value = ref[0]
    for device in range(1, ref.shape[0]):
        value = value + ref[device]
    return value


def fold(value):
    half = value.shape[0] // 2
    return value[:half] + pltpu.roll(value[half:], MAT // 2, 1)


def unfold(value):
    lane, _ = lane_row(value.shape)
    keep = lane < MAT // 2
    return rows([jnp.where(keep, value, 0.0), jnp.where(keep, pltpu.roll(value, MAT // 2, 1), 0.0)])


def make_kernels(n, scale):
    def put_small(ref, k, value):
        ref[k * n : (k + 1) * n] = jnp.broadcast_to(value, (n, MAT)) if value.shape[1] == 1 else lanes(
            [value, jnp.zeros((n, MAT - n), F32)]
        )

    def get_small(ref, k):
        return ref[k * n : (k + 1) * n, :n]

    def k_a(cols, iface, basis, h_a, h_f, h_b, w_high, w_low, inv_d, kb, mb, u, outgoing, grams, xs):
        put_sources(xs, 0, basis[...])
        put_sources(xs, basis.shape[1] // xs.shape[2], halo_lanes((h_a, h_f, h_b), 0, n))
        apply_pair(xs, cols, w_high, w_low, kb, mb)
        d = inv_d[...]
        u[:n] = kb[...] * d
        u[n:] = mb[...] * d
        send_tiles(iface, outgoing, 0, u)
        right = rows([basis[...], u[...], kb[...], mb[...], jnp.zeros((MAT - 5 * n, basis.shape[1]), F32)])
        both = nt(rows([basis[...], mb[...]]), right) * scale
        lane, row = lane_row((n, MAT))
        chosen = jnp.where(lane < 3 * n, both[:n], both[n:])
        mass = pltpu.roll(chosen, MAT - 4 * n, 1)
        packed = jnp.where((lane < n) & (lane > row), mass, jnp.where(lane < 4 * n, chosen, 0.0))
        mass_diag = jnp.sum(jnp.where((lane == row) & (lane < n), mass, 0.0), axis=0, keepdims=True)
        packed = fold(packed)
        for device in range(grams.shape[0]):
            grams[device, : n // 2, 0, :] = packed
            grams[device, n // 2] = mass_diag

    def k_b0(red, kb, mb, u, ko_out, mo_out, c0_out, words, small, theta_out):
        packed, mass_diag = red[0, : n // 2, 0, :], red[0, n // 2]
        for device in range(1, red.shape[0]):
            packed = packed + red[device, : n // 2, 0, :]
            mass_diag = mass_diag + red[device, n // 2]
        packed = unfold(packed)
        turned, g_u1b, g_u2b, g_km = blocks_of(packed, n)[:4]
        lane, row = lane_row((n, MAT))
        g_bb = jnp.where(lane < n, jnp.where(lane <= row, packed, turned), 0.0)
        g_mm = jnp.where(lane == row, mass_diag, jnp.where(lane > row, packed, turned))
        g_mm = jnp.where(lane < n, g_mm, 0.0)
        inv_v, inv_c = inverse_chols(g_bb, g_mm)
        lv, lc = inv_v[:, :n], inv_c[:, :n]
        cross = nt(mm(lv, g_km[:, :n]), lc)
        theta = diagonal(cross) * diagonal(inv_c) / diagonal(inv_v)
        g1 = mm3(lv, u[:n])
        both = mm3(rows([lv, lc]), u[n:])
        g2, f1 = both[:n], both[n:]
        for k, value in ((0, f1), (3, g1), (4, g2)):
            words[k * n : (k + 1) * n] = value
        c0_out[...] = -relax * (g1 - theta * g2)
        ko_out[...] = mm3(lv, kb[...])
        mo_out[...] = mm3(lv, mb[...])
        e1 = nt(mm(lv, g_u1b[:, :n]), lv)
        e2 = nt(mm(lv, g_u2b[:, :n]), lv)
        right = -relax * (e1 - theta * e2)
        for k, value in enumerate((cross, g_mm[:, :n], e1, e2, g_u2b[:, :n], theta, lv, lc, right)):
            put_small(small, k, value)
        theta_out[...] = jnp.sum(jnp.where(lane == row, theta, 0.0), axis=0, keepdims=True)[:, :n]

    def k_b1(
        cols, iface, h_a, h_f, h_b, w_high, w_low, inv_d, ko, mo, c0, words_in, small,
        p_out, image_out, words, words_halo, kf_out, outgoing, xs, res,
    ):
        lv, lc, right = (get_small(small, k) for k in (6, 7, 8))
        theta = small[5 * n : 6 * n, :1]
        g1 = mm3(lv, halo_lanes((h_a, h_f, h_b), 0, n))
        both = mm3(rows([lv, lc]), halo_lanes((h_a, h_f, h_b), n, 2 * n))
        g2, f1 = both[:n], both[n:]
        put_sources(xs, 0, rows([c0[...], words_in[:n]]))
        put_sources(xs, c0.shape[1] // xs.shape[2], rows([-relax * (g1 - theta * g2), f1]))
        apply_pair(xs, cols, w_high, w_low, res.at[0], res.at[1])
        for k, value in ((0, f1), (1, g1), (2, g2)):
            words_halo[k * n : (k + 1) * n] = value
        d = inv_d[...]
        image = res[0, :n] - theta * res[1, :n] - mm3(lanes([right, -theta * right]), rows([ko[...], mo[...]]))
        image_out[...] = image
        kf_out[:n] = res[0, n:]
        kf_out[n:] = res[1, n:]
        words[:n] = words_in[:n]
        words[n : 2 * n] = res[0, n:] * d
        words[2 * n : 3 * n] = res[1, n:] * d
        words[3 * n :] = words_in[3 * n :]
        p_out[...] = 2.0 * c0[...] - relax * d * image
        send_tiles(iface, outgoing, 0, p_out)
        send_tiles(iface, outgoing, n, words.at[n : 3 * n])

    def k_c0(small, basis, mb, image0, kf, p, words, v_out, tests_high, tests_low, small_b, part):
        lv, lc = get_small(small, 6), get_small(small, 7)
        v = mm3(lv, basis[...])
        v_out[...] = v
        high, low = split(rows([mm3(lc, mb[...]), v]))
        tests_high[...] = high
        tests_low[...] = low
        put_small(small_b, 0, nt(mm(lv, get_small(small, 1)), lc))
        put_small(small_b, 1, nt(mm(lc, get_small(small, 4)), lv))
        right = rows([image0[...], kf[...], p[...], words[n : 3 * n], jnp.zeros((2 * n, p.shape[1]), F32)])
        both = nt3(high, low, right) * scale
        lane, _ = lane_row((n, MAT))
        part[...] = jnp.where(lane < 3 * n, both[:n], both[n:])

    def half(cols, p, halo, small, c0, w_high, w_low, inv_d, tests_high, tests_low, xs, res):
        put_sources(xs, 0, p)
        put_sources(xs, p.shape[1] // xs.shape[2], halo)
        apply_pair(xs, cols, w_high, w_low, res.at[0], res.at[1])
        theta = small[5 * n : 6 * n, :1]
        image = res[0] - theta * res[1]
        fresh = p + c0[...] - relax * inv_d[...] * image
        both = nt3(tests_high[...], tests_low[...], rows([image, fresh])) * scale
        both = lanes([both, jnp.zeros((2 * n, MAT - 2 * n), F32)])
        lane, _ = lane_row((n, MAT))
        return fresh, jnp.where(lane < n, both[:n], both[n:])

    def k_c1(
        cols, iface, p, h_a, h_f, h_b, c0, small, part, tests_high, tests_low, w_high, w_low, inv_d,
        p_out, outgoing, grams, xs, res,
    ):
        fresh, added = half(
            cols, p[...], halo_lanes((h_a, h_f, h_b), 0, n), small, c0, w_high, w_low, inv_d,
            tests_high, tests_low, xs, res,
        )
        p_out[...] = fresh
        send_tiles(iface, outgoing, 0, p_out)
        lane, _ = lane_row((n, MAT))
        fill_blocks(grams, jnp.where(lane < 6 * n, part[...], pltpu.roll(added, 6 * n, 1)))

    def solve(small, small_b, g_left, g_kf, g_mf, g_p, g_h1, g_h2, g_a, g_fresh):
        cross, e1, e2 = (get_small(small, k) for k in (0, 2, 3))
        mass, ef = (get_small(small_b, k) for k in range(2))
        theta = small[5 * n : 6 * n, :1]
        right = g_p + relax * mm(g_left, ef)
        left = (
            g_a
            + mm(lanes([relax * g_left, -relax * theta * g_left]), rows([g_kf, g_mf]))
            + mm(lanes([-right, theta * right]), rows([cross, mass]))
        )
        coef = lanes(
            [
                relax * (g_left + left),
                -relax * relax * g_left,
                relax * relax * theta * g_left,
                relax * right,
                -relax * theta * right,
            ]
        )
        after = g_fresh + mm(coef, rows([ef, g_h1, g_h2, e1, e2]))
        return coef, after

    def k_d0(red, p, words, small, small_b, c_out, words_grams, coefs):
        g = [value[:, :n] for value in blocks_of(total(red), n)]
        coef, right = solve(small, small_b, *g)
        for k, index in enumerate((1, 2, 4, 5)):
            put_small(words_grams, k, g[index])
        coefs[:n] = lanes([coef, jnp.zeros((n, MAT - 5 * n), F32)])
        put_small(coefs, 1, right)
        c_out[...] = p[...] + mm3(coef, words[...])

    def k_d1(
        cols, iface, c_local, coefs, h_a, h_f, h_b, q_a, q_f, q_b, ko, mo, c0, words_halo, small,
        w_high, w_low, inv_d, p_out, image_out, outgoing, xs, res,
    ):
        coef, right = coefs[:n, : 5 * n], get_small(coefs, 1)
        theta = small[5 * n : 6 * n, :1]
        around = rows([words_halo[:n], halo_lanes((q_a, q_f, q_b), n, 3 * n), words_halo[n:]])
        c_halo = halo_lanes((h_a, h_f, h_b), 0, n) + mm3(coef, around)
        put_sources(xs, 0, c_local[...])
        put_sources(xs, c_local.shape[1] // xs.shape[2], c_halo)
        apply_pair(xs, cols, w_high, w_low, res.at[0], res.at[1])
        image = res[0] - theta * res[1] - mm3(lanes([right, -theta * right]), rows([ko[...], mo[...]]))
        image_out[...] = image
        p_out[...] = c_local[...] + c0[...] - relax * inv_d[...] * image
        send_tiles(iface, outgoing, 0, p_out)

    def k_e0(image2, p, tests_high, tests_low, part):
        right = rows([image2[...], p[...], jnp.zeros((MAT - 2 * n, p.shape[1]), F32)])
        both = nt3(tests_high[...], tests_low[...], right) * scale
        lane, _ = lane_row((n, MAT))
        part[...] = jnp.where(lane < n, both[:n], both[n:])

    def k_e1(
        cols, p, h_a, h_f, h_b, c0, small, part, tests_high, tests_low, w_high, w_low, inv_d, p_out, grams, xs, res
    ):
        fresh, added = half(
            cols, p[...], halo_lanes((h_a, h_f, h_b), 0, n), small, c0, w_high, w_low, inv_d,
            tests_high, tests_low, xs, res,
        )
        p_out[...] = fresh
        lane, _ = lane_row((n, MAT))
        both = jnp.where(lane < 2 * n, part[...], pltpu.roll(added, 2 * n, 1))
        fill_blocks(grams, fold(jnp.where(lane < 4 * n, both, 0.0)))

    def k_f(red, p, v, words, small, small_b, words_grams, out):
        g_left, g_p, g_a, g_fresh = (value[:, :n] for value in blocks_of(unfold(total(red)), n)[:4])
        g_kf, g_mf, g_h1, g_h2 = (get_small(words_grams, k) for k in range(4))
        coef, right = solve(small, small_b, g_left, g_kf, g_mf, g_p, g_h1, g_h2, g_a, g_fresh)
        out[...] = p[...] + mm3(lanes([coef, -right]), rows([words[...], v[...]]))

    return k_a, k_b0, k_b1, k_c0, k_c1, k_d0, k_d1, k_e0, k_e1, k_f


def shards(basis, k_tiles, m_tiles, tile_part, tile_slot, iface):
    n, local = basis.shape
    tiles, blocks, width, _ = k_tiles.shape
    count = iface.shape[0]
    parts = lax.axis_size("parts")
    half_way = parts // 2
    scale = 1.0 / (local * parts)
    chip = [(source, source ^ 1) for source in range(parts)]
    other = [(source, (source + 1 if source % 2 else source - 1) % parts) for source in range(parts)]
    far = [(source, (source + half_way) % parts) for source in range(parts)]

    def halo(outgoing):
        return [lax.ppermute(outgoing, "parts", pairs) for pairs in (chip, far, other)]

    def reduced(blocks_out):
        return lax.all_to_all(blocks_out, "parts", 0, 0, tiled=True)

    k_a, k_b0, k_b1, k_c0, k_c1, k_d0, k_d1, k_e0, k_e1, k_f = make_kernels(n, scale)
    sources = tiles + 3 * count
    xs = lambda m: pltpu.VMEM((sources, 2 * m, width), BF16)
    vec = ((n, local), F32)
    vecs = lambda m: ((m * n, local), F32)
    mats = lambda m: ((m * n, MAT), F32)
    out = lambda m: ((count, m, width), F32)
    grams16 = ((parts, n, MAT), F32)
    grams8 = ((parts, n // 2, MAT), F32)
    res = pltpu.VMEM((2, n, local), F32)

    (outgoing,) = call(
        k_first, [out(n)], [HBM, HBM], [pltpu.SMEM((count,), jnp.int32), pltpu.SemaphoreType.DMA((count,))]
    )(in_hbm(iface), in_hbm(basis))
    h0 = halo(outgoing)
    w_high, w_low, inv_d, cols = call(
        make_prep(count),
        [((tiles, blocks * width, 2 * width), BF16)] * 2 + [((1, local), F32), ((tiles, blocks), jnp.int32)],
        [HBM] * 4,
        [pltpu.VMEM(k_tiles.shape, F32)] * 2
        + [pltpu.VMEM((tiles, blocks), jnp.int32)] * 2
        + [pltpu.SemaphoreType.DMA((2, tiles + 1))],
    )(*(in_hbm(value) for value in (tile_part, tile_slot, k_tiles, m_tiles)))
    w = (w_high, w_low, inv_d)
    packed = ((parts, n // 2 + 1, 1, MAT), F32)
    kb, mb, u, outgoing, grams = call(
        k_a, [vec, vec, vecs(2), out(2 * n), packed], [SM, SM] + [VM] * 7, [xs(n)]
    )(cols, iface, basis, *h0, *w)
    red = reduced(grams)
    h1 = halo(outgoing)
    ko, mo, c0, words, small, theta = call(
        k_b0, [vec] * 3 + [vecs(5), mats(9), ((1, n), F32)], [VM] * 4
    )(red, kb, mb, u)
    p1, image0, words, words_halo, kf, outgoing = call(
        k_b1,
        [vec, vec, vecs(5), ((3 * n, 3 * count * width), F32), vecs(2), out(3 * n)],
        [SM, SM] + [VM] * 11,
        [xs(2 * n), pltpu.VMEM((2, 2 * n, local), F32)],
    )(cols, iface, *h1, *w, ko, mo, c0, words, small)
    h2 = halo(outgoing)
    v, tests_high, tests_low, small_b, part = call(
        k_c0, [vec] + [((2 * n, local), BF16)] * 2 + [mats(2), mats(1)], [VM] * 7
    )(small, basis, mb, image0, kf, p1, words)
    tests = (tests_high, tests_low)
    p2, outgoing, grams = call(k_c1, [vec, out(n), grams16], [SM, SM] + [VM] * 12, [xs(n), res])(
        cols, iface, p1, *h2, c0, small, part, *tests, *w
    )
    red = reduced(grams)
    h3 = halo(outgoing)
    c2, words_grams, coefs = call(k_d0, [vec, mats(4), mats(2)], [VM] * 5)(
        red, p2, words, small, small_b
    )
    p3, image2, outgoing = call(k_d1, [vec, vec, out(n)], [SM, SM] + [VM] * 16, [xs(n), res])(
        cols, iface, c2, coefs, *h3, *h2, ko, mo, c0, words_halo, small, *w
    )
    h4 = halo(outgoing)
    (part,) = call(k_e0, [mats(1)], [VM] * 4)(image2, p3, *tests)
    p4, grams = call(k_e1, [vec, grams8], [SM] + [VM] * 12, [xs(n), res])(cols, p3, *h4, c0, small, part, *tests, *w)
    red = reduced(grams)
    (correct,) = call(k_f, [vec], [VM] * 7)(red, p4, v, words, small, small_b, words_grams)
    return (correct, theta.reshape(-1))


def solution(mesh):
    placed = (
        P(None, "parts"),
        P("parts", None, None, None),
        P("parts", None, None, None),
        P("parts", None),
        P("parts", None),
        P("parts"),
    )
    return jax.shard_map(
        shards, mesh=mesh, in_specs=placed, out_specs=(P(None, "parts"), P()), check_vma=False
    )
```

```python
import jax
import jax.numpy as jnp
from jax import lax
from jax.experimental import pallas as pl
from jax.experimental.pallas import tpu as pltpu
from jax.sharding import PartitionSpec as P


relax = 0.4

F32 = jnp.float32
BF16 = jnp.bfloat16
VM = pl.BlockSpec(memory_space=pltpu.VMEM)
SM = pl.BlockSpec(memory_space=pltpu.SMEM)
HBM = pl.BlockSpec(memory_space=pltpu.MemorySpace.HBM)
MAT = 128


def call(kernel, outs, specs, scratch=()):
    return pl.pallas_call(
        kernel,
        in_specs=specs,
        out_specs=[VM] * len(outs),
        out_shape=[jax.ShapeDtypeStruct(shape, dtype) for shape, dtype in outs],
        scratch_shapes=list(scratch),
        compiler_params=pltpu.CompilerParams(vmem_limit_bytes=24 << 20),
    )


def in_hbm(value):
    return pltpu.with_memory_space_constraint(value, pltpu.MemorySpace.HBM)


def mm(left, right):
    return jnp.dot(left, right, precision=lax.Precision.HIGHEST, preferred_element_type=F32)


def nt(left, right):
    return lax.dot_general(
        left, right, (((1,), (1,)), ((), ())), precision=lax.Precision.HIGHEST, preferred_element_type=F32
    )


def split(value):
    high = value.astype(BF16)
    return high, (value - high.astype(F32)).astype(BF16)


def mm3(left, right):
    lh, ll = split(left)
    rh, rl = split(right)
    n = left.shape[0]
    both = jnp.dot(jnp.concatenate([lh, ll], axis=0), rh, preferred_element_type=F32)
    return both[:n] + both[n:] + jnp.dot(lh, rl, preferred_element_type=F32)


def nt3(high, low, right):
    dims = (((1,), (1,)), ((), ()))
    n = high.shape[0]
    left = jnp.concatenate([high, low], axis=0)
    both = sum(lax.dot_general(left, part, dims, preferred_element_type=F32) for part in split(right))
    return both[:n] + both[n:]


def rows(parts):
    return jnp.concatenate(parts, axis=0)


def lanes(parts):
    return jnp.concatenate(parts, axis=1)


def halo_lanes(refs, first, last):
    return lanes([ref[slot, first:last] for ref in refs for slot in range(ref.shape[0])])


def put_sources(xs, at, value):
    n, width = value.shape[0], xs.shape[2]
    for t in range(value.shape[1] // width):
        high, low = split(value[:, t * width : (t + 1) * width])
        xs[at + t, :n] = high
        xs[at + t, n:] = low


def apply_pair(xs, cols, w_high, w_low, k_out, m_out):
    tiles, blocks = cols.shape
    width = xs.shape[2]
    n = xs.shape[1] // 2
    for i in range(tiles):
        lhs = lanes([xs[cols[i, b]] for b in range(blocks)])
        both = jnp.dot(lhs, w_high[i], preferred_element_type=F32)
        low = jnp.dot(lhs[:n], w_low[i], preferred_element_type=F32)
        result = both[:n] + both[n:] + low
        k_out[:, i * width : (i + 1) * width] = result[:, :width]
        m_out[:, i * width : (i + 1) * width] = result[:, width:]


def send_tiles(iface, outgoing, at, ref):
    width = outgoing.shape[2]
    n = ref.shape[0]
    for slot in range(outgoing.shape[0]):
        start = pl.multiple_of(iface[slot] * width, width)
        outgoing[slot, at : at + n] = ref[:, pl.ds(start, width)]


def lane_row(shape):
    return lax.broadcasted_iota(jnp.int32, shape, 1), lax.broadcasted_iota(jnp.int32, shape, 0)


def blocks_of(summed, n):
    square = rows([summed, jnp.zeros((MAT - n, MAT), F32)])
    turned = square.T
    return [turned[k * n : (k + 1) * n] for k in range(MAT // n)]


def inverse_chols(first, second):
    n = first.shape[0]
    shape = first.shape
    lane, row = lane_row(shape)
    half = MAT // 2
    columns = [
        jnp.where(
            lane < half,
            jnp.broadcast_to(first[:, j : j + 1], shape),
            jnp.broadcast_to(second[:, j : j + 1], shape),
        )
        for j in range(n)
    ]
    inverse = jnp.where(lane % half == row, 1.0, 0.0)
    pivots = jnp.ones(shape, F32)
    for k in range(n):
        pivot = columns[k][k : k + 1, :]
        pivots = jnp.where(row == k, pivot, pivots)
        if k == n - 1:
            break
        factor = jnp.where(row > k, columns[k], 0.0) * (1.0 / pivot)
        for j in range(k + 1, n):
            columns[j] = columns[j] - factor * columns[j][k : k + 1, :]
        inverse = inverse - factor * inverse[k : k + 1, :]
    inverse = inverse * lax.rsqrt(pivots)
    return [jnp.where(lane < n, value, 0.0) for value in (inverse, pltpu.roll(inverse, half, 1))]


def diagonal(a):
    lane, row = lane_row(a.shape)
    return jnp.sum(jnp.where(lane == row, a, 0.0), axis=1, keepdims=True)


def k_first(iface_hbm, basis_hbm, outgoing, iface, basis, sems):
    copies = [
        pltpu.make_async_copy(iface_hbm, iface, sems.at[0]),
        pltpu.make_async_copy(basis_hbm, basis, sems.at[1]),
    ]
    for copy in copies:
        copy.start()
    for copy in copies:
        copy.wait()
    send_tiles(iface, outgoing, 0, basis)


def make_prep(count):
    def k_prep(part_hbm, slot_hbm, k_hbm, m_hbm, w_high, w_low, inv_d, cols, k, m, part_in, slot_in, sems):
        tiles, blocks, width, _ = k.shape
        pattern = [
            pltpu.make_async_copy(source, target, sems.at[which, tiles])
            for which, (source, target) in enumerate(((part_hbm, part_in), (slot_hbm, slot_in)))
        ]
        for copy in pattern:
            copy.start()
        copies = []
        for i in range(tiles):
            pair = [
                pltpu.make_async_copy(source.at[i], target.at[i], sems.at[which, i])
                for which, (source, target) in enumerate(((k_hbm, k), (m_hbm, m)))
            ]
            for copy in pair:
                copy.start()
            copies.append(pair)
        parts = lax.axis_size("parts")
        me = lax.axis_index("parts")
        for copy in pattern:
            copy.wait()
        part, slot = part_in[...], slot_in[...]
        remote = jnp.where(part == me ^ 1, 0, jnp.where(part == (me + parts // 2) % parts, count, 2 * count))
        cols[...] = jnp.where(part == me, slot, tiles + remote + slot)
        row = lax.broadcasted_iota(jnp.int32, (width, width), 0)
        lane = lax.broadcasted_iota(jnp.int32, (width, width), 1)
        for i in range(tiles):
            for which, source in enumerate((k, m)):
                copies[i][which].wait()
                for b in range(blocks):
                    high, low = split(source[i, b].T)
                    w_high[i, b * width : (b + 1) * width, which * width : (which + 1) * width] = high
                    w_low[i, b * width : (b + 1) * width, which * width : (which + 1) * width] = low
            diag = jnp.sum(jnp.where(row == lane, k[i, 0], 0.0), axis=0, keepdims=True)
            inv_d[:, i * width : (i + 1) * width] = 1.0 / diag

    return k_prep


def fill_blocks(out, value):
    for device in range(out.shape[0]):
        out[device] = value


def total(ref):
    value = ref[0]
    for device in range(1, ref.shape[0]):
        value = value + ref[device]
    return value


def fold(value):
    half = value.shape[0] // 2
    return value[:half] + pltpu.roll(value[half:], MAT // 2, 1)


def unfold(value):
    lane, _ = lane_row(value.shape)
    keep = lane < MAT // 2
    return rows([jnp.where(keep, value, 0.0), jnp.where(keep, pltpu.roll(value, MAT // 2, 1), 0.0)])


def pack_rows(value):
    lane, row = lane_row(value.shape)
    m = value.shape[0] // 2
    n = MAT // m
    shift = n
    while shift < MAT:
        value = value + pltpu.roll(value, shift, 1)
        shift *= 2
    value = jnp.where(lane // n == row % m, value, 0.0)
    return [jnp.sum(value[k * m : (k + 1) * m], axis=0, keepdims=True) for k in range(2)]


def unpack_rows(pair, m):
    value = rows([jnp.broadcast_to(part, (m, MAT)) for part in pair])
    lane, row = lane_row(value.shape)
    n = MAT // m
    value = jnp.where(lane // n == row % m, value, 0.0)
    shift = n
    while shift < MAT:
        value = value + pltpu.roll(value, shift, 1)
        shift *= 2
    return value


def make_kernels(n, scale):
    def put_small(ref, k, value):
        ref[k * n : (k + 1) * n] = jnp.broadcast_to(value, (n, MAT)) if value.shape[1] == 1 else lanes(
            [value, jnp.zeros((n, MAT - n), F32)]
        )

    def get_small(ref, k):
        return ref[k * n : (k + 1) * n, :n]

    def k_a(cols, iface, basis, h_a, h_f, h_b, w_high, w_low, inv_d, kb, mb, u, outgoing, grams, xs):
        put_sources(xs, 0, basis[...])
        put_sources(xs, basis.shape[1] // xs.shape[2], halo_lanes((h_a, h_f, h_b), 0, n))
        apply_pair(xs, cols, w_high, w_low, kb, mb)
        d = inv_d[...]
        u[:n] = kb[...] * d
        u[n:] = mb[...] * d
        send_tiles(iface, outgoing, 0, u)
        right = rows([basis[...], u[...], kb[...], mb[...], jnp.zeros((MAT - 5 * n, basis.shape[1]), F32)])
        both = nt3(*split(rows([basis[...], mb[...]])), right) * scale
        lane, row = lane_row((n, MAT))
        chosen = jnp.where(lane < 3 * n, both[:n], both[n:])
        mass = pltpu.roll(chosen, MAT - 4 * n, 1)
        packed = jnp.where((lane < n) & (lane > row), mass, jnp.where(lane < 4 * n, chosen, 0.0))
        mass_diag = jnp.sum(jnp.where((lane == row) & (lane < n), mass, 0.0), axis=0, keepdims=True)
        packed = fold(packed)
        for device in range(grams.shape[0]):
            grams[device, : n // 2, 0, :] = packed
            grams[device, n // 2] = mass_diag

    def k_b0(red, kb, mb, u, ko_out, mo_out, c0_out, words, small, theta_out):
        packed, mass_diag = red[0, : n // 2, 0, :], red[0, n // 2]
        for device in range(1, red.shape[0]):
            packed = packed + red[device, : n // 2, 0, :]
            mass_diag = mass_diag + red[device, n // 2]
        packed = unfold(packed)
        turned, g_u1b, g_u2b, g_km = blocks_of(packed, n)[:4]
        lane, row = lane_row((n, MAT))
        g_bb = jnp.where(lane < n, jnp.where(lane <= row, packed, turned), 0.0)
        g_mm = jnp.where(lane == row, mass_diag, jnp.where(lane > row, packed, turned))
        g_mm = jnp.where(lane < n, g_mm, 0.0)
        inv_v, inv_c = inverse_chols(g_bb, g_mm)
        lv, lc = inv_v[:, :n], inv_c[:, :n]
        cross = nt(mm(lv, g_km[:, :n]), lc)
        theta = diagonal(cross) * diagonal(inv_c) / diagonal(inv_v)
        g1 = mm3(lv, u[:n])
        both = mm3(rows([lv, lc]), u[n:])
        g2, f1 = both[:n], both[n:]
        for k, value in ((0, f1), (3, g1), (4, g2)):
            words[k * n : (k + 1) * n] = value
        c0_out[...] = -relax * (g1 - theta * g2)
        ko_out[...] = mm3(lv, kb[...])
        mo_out[...] = mm3(lv, mb[...])
        e1 = nt(mm(lv, g_u1b[:, :n]), lv)
        e2 = nt(mm(lv, g_u2b[:, :n]), lv)
        right = -relax * (e1 - theta * e2)
        for k, value in enumerate((cross, g_mm[:, :n], e1, e2, g_u2b[:, :n], theta, lv, lc, right)):
            put_small(small, k, value)
        theta_out[...] = jnp.sum(jnp.where(lane == row, theta, 0.0), axis=0, keepdims=True)[:, :n]

    def k_b1(
        cols, iface, h_a, h_f, h_b, w_high, w_low, inv_d, ko, mo, c0, words_in, small,
        p_out, image_out, words, words_halo, kf_out, outgoing, xs, res,
    ):
        lv, lc, right = (get_small(small, k) for k in (6, 7, 8))
        theta = small[5 * n : 6 * n, :1]
        g1 = mm3(lv, halo_lanes((h_a, h_f, h_b), 0, n))
        both = mm3(rows([lv, lc]), halo_lanes((h_a, h_f, h_b), n, 2 * n))
        g2, f1 = both[:n], both[n:]
        put_sources(xs, 0, rows([c0[...], words_in[:n]]))
        put_sources(xs, c0.shape[1] // xs.shape[2], rows([-relax * (g1 - theta * g2), f1]))
        apply_pair(xs, cols, w_high, w_low, res.at[0], res.at[1])
        for k, value in ((0, f1), (1, g1), (2, g2)):
            words_halo[k * n : (k + 1) * n] = value
        d = inv_d[...]
        image = res[0, :n] - theta * res[1, :n] - mm3(lanes([right, -theta * right]), rows([ko[...], mo[...]]))
        image_out[...] = image
        kf_out[:n] = res[0, n:]
        kf_out[n:] = res[1, n:]
        words[:n] = words_in[:n]
        words[n : 2 * n] = res[0, n:] * d
        words[2 * n : 3 * n] = res[1, n:] * d
        words[3 * n :] = words_in[3 * n :]
        p_out[...] = 2.0 * c0[...] - relax * d * image
        send_tiles(iface, outgoing, 0, p_out)
        send_tiles(iface, outgoing, n, words.at[n : 3 * n])

    def k_c0(small, basis, mb, image0, kf, p, words, v_out, tests_high, tests_low, small_b, part):
        lv, lc = get_small(small, 6), get_small(small, 7)
        v = mm3(lv, basis[...])
        v_out[...] = v
        high, low = split(rows([mm3(lc, mb[...]), v]))
        tests_high[...] = high
        tests_low[...] = low
        mass = nt(mm(lv, get_small(small, 1)), lc)
        ef = nt(mm(lc, get_small(small, 4)), lv)
        for k, value in enumerate((mass, ef, mm(ef, get_small(small, 0)), mm(ef, mass))):
            put_small(small_b, k, value)
        right = rows([image0[...], kf[...], p[...], words[n : 3 * n], jnp.zeros((2 * n, p.shape[1]), F32)])
        both = nt3(high, low, right) * scale
        lane, _ = lane_row((n, MAT))
        part[...] = jnp.where(lane < 3 * n, both[:n], both[n:])

    def half(cols, p, halo, small, c0, w_high, w_low, inv_d, tests_high, tests_low, xs, res):
        put_sources(xs, 0, p)
        put_sources(xs, p.shape[1] // xs.shape[2], halo)
        apply_pair(xs, cols, w_high, w_low, res.at[0], res.at[1])
        theta = small[5 * n : 6 * n, :1]
        image = res[0] - theta * res[1]
        fresh = p + c0[...] - relax * inv_d[...] * image
        both = nt3(tests_high[...], tests_low[...], rows([image, fresh])) * scale
        both = lanes([both, jnp.zeros((2 * n, MAT - 2 * n), F32)])
        lane, _ = lane_row((n, MAT))
        return fresh, jnp.where(lane < n, both[:n], both[n:])

    def k_c1(
        cols, iface, p, h_a, h_f, h_b, c0, small, part, pair, tests_high, tests_low, w_high, w_low, inv_d,
        p_out, outgoing, grams, xs, res,
    ):
        fresh, added = half(
            cols, p[...], halo_lanes((h_a, h_f, h_b), 0, n), small, c0, w_high, w_low, inv_d,
            tests_high, tests_low, xs, res,
        )
        p_out[...] = fresh
        send_tiles(iface, outgoing, 0, p_out)
        chip = part[...] + pair[...]
        chip = jnp.where(lax.axis_index("parts") % 2 == 0, chip, pltpu.roll(chip, MAT - 3 * n, 1))
        lane, _ = lane_row((n, MAT))
        first = jnp.where(lane < 3 * n, chip, pltpu.roll(added, 3 * n, 1))
        packed = fold(jnp.where(lane < 4 * n, first, 0.0))
        fifth = pack_rows(jnp.where(lane < n, pltpu.roll(added, MAT - n, 1), 0.0))
        for device in range(grams.shape[0]):
            grams[device, : n // 2, 0, :] = packed
            for k in range(2):
                grams[device, n // 2 + k] = fifth[k]

    def solve(small, small_b, kf_test, mf_test, g_left, g_p, g_a):
        cross, mass, ef = get_small(small, 0), get_small(small_b, 0), get_small(small_b, 1)
        theta = small[5 * n : 6 * n, :1]
        right = g_p + relax * mm(g_left, ef)
        left = g_a + mm(
            lanes([relax * g_left, -relax * theta * g_left, -g_p, theta * g_p]),
            rows([kf_test, mf_test, cross, mass]),
        )
        return lanes(
            [
                relax * (g_left + left),
                -relax * relax * g_left,
                relax * relax * theta * g_left,
                relax * right,
                -relax * theta * right,
            ]
        )

    def k_d0(red, p, words, small, small_b, c_out, tests_out, onto_v, coefs):
        half_n = n // 2
        sums = [red[device, :half_n, 0, :] for device in range(2)]
        fifth = [red[0, half_n + k] + red[1, half_n + k] for k in range(2)]
        for device in range(2, red.shape[0]):
            sums[device % 2] = sums[device % 2] + red[device, :half_n, 0, :]
            for k in range(2):
                fifth[k] = fifth[k] + red[device, half_n + k]
        lane, _ = lane_row((n, MAT))
        whole = jnp.where(lane < 4 * n, unfold(sums[0]), jnp.where(lane < 5 * n, unpack_rows(fifth, half_n), 0.0))
        g_left, g_kf, g_mf, g_a, g_fresh = (value[:, :n] for value in blocks_of(whole, n)[:5])
        g_p, g_h1, g_h2, g_a_odd = (value[:, :n] for value in blocks_of(unfold(sums[1]), n)[:4])
        g_a = g_a + g_a_odd
        kf_test, mf_test = g_kf - get_small(small_b, 2), g_mf - get_small(small_b, 3)
        coef = solve(small, small_b, kf_test, mf_test, g_left, g_p, g_a)
        c_out[...] = p[...] + mm3(coef, words[...])
        put_small(tests_out, 0, kf_test)
        put_small(tests_out, 1, mf_test)
        onto = (get_small(small_b, 1), g_h1, g_h2, get_small(small, 2), get_small(small, 3))
        for k, value in enumerate(onto):
            put_small(onto_v, k, value)
        coefs[:n] = lanes([coef, jnp.zeros((n, MAT - 5 * n), F32)])
        put_small(coefs, 1, g_fresh + mm(coef, rows(list(onto))))

    def k_d1(
        cols, iface, c_local, coefs, h_a, h_f, h_b, q_a, q_f, q_b, ko, mo, c0, words_halo, small,
        w_high, w_low, inv_d, p_out, image_out, outgoing, xs, res,
    ):
        coef, right = coefs[:n, : 5 * n], get_small(coefs, 1)
        theta = small[5 * n : 6 * n, :1]
        around = rows([words_halo[:n], halo_lanes((q_a, q_f, q_b), n, 3 * n), words_halo[n:]])
        c_halo = halo_lanes((h_a, h_f, h_b), 0, n) + mm3(coef, around)
        put_sources(xs, 0, c_local[...])
        put_sources(xs, c_local.shape[1] // xs.shape[2], c_halo)
        apply_pair(xs, cols, w_high, w_low, res.at[0], res.at[1])
        image = res[0] - theta * res[1] - mm3(lanes([right, -theta * right]), rows([ko[...], mo[...]]))
        image_out[...] = image
        p_out[...] = c_local[...] + c0[...] - relax * inv_d[...] * image
        send_tiles(iface, outgoing, 0, p_out)

    def k_e0(image2, p, tests_high, tests_low, v, words, onto_v, part, last_high, last_low):
        right = rows([image2[...], p[...], jnp.zeros((MAT - 2 * n, p.shape[1]), F32)])
        both = nt3(tests_high[...], tests_low[...], right) * scale
        lane, _ = lane_row((n, MAT))
        part[...] = jnp.where(lane < n, both[:n], both[n:])
        free = words[...] - mm3(onto_v[:, :n], v[...])
        last_high[...], last_low[...] = split(rows([free, v[...]]))

    def k_e1(
        cols, p, h_a, h_f, h_b, c0, small, part, tests_high, tests_low, w_high, w_low, inv_d, p_out, grams, xs, res
    ):
        fresh, added = half(
            cols, p[...], halo_lanes((h_a, h_f, h_b), 0, n), small, c0, w_high, w_low, inv_d,
            tests_high, tests_low, xs, res,
        )
        p_out[...] = fresh
        lane, _ = lane_row((n, MAT))
        both = jnp.where(lane < 2 * n, part[...], pltpu.roll(added, 2 * n, 1))
        fill_blocks(grams, fold(jnp.where(lane < 4 * n, both, 0.0)))

    def k_f(red, p, small, small_b, tests_in, last_high, last_low, out):
        g_left, g_p, g_a, g_fresh = (value[:, :n] for value in blocks_of(unfold(total(red)), n)[:4])
        coef = solve(small, small_b, get_small(tests_in, 0), get_small(tests_in, 1), g_left, g_p, g_a)
        high, low = split(lanes([coef, -g_fresh]))
        both = jnp.dot(rows([high, low]), last_high[...], preferred_element_type=F32)
        low = jnp.dot(high, last_low[...], preferred_element_type=F32)
        out[...] = p[...] + both[:n] + both[n:] + low

    return k_a, k_b0, k_b1, k_c0, k_c1, k_d0, k_d1, k_e0, k_e1, k_f


def shards(basis, k_tiles, m_tiles, tile_part, tile_slot, iface):
    n, local = basis.shape
    tiles, blocks, width, _ = k_tiles.shape
    count = iface.shape[0]
    parts = lax.axis_size("parts")
    half_way = parts // 2
    scale = 1.0 / (local * parts)
    chip = [(source, source ^ 1) for source in range(parts)]
    other = [(source, (source + 1 if source % 2 else source - 1) % parts) for source in range(parts)]
    far = [(source, (source + half_way) % parts) for source in range(parts)]

    def halo(outgoing):
        return [lax.ppermute(outgoing, "parts", pairs) for pairs in (chip, far, other)]

    def reduced(blocks_out):
        return lax.all_to_all(blocks_out, "parts", 0, 0, tiled=True)

    k_a, k_b0, k_b1, k_c0, k_c1, k_d0, k_d1, k_e0, k_e1, k_f = make_kernels(n, scale)
    sources = tiles + 3 * count
    xs = lambda m: pltpu.VMEM((sources, 2 * m, width), BF16)
    vec = ((n, local), F32)
    vecs = lambda m: ((m * n, local), F32)
    mats = lambda m: ((m * n, MAT), F32)
    out = lambda m: ((count, m, width), F32)
    grams8 = ((parts, n // 2, MAT), F32)
    res = pltpu.VMEM((2, n, local), F32)

    (outgoing,) = call(
        k_first,
        [out(n)],
        [HBM, HBM],
        [pltpu.SMEM((count,), jnp.int32), pltpu.VMEM((n, local), F32), pltpu.SemaphoreType.DMA((2,))],
    )(in_hbm(iface), in_hbm(basis))
    h0 = halo(outgoing)
    w_high, w_low, inv_d, cols = call(
        make_prep(count),
        [((tiles, blocks * width, 2 * width), BF16)] * 2 + [((1, local), F32), ((tiles, blocks), jnp.int32)],
        [HBM] * 4,
        [pltpu.VMEM(k_tiles.shape, F32)] * 2
        + [pltpu.VMEM((tiles, blocks), jnp.int32)] * 2
        + [pltpu.SemaphoreType.DMA((2, tiles + 1))],
    )(*(in_hbm(value) for value in (tile_part, tile_slot, k_tiles, m_tiles)))
    w = (w_high, w_low, inv_d)
    packed = ((parts, n // 2 + 1, 1, MAT), F32)
    kb, mb, u, outgoing, grams = call(
        k_a, [vec, vec, vecs(2), out(2 * n), packed], [SM, SM] + [VM] * 7, [xs(n)]
    )(cols, iface, basis, *h0, *w)
    red = reduced(grams)
    h1 = halo(outgoing)
    ko, mo, c0, words, small, theta = call(
        k_b0, [vec] * 3 + [vecs(5), mats(9), ((1, n), F32)], [VM] * 4
    )(red, kb, mb, u)
    p1, image0, words, words_halo, kf, outgoing = call(
        k_b1,
        [vec, vec, vecs(5), ((3 * n, 3 * count * width), F32), vecs(2), out(3 * n)],
        [SM, SM] + [VM] * 11,
        [xs(2 * n), pltpu.VMEM((2, 2 * n, local), F32)],
    )(cols, iface, *h1, *w, ko, mo, c0, words, small)
    h2 = halo(outgoing)
    v, tests_high, tests_low, small_b, part = call(
        k_c0, [vec] + [((2 * n, local), BF16)] * 2 + [mats(4), mats(1)], [VM] * 7
    )(small, basis, mb, image0, kf, p1, words)
    tests = (tests_high, tests_low)
    pair = lax.ppermute(part, "parts", chip)
    packed = ((parts, n // 2 + 2, 1, MAT), F32)
    p2, outgoing, grams = call(k_c1, [vec, out(n), packed], [SM, SM] + [VM] * 13, [xs(n), res])(
        cols, iface, p1, *h2, c0, small, part, pair, *tests, *w
    )
    red = reduced(grams)
    h3 = halo(outgoing)
    c2, word_tests, onto_v, coefs = call(k_d0, [vec, mats(2), mats(5), mats(2)], [VM] * 5)(
        red, p2, words, small, small_b
    )
    p3, image2, outgoing = call(k_d1, [vec, vec, out(n)], [SM, SM] + [VM] * 16, [xs(n), res])(
        cols, iface, c2, coefs, *h3, *h2, ko, mo, c0, words_halo, small, *w
    )
    h4 = halo(outgoing)
    part, *last = call(k_e0, [mats(1)] + [((6 * n, local), BF16)] * 2, [VM] * 7)(image2, p3, *tests, v, words, onto_v)
    p4, grams = call(k_e1, [vec, grams8], [SM] + [VM] * 12, [xs(n), res])(cols, p3, *h4, c0, small, part, *tests, *w)
    red = reduced(grams)
    (correct,) = call(k_f, [vec], [VM] * 7)(red, p4, small, small_b, word_tests, *last)
    return (correct, theta.reshape(-1))


def solution(mesh):
    placed = (
        P(None, "parts"),
        P("parts", None, None, None),
        P("parts", None, None, None),
        P("parts", None),
        P("parts", None),
        P("parts"),
    )
    return jax.shard_map(
        shards, mesh=mesh, in_specs=placed, out_specs=(P(None, "parts"), P()), check_vma=False
    )
```

```python
import jax
import jax.numpy as jnp
from jax import lax
from jax.experimental import pallas as pl
from jax.experimental.pallas import tpu as pltpu
from jax.sharding import PartitionSpec as P


relax = 0.4

F32 = jnp.float32
BF16 = jnp.bfloat16
VM = pl.BlockSpec(memory_space=pltpu.VMEM)
HBM = pl.BlockSpec(memory_space=pltpu.MemorySpace.HBM)
MAT = 128


def call(kernel, outs, specs, scratch=()):
    return pl.pallas_call(
        kernel,
        in_specs=specs,
        out_specs=[VM] * len(outs),
        out_shape=[jax.ShapeDtypeStruct(shape, dtype) for shape, dtype in outs],
        scratch_shapes=list(scratch),
        compiler_params=pltpu.CompilerParams(vmem_limit_bytes=24 << 20),
    )


def in_hbm(value):
    return pltpu.with_memory_space_constraint(value, pltpu.MemorySpace.HBM)


def mm(left, right):
    return jnp.dot(left, right, precision=lax.Precision.HIGHEST, preferred_element_type=F32)


def nt(left, right):
    return lax.dot_general(
        left, right, (((1,), (1,)), ((), ())), precision=lax.Precision.HIGHEST, preferred_element_type=F32
    )


def split(value):
    high = value.astype(BF16)
    return high, (value - high.astype(F32)).astype(BF16)


def mm3(left, right):
    lh, ll = split(left)
    rh, rl = split(right)
    n = left.shape[0]
    both = jnp.dot(jnp.concatenate([lh, ll], axis=0), rh, preferred_element_type=F32)
    return both[:n] + both[n:] + jnp.dot(lh, rl, preferred_element_type=F32)


def nt3(high, low, right):
    dims = (((1,), (1,)), ((), ()))
    n = high.shape[0]
    left = jnp.concatenate([high, low], axis=0)
    both = sum(lax.dot_general(left, part, dims, preferred_element_type=F32) for part in split(right))
    return both[:n] + both[n:]


def rows(parts):
    return jnp.concatenate(parts, axis=0)


def lanes(parts):
    return jnp.concatenate(parts, axis=1)


def halo_lanes(refs, first, last):
    return lanes([ref[slot, first:last] for ref in refs for slot in range(ref.shape[0])])


def put_sources(xs, at, value):
    n, width = value.shape[0], xs.shape[2]
    for t in range(value.shape[1] // width):
        high, low = split(value[:, t * width : (t + 1) * width])
        xs[at + t, :n] = high
        xs[at + t, n:] = low


def apply_pair(xs, cols, w_high, w_low, k_out, m_out):
    tiles, blocks = cols.shape
    width = xs.shape[2]
    n = xs.shape[1] // 2
    for i in range(tiles):
        lhs = lanes([xs[cols[i, b]] for b in range(blocks)])
        both = jnp.dot(lhs, w_high[i], preferred_element_type=F32)
        low = jnp.dot(lhs[:n], w_low[i], preferred_element_type=F32)
        result = both[:n] + both[n:] + low
        k_out[:, i * width : (i + 1) * width] = result[:, :width]
        m_out[:, i * width : (i + 1) * width] = result[:, width:]


def apply_iface(xs, cols, w_high, w_low, tile):
    n = xs.shape[1] // 2
    width = xs.shape[2]
    lhs = lanes([xs[cols[tile, b]] for b in range(cols.shape[1])])
    both = jnp.dot(lhs, w_high[tile], preferred_element_type=F32)
    low = jnp.dot(lhs[:n], w_low[tile], preferred_element_type=F32)
    result = both[:n] + both[n:] + low
    return result[:, :width], result[:, width:]


def lanes_of(tile, width):
    return pl.ds(pl.multiple_of(tile * width, width), width)


def send_tiles(iface, outgoing, at, ref):
    width = outgoing.shape[2]
    n = ref.shape[0]
    for slot in range(outgoing.shape[0]):
        start = pl.multiple_of(iface[slot] * width, width)
        outgoing[slot, at : at + n] = ref[:, pl.ds(start, width)]


def lane_row(shape):
    return lax.broadcasted_iota(jnp.int32, shape, 1), lax.broadcasted_iota(jnp.int32, shape, 0)


def blocks_of(summed, n):
    square = rows([summed, jnp.zeros((MAT - n, MAT), F32)])
    turned = square.T
    return [turned[k * n : (k + 1) * n] for k in range(MAT // n)]


def inverse_chols(first, second):
    n = first.shape[0]
    shape = first.shape
    lane, row = lane_row(shape)
    half = MAT // 2
    columns = [
        jnp.where(
            lane < half,
            jnp.broadcast_to(first[:, j : j + 1], shape),
            jnp.broadcast_to(second[:, j : j + 1], shape),
        )
        for j in range(n)
    ]
    inverse = jnp.where(lane % half == row, 1.0, 0.0)
    pivots = jnp.ones(shape, F32)
    for k in range(n):
        pivot = columns[k][k : k + 1, :]
        pivots = jnp.where(row == k, pivot, pivots)
        if k == n - 1:
            break
        factor = jnp.where(row > k, columns[k], 0.0) * (1.0 / pivot)
        for j in range(k + 1, n):
            columns[j] = columns[j] - factor * columns[j][k : k + 1, :]
        inverse = inverse - factor * inverse[k : k + 1, :]
    inverse = inverse * lax.rsqrt(pivots)
    return [jnp.where(lane < n, value, 0.0) for value in (inverse, pltpu.roll(inverse, half, 1))]


def diagonal(a):
    lane, row = lane_row(a.shape)
    return jnp.sum(jnp.where(lane == row, a, 0.0), axis=1, keepdims=True)


def k_first(iface_hbm, basis_hbm, outgoing, iface, basis, sems):
    copies = [
        pltpu.make_async_copy(iface_hbm, iface, sems.at[0]),
        pltpu.make_async_copy(basis_hbm, basis, sems.at[1]),
    ]
    for copy in copies:
        copy.start()
    for copy in copies:
        copy.wait()
    send_tiles(iface, outgoing, 0, basis)


def make_prep(count):
    def k_prep(part_hbm, slot_hbm, k_hbm, m_hbm, w_high, w_low, inv_d, cols, k, m, part_in, slot_in, sems):
        tiles, blocks, width, _ = k.shape
        pattern = [
            pltpu.make_async_copy(source, target, sems.at[which, tiles])
            for which, (source, target) in enumerate(((part_hbm, part_in), (slot_hbm, slot_in)))
        ]
        for copy in pattern:
            copy.start()
        copies = []
        for i in range(tiles):
            pair = [
                pltpu.make_async_copy(source.at[i], target.at[i], sems.at[which, i])
                for which, (source, target) in enumerate(((k_hbm, k), (m_hbm, m)))
            ]
            for copy in pair:
                copy.start()
            copies.append(pair)
        parts = lax.axis_size("parts")
        me = lax.axis_index("parts")
        for copy in pattern:
            copy.wait()
        part, slot = part_in[...], slot_in[...]
        remote = jnp.where(part == me ^ 1, 0, jnp.where(part == (me + parts // 2) % parts, count, 2 * count))
        cols[...] = jnp.where(part == me, slot, tiles + remote + slot)
        row = lax.broadcasted_iota(jnp.int32, (width, width), 0)
        lane = lax.broadcasted_iota(jnp.int32, (width, width), 1)
        for i in range(tiles):
            for which, source in enumerate((k, m)):
                copies[i][which].wait()
                for b in range(blocks):
                    high, low = split(source[i, b].T)
                    w_high[i, b * width : (b + 1) * width, which * width : (which + 1) * width] = high
                    w_low[i, b * width : (b + 1) * width, which * width : (which + 1) * width] = low
            diag = jnp.sum(jnp.where(row == lane, k[i, 0], 0.0), axis=0, keepdims=True)
            inv_d[:, i * width : (i + 1) * width] = 1.0 / diag

    return k_prep


def fill_blocks(out, value):
    for device in range(out.shape[0]):
        out[device] = value


def total(ref):
    value = ref[0]
    for device in range(1, ref.shape[0]):
        value = value + ref[device]
    return value


def fold(value):
    half = value.shape[0] // 2
    return value[:half] + pltpu.roll(value[half:], MAT // 2, 1)


def unfold(value):
    lane, _ = lane_row(value.shape)
    keep = lane < MAT // 2
    return rows([jnp.where(keep, value, 0.0), jnp.where(keep, pltpu.roll(value, MAT // 2, 1), 0.0)])


def pack_rows(value):
    lane, row = lane_row(value.shape)
    m = value.shape[0] // 2
    n = MAT // m
    shift = n
    while shift < MAT:
        value = value + pltpu.roll(value, shift, 1)
        shift *= 2
    value = jnp.where(lane // n == row % m, value, 0.0)
    return [jnp.sum(value[k * m : (k + 1) * m], axis=0, keepdims=True) for k in range(2)]


def unpack_rows(pair, m):
    value = rows([jnp.broadcast_to(part, (m, MAT)) for part in pair])
    lane, row = lane_row(value.shape)
    n = MAT // m
    value = jnp.where(lane // n == row % m, value, 0.0)
    shift = n
    while shift < MAT:
        value = value + pltpu.roll(value, shift, 1)
        shift *= 2
    return value


def make_kernels(n, scale):
    def put_small(ref, k, value):
        ref[k * n : (k + 1) * n] = jnp.broadcast_to(value, (n, MAT)) if value.shape[1] == 1 else lanes(
            [value, jnp.zeros((n, MAT - n), F32)]
        )

    def get_small(ref, k):
        return ref[k * n : (k + 1) * n, :n]

    def k_a(cols, iface, basis, h_a, h_f, h_b, w_high, w_low, inv_d, kb, mb, u, outgoing, grams, xs):
        put_sources(xs, 0, basis[...])
        put_sources(xs, basis.shape[1] // xs.shape[2], halo_lanes((h_a, h_f, h_b), 0, n))
        apply_pair(xs, cols, w_high, w_low, kb, mb)
        d = inv_d[...]
        u[:n] = kb[...] * d
        u[n:] = mb[...] * d
        send_tiles(iface, outgoing, 0, u)
        right = rows([basis[...], u[...], kb[...], mb[...], jnp.zeros((MAT - 5 * n, basis.shape[1]), F32)])
        both = nt3(*split(rows([basis[...], mb[...]])), right) * scale
        lane, row = lane_row((n, MAT))
        chosen = jnp.where(lane < 3 * n, both[:n], both[n:])
        mass = pltpu.roll(chosen, MAT - 4 * n, 1)
        packed = jnp.where((lane < n) & (lane > row), mass, jnp.where(lane < 4 * n, chosen, 0.0))
        mass_diag = jnp.sum(jnp.where((lane == row) & (lane < n), mass, 0.0), axis=0, keepdims=True)
        packed = fold(packed)
        for device in range(grams.shape[0]):
            grams[device, : n // 2, 0, :] = packed
            grams[device, n // 2] = mass_diag

    def k_b0(red, kb, mb, u, ko_out, mo_out, c0_out, words, small, theta_out):
        packed, mass_diag = red[0, : n // 2, 0, :], red[0, n // 2]
        for device in range(1, red.shape[0]):
            packed = packed + red[device, : n // 2, 0, :]
            mass_diag = mass_diag + red[device, n // 2]
        packed = unfold(packed)
        turned, g_u1b, g_u2b, g_km = blocks_of(packed, n)[:4]
        lane, row = lane_row((n, MAT))
        g_bb = jnp.where(lane < n, jnp.where(lane <= row, packed, turned), 0.0)
        g_mm = jnp.where(lane == row, mass_diag, jnp.where(lane > row, packed, turned))
        g_mm = jnp.where(lane < n, g_mm, 0.0)
        inv_v, inv_c = inverse_chols(g_bb, g_mm)
        lv, lc = inv_v[:, :n], inv_c[:, :n]
        cross = nt(mm(lv, g_km[:, :n]), lc)
        theta = diagonal(cross) * diagonal(inv_c) / diagonal(inv_v)
        g1 = mm3(lv, u[:n])
        both = mm3(rows([lv, lc]), u[n:])
        g2, f1 = both[:n], both[n:]
        for k, value in ((0, f1), (3, g1), (4, g2)):
            words[k * n : (k + 1) * n] = value
        c0_out[...] = -relax * (g1 - theta * g2)
        ko_out[...] = mm3(lv, kb[...])
        mo_out[...] = mm3(lv, mb[...])
        e1 = nt(mm(lv, g_u1b[:, :n]), lv)
        e2 = nt(mm(lv, g_u2b[:, :n]), lv)
        right = -relax * (e1 - theta * e2)
        for k, value in enumerate((cross, g_mm[:, :n], e1, e2, g_u2b[:, :n], theta, lv, lc, right)):
            put_small(small, k, value)
        theta_out[...] = jnp.sum(jnp.where(lane == row, theta, 0.0), axis=0, keepdims=True)[:, :n]

    def k_b1(
        cols, iface, h_a, h_f, h_b, w_high, w_low, inv_d, ko, mo, c0, words_in, small, words_halo, outgoing, xs
    ):
        lv, lc, right = (get_small(small, k) for k in (6, 7, 8))
        theta = small[5 * n : 6 * n, :1]
        g1 = mm3(lv, halo_lanes((h_a, h_f, h_b), 0, n))
        both = mm3(rows([lv, lc]), halo_lanes((h_a, h_f, h_b), n, 2 * n))
        g2, f1 = both[:n], both[n:]
        put_sources(xs, 0, rows([c0[...], words_in[:n]]))
        put_sources(xs, c0.shape[1] // xs.shape[2], rows([-relax * (g1 - theta * g2), f1]))
        for k, value in ((0, f1), (1, g1), (2, g2)):
            words_halo[k * n : (k + 1) * n] = value
        coef = lanes([right, -theta * right])
        for slot in range(outgoing.shape[0]):
            tile = iface[slot]
            at = lanes_of(tile, xs.shape[2])
            k_tile, m_tile = apply_iface(xs, cols, w_high, w_low, tile)
            d = inv_d[:, at]
            image = k_tile[:n] - theta * m_tile[:n] - mm3(coef, rows([ko[:, at], mo[:, at]]))
            outgoing[slot, :n] = 2.0 * c0[:, at] - relax * d * image
            outgoing[slot, n : 2 * n] = k_tile[n:] * d
            outgoing[slot, 2 * n :] = m_tile[n:] * d

    def k_b2(
        cols, xs, w_high, w_low, inv_d, ko, mo, c0, words_in, small, p_out, image_out, words, kf_out, res
    ):
        right = get_small(small, 8)
        theta = small[5 * n : 6 * n, :1]
        apply_pair(xs, cols, w_high, w_low, res.at[0], res.at[1])
        d = inv_d[...]
        image = res[0, :n] - theta * res[1, :n] - mm3(lanes([right, -theta * right]), rows([ko[...], mo[...]]))
        image_out[...] = image
        kf_out[:n] = res[0, n:]
        kf_out[n:] = res[1, n:]
        words[:n] = words_in[:n]
        words[n : 2 * n] = res[0, n:] * d
        words[2 * n : 3 * n] = res[1, n:] * d
        words[3 * n :] = words_in[3 * n :]
        p_out[...] = 2.0 * c0[...] - relax * d * image

    def k_c0(small, basis, mb, image0, kf, p, words, v_out, tests_high, tests_low, small_b, part):
        lv, lc = get_small(small, 6), get_small(small, 7)
        v = mm3(lv, basis[...])
        v_out[...] = v
        high, low = split(rows([mm3(lc, mb[...]), v]))
        tests_high[...] = high
        tests_low[...] = low
        mass = nt(mm(lv, get_small(small, 1)), lc)
        ef = nt(mm(lc, get_small(small, 4)), lv)
        for k, value in enumerate((mass, ef, mm(ef, get_small(small, 0)), mm(ef, mass))):
            put_small(small_b, k, value)
        right = rows([image0[...], kf[...], p[...], words[n : 3 * n], jnp.zeros((2 * n, p.shape[1]), F32)])
        both = nt3(high, low, right) * scale
        lane, _ = lane_row((n, MAT))
        part[...] = jnp.where(lane < 3 * n, both[:n], both[n:])

    def half(cols, p, halo, small, c0, w_high, w_low, inv_d, tests_high, tests_low, xs, res):
        put_sources(xs, 0, p)
        put_sources(xs, p.shape[1] // xs.shape[2], halo)
        apply_pair(xs, cols, w_high, w_low, res.at[0], res.at[1])
        theta = small[5 * n : 6 * n, :1]
        image = res[0] - theta * res[1]
        fresh = p + c0[...] - relax * inv_d[...] * image
        both = nt3(tests_high[...], tests_low[...], rows([image, fresh])) * scale
        both = lanes([both, jnp.zeros((2 * n, MAT - 2 * n), F32)])
        lane, _ = lane_row((n, MAT))
        return fresh, jnp.where(lane < n, both[:n], both[n:])

    def k_c1(
        cols, iface, p, h_a, h_f, h_b, c0, small, part, pair, tests_high, tests_low, w_high, w_low, inv_d,
        p_out, outgoing, grams, xs, res,
    ):
        fresh, added = half(
            cols, p[...], halo_lanes((h_a, h_f, h_b), 0, n), small, c0, w_high, w_low, inv_d,
            tests_high, tests_low, xs, res,
        )
        p_out[...] = fresh
        send_tiles(iface, outgoing, 0, p_out)
        chip = part[...] + pair[...]
        chip = jnp.where(lax.axis_index("parts") % 2 == 0, chip, pltpu.roll(chip, MAT - 3 * n, 1))
        lane, _ = lane_row((n, MAT))
        first = jnp.where(lane < 3 * n, chip, pltpu.roll(added, 3 * n, 1))
        packed = fold(jnp.where(lane < 4 * n, first, 0.0))
        fifth = pack_rows(jnp.where(lane < n, pltpu.roll(added, MAT - n, 1), 0.0))
        for device in range(grams.shape[0]):
            grams[device, : n // 2, 0, :] = packed
            for k in range(2):
                grams[device, n // 2 + k] = fifth[k]

    def solve(small, small_b, kf_test, mf_test, g_left, g_p, g_a):
        cross, mass, ef = get_small(small, 0), get_small(small_b, 0), get_small(small_b, 1)
        theta = small[5 * n : 6 * n, :1]
        right = g_p + relax * mm(g_left, ef)
        left = g_a + mm(
            lanes([relax * g_left, -relax * theta * g_left, -g_p, theta * g_p]),
            rows([kf_test, mf_test, cross, mass]),
        )
        return lanes(
            [
                relax * (g_left + left),
                -relax * relax * g_left,
                relax * relax * theta * g_left,
                relax * right,
                -relax * theta * right,
            ]
        )

    def k_d0(red, p, words, small, small_b, c_out, tests_out, onto_v, coefs):
        half_n = n // 2
        sums = [red[device, :half_n, 0, :] for device in range(2)]
        fifth = [red[0, half_n + k] + red[1, half_n + k] for k in range(2)]
        for device in range(2, red.shape[0]):
            sums[device % 2] = sums[device % 2] + red[device, :half_n, 0, :]
            for k in range(2):
                fifth[k] = fifth[k] + red[device, half_n + k]
        lane, _ = lane_row((n, MAT))
        whole = jnp.where(lane < 4 * n, unfold(sums[0]), jnp.where(lane < 5 * n, unpack_rows(fifth, half_n), 0.0))
        g_left, g_kf, g_mf, g_a, g_fresh = (value[:, :n] for value in blocks_of(whole, n)[:5])
        g_p, g_h1, g_h2, g_a_odd = (value[:, :n] for value in blocks_of(unfold(sums[1]), n)[:4])
        g_a = g_a + g_a_odd
        kf_test, mf_test = g_kf - get_small(small_b, 2), g_mf - get_small(small_b, 3)
        coef = solve(small, small_b, kf_test, mf_test, g_left, g_p, g_a)
        c_out[...] = p[...] + mm3(coef, words[...])
        put_small(tests_out, 0, kf_test)
        put_small(tests_out, 1, mf_test)
        onto = (get_small(small_b, 1), g_h1, g_h2, get_small(small, 2), get_small(small, 3))
        for k, value in enumerate(onto):
            put_small(onto_v, k, value)
        coefs[:n] = lanes([coef, jnp.zeros((n, MAT - 5 * n), F32)])
        put_small(coefs, 1, g_fresh + mm(coef, rows(list(onto))))

    def k_d1(
        cols, iface, c_local, coefs, h_a, h_f, h_b, q_a, q_f, q_b, ko, mo, c0, words_halo, small,
        w_high, w_low, inv_d, outgoing, xs,
    ):
        coef, right = coefs[:n, : 5 * n], get_small(coefs, 1)
        theta = small[5 * n : 6 * n, :1]
        around = rows([words_halo[:n], halo_lanes((q_a, q_f, q_b), n, 3 * n), words_halo[n:]])
        c_halo = halo_lanes((h_a, h_f, h_b), 0, n) + mm3(coef, around)
        put_sources(xs, 0, c_local[...])
        put_sources(xs, c_local.shape[1] // xs.shape[2], c_halo)
        onto = lanes([right, -theta * right])
        for slot in range(outgoing.shape[0]):
            tile = iface[slot]
            at = lanes_of(tile, xs.shape[2])
            k_tile, m_tile = apply_iface(xs, cols, w_high, w_low, tile)
            image = k_tile - theta * m_tile - mm3(onto, rows([ko[:, at], mo[:, at]]))
            outgoing[slot] = c_local[:, at] + c0[:, at] - relax * inv_d[:, at] * image

    def k_d2(cols, xs, c_local, coefs, ko, mo, c0, small, w_high, w_low, inv_d, p_out, image_out, res):
        right = get_small(coefs, 1)
        theta = small[5 * n : 6 * n, :1]
        apply_pair(xs, cols, w_high, w_low, res.at[0], res.at[1])
        image = res[0] - theta * res[1] - mm3(lanes([right, -theta * right]), rows([ko[...], mo[...]]))
        image_out[...] = image
        p_out[...] = c_local[...] + c0[...] - relax * inv_d[...] * image

    def k_e0(image2, p, tests_high, tests_low, v, words, onto_v, part, last_high, last_low):
        right = rows([image2[...], p[...], jnp.zeros((MAT - 2 * n, p.shape[1]), F32)])
        both = nt3(tests_high[...], tests_low[...], right) * scale
        lane, _ = lane_row((n, MAT))
        part[...] = jnp.where(lane < n, both[:n], both[n:])
        free = words[...] - mm3(onto_v[:, :n], v[...])
        last_high[...], last_low[...] = split(rows([free, v[...]]))

    def k_e1(
        cols, p, h_a, h_f, h_b, c0, small, part, tests_high, tests_low, w_high, w_low, inv_d, p_out, grams, xs, res
    ):
        fresh, added = half(
            cols, p[...], halo_lanes((h_a, h_f, h_b), 0, n), small, c0, w_high, w_low, inv_d,
            tests_high, tests_low, xs, res,
        )
        p_out[...] = fresh
        lane, _ = lane_row((n, MAT))
        both = jnp.where(lane < 2 * n, part[...], pltpu.roll(added, 2 * n, 1))
        fill_blocks(grams, fold(jnp.where(lane < 4 * n, both, 0.0)))

    def k_f(red, p, small, small_b, tests_in, last_high, last_low, out):
        g_left, g_p, g_a, g_fresh = (value[:, :n] for value in blocks_of(unfold(total(red)), n)[:4])
        coef = solve(small, small_b, get_small(tests_in, 0), get_small(tests_in, 1), g_left, g_p, g_a)
        high, low = split(lanes([coef, -g_fresh]))
        both = jnp.dot(rows([high, low]), last_high[...], preferred_element_type=F32)
        low = jnp.dot(high, last_low[...], preferred_element_type=F32)
        out[...] = p[...] + both[:n] + both[n:] + low

    return k_a, k_b0, k_b1, k_b2, k_c0, k_c1, k_d0, k_d1, k_d2, k_e0, k_e1, k_f


def shards(basis, k_tiles, m_tiles, tile_part, tile_slot, iface):
    n, local = basis.shape
    tiles, blocks, width, _ = k_tiles.shape
    count = iface.shape[0]
    parts = lax.axis_size("parts")
    half_way = parts // 2
    scale = 1.0 / (local * parts)
    chip = [(source, source ^ 1) for source in range(parts)]
    other = [(source, (source + 1 if source % 2 else source - 1) % parts) for source in range(parts)]
    far = [(source, (source + half_way) % parts) for source in range(parts)]

    def halo(outgoing):
        return [lax.ppermute(outgoing, "parts", pairs) for pairs in (chip, far, other)]

    def reduced(blocks_out):
        return lax.all_to_all(blocks_out, "parts", 0, 0, tiled=True)

    k_a, k_b0, k_b1, k_b2, k_c0, k_c1, k_d0, k_d1, k_d2, k_e0, k_e1, k_f = make_kernels(n, scale)
    sources = tiles + 3 * count
    xs = lambda m: pltpu.VMEM((sources, 2 * m, width), BF16)
    vec = ((n, local), F32)
    vecs = lambda m: ((m * n, local), F32)
    mats = lambda m: ((m * n, MAT), F32)
    out = lambda m: ((count, m, width), F32)
    grams8 = ((parts, n // 2, MAT), F32)
    res = pltpu.VMEM((2, n, local), F32)

    (outgoing,) = call(
        k_first,
        [out(n)],
        [HBM, HBM],
        [pltpu.VMEM((count,), jnp.int32), pltpu.VMEM((n, local), F32), pltpu.SemaphoreType.DMA((2,))],
    )(in_hbm(iface), in_hbm(basis))
    h0 = halo(outgoing)
    w_high, w_low, inv_d, cols = call(
        make_prep(count),
        [((tiles, blocks * width, 2 * width), BF16)] * 2 + [((1, local), F32), ((tiles, blocks), jnp.int32)],
        [HBM] * 4,
        [pltpu.VMEM(k_tiles.shape, F32)] * 2
        + [pltpu.VMEM((tiles, blocks), jnp.int32)] * 2
        + [pltpu.SemaphoreType.DMA((2, tiles + 1))],
    )(*(in_hbm(value) for value in (tile_part, tile_slot, k_tiles, m_tiles)))
    w = (w_high, w_low, inv_d)
    packed = ((parts, n // 2 + 1, 1, MAT), F32)
    kb, mb, u, outgoing, grams = call(
        k_a, [vec, vec, vecs(2), out(2 * n), packed], [VM, VM] + [VM] * 7, [xs(n)]
    )(cols, iface, basis, *h0, *w)
    red = reduced(grams)
    h1 = halo(outgoing)
    ko, mo, c0, words, small, theta = call(
        k_b0, [vec] * 3 + [vecs(5), mats(9), ((1, n), F32)], [VM] * 4
    )(red, kb, mb, u)
    sources_of = lambda m: ((sources, 2 * m, width), BF16)
    words_halo, outgoing, source = call(
        k_b1, [((3 * n, 3 * count * width), F32), out(3 * n), sources_of(2 * n)], [VM, VM] + [VM] * 11
    )(cols, iface, *h1, *w, ko, mo, c0, words, small)
    h2 = halo(outgoing)
    p1, image0, words, kf = call(
        k_b2, [vec, vec, vecs(5), vecs(2)], [VM] + [VM] * 9, [pltpu.VMEM((2, 2 * n, local), F32)]
    )(cols, source, *w, ko, mo, c0, words, small)
    v, tests_high, tests_low, small_b, part = call(
        k_c0, [vec] + [((2 * n, local), BF16)] * 2 + [mats(4), mats(1)], [VM] * 7
    )(small, basis, mb, image0, kf, p1, words)
    tests = (tests_high, tests_low)
    pair = lax.ppermute(part, "parts", chip)
    packed = ((parts, n // 2 + 2, 1, MAT), F32)
    p2, outgoing, grams = call(k_c1, [vec, out(n), packed], [VM, VM] + [VM] * 13, [xs(n), res])(
        cols, iface, p1, *h2, c0, small, part, pair, *tests, *w
    )
    red = reduced(grams)
    h3 = halo(outgoing)
    c2, word_tests, onto_v, coefs = call(k_d0, [vec, mats(2), mats(5), mats(2)], [VM] * 5)(
        red, p2, words, small, small_b
    )
    outgoing, source = call(k_d1, [out(n), sources_of(n)], [VM, VM] + [VM] * 16)(
        cols, iface, c2, coefs, *h3, *h2, ko, mo, c0, words_halo, small, *w
    )
    h4 = halo(outgoing)
    p3, image2 = call(k_d2, [vec, vec], [VM] + [VM] * 10, [res])(cols, source, c2, coefs, ko, mo, c0, small, *w)
    part, *last = call(k_e0, [mats(1)] + [((6 * n, local), BF16)] * 2, [VM] * 7)(image2, p3, *tests, v, words, onto_v)
    p4, grams = call(k_e1, [vec, grams8], [VM] + [VM] * 12, [xs(n), res])(cols, p3, *h4, c0, small, part, *tests, *w)
    red = reduced(grams)
    (correct,) = call(k_f, [vec], [VM] * 7)(red, p4, small, small_b, word_tests, *last)
    return (correct, theta.reshape(-1))


def solution(mesh):
    placed = (
        P(None, "parts"),
        P("parts", None, None, None),
        P("parts", None, None, None),
        P("parts", None),
        P("parts", None),
        P("parts"),
    )
    return jax.shard_map(
        shards, mesh=mesh, in_specs=placed, out_specs=(P(None, "parts"), P()), check_vma=False
    )
```

```python
import jax
import jax.numpy as jnp
from jax import lax
from jax.experimental import pallas as pl
from jax.experimental.pallas import tpu as pltpu
from jax.sharding import PartitionSpec as P


relax = 0.4

F32 = jnp.float32
BF16 = jnp.bfloat16
VM = pl.BlockSpec(memory_space=pltpu.VMEM)
HBM = pl.BlockSpec(memory_space=pltpu.MemorySpace.HBM)
MAT = 128


def call(kernel, outs, specs, scratch=()):
    return pl.pallas_call(
        kernel,
        in_specs=specs,
        out_specs=[VM] * len(outs),
        out_shape=[jax.ShapeDtypeStruct(shape, dtype) for shape, dtype in outs],
        scratch_shapes=list(scratch),
        compiler_params=pltpu.CompilerParams(vmem_limit_bytes=24 << 20),
    )


def in_hbm(value):
    return pltpu.with_memory_space_constraint(value, pltpu.MemorySpace.HBM)


def mm(left, right):
    return jnp.dot(left, right, precision=lax.Precision.HIGHEST, preferred_element_type=F32)


def nt(left, right):
    return lax.dot_general(
        left, right, (((1,), (1,)), ((), ())), precision=lax.Precision.HIGHEST, preferred_element_type=F32
    )


def split(value):
    high = value.astype(BF16)
    return high, (value - high.astype(F32)).astype(BF16)


def mm3(left, right):
    lh, ll = split(left)
    rh, rl = split(right)
    n = left.shape[0]
    both = jnp.dot(jnp.concatenate([lh, ll], axis=0), rh, preferred_element_type=F32)
    return both[:n] + both[n:] + jnp.dot(lh, rl, preferred_element_type=F32)


def nt3(high, low, right):
    dims = (((1,), (1,)), ((), ()))
    n = high.shape[0]
    left = jnp.concatenate([high, low], axis=0)
    both = sum(lax.dot_general(left, part, dims, preferred_element_type=F32) for part in split(right))
    return both[:n] + both[n:]


def rows(parts):
    return jnp.concatenate(parts, axis=0)


def lanes(parts):
    return jnp.concatenate(parts, axis=1)


def halo_lanes(refs, first, last):
    return lanes([ref[slot, first:last] for ref in refs for slot in range(ref.shape[0])])


def put_sources(xs, at, value):
    n, width = value.shape[0], xs.shape[2]
    for t in range(value.shape[1] // width):
        high, low = split(value[:, t * width : (t + 1) * width])
        xs[at + t, :n] = high
        xs[at + t, n:] = low


def apply_pair(xs, cols, w_high, w_low, k_out, m_out):
    tiles, blocks = cols.shape
    width = xs.shape[2]
    n = xs.shape[1] // 2
    for i in range(tiles):
        lhs = lanes([xs[cols[i, b]] for b in range(blocks)])
        both = jnp.dot(lhs, w_high[i], preferred_element_type=F32)
        low = jnp.dot(lhs[:n], w_low[i], preferred_element_type=F32)
        result = both[:n] + both[n:] + low
        k_out[:, i * width : (i + 1) * width] = result[:, :width]
        m_out[:, i * width : (i + 1) * width] = result[:, width:]


def apply_iface(xs, cols, w_high, w_low, tile, n):
    low_at = xs.shape[1] // 2
    width = xs.shape[2]
    blocks = range(cols.shape[1])
    lhs = rows([lanes([xs[cols[tile, b], at : at + n] for b in blocks]) for at in (0, low_at)])
    both = jnp.dot(lhs, w_high[tile], preferred_element_type=F32)
    low = jnp.dot(lhs[:n], w_low[tile], preferred_element_type=F32)
    result = both[:n] + both[n:] + low
    return result[:, :width], result[:, width:]


def lanes_of(tile, width):
    return pl.ds(pl.multiple_of(tile * width, width), width)


def send_tiles(iface, outgoing, at, ref):
    width = outgoing.shape[2]
    n = ref.shape[0]
    for slot in range(outgoing.shape[0]):
        start = pl.multiple_of(iface[slot] * width, width)
        outgoing[slot, at : at + n] = ref[:, pl.ds(start, width)]


def lane_row(shape):
    return lax.broadcasted_iota(jnp.int32, shape, 1), lax.broadcasted_iota(jnp.int32, shape, 0)


def blocks_of(summed, n):
    square = rows([summed, jnp.zeros((MAT - n, MAT), F32)])
    turned = square.T
    return [turned[k * n : (k + 1) * n] for k in range(MAT // n)]


def inverse_chols(first, second):
    n = first.shape[0]
    shape = first.shape
    lane, row = lane_row(shape)
    half = MAT // 2
    columns = [
        jnp.where(
            lane < half,
            jnp.broadcast_to(first[:, j : j + 1], shape),
            jnp.broadcast_to(second[:, j : j + 1], shape),
        )
        for j in range(n)
    ]
    inverse = jnp.where(lane % half == row, 1.0, 0.0)
    pivots = jnp.ones(shape, F32)
    for k in range(n):
        pivot = columns[k][k : k + 1, :]
        pivots = jnp.where(row == k, pivot, pivots)
        if k == n - 1:
            break
        factor = jnp.where(row > k, columns[k], 0.0) * (1.0 / pivot)
        for j in range(k + 1, n):
            columns[j] = columns[j] - factor * columns[j][k : k + 1, :]
        inverse = inverse - factor * inverse[k : k + 1, :]
    inverse = inverse * lax.rsqrt(pivots)
    return [jnp.where(lane < n, value, 0.0) for value in (inverse, pltpu.roll(inverse, half, 1))]


def diagonal(a):
    lane, row = lane_row(a.shape)
    return jnp.sum(jnp.where(lane == row, a, 0.0), axis=1, keepdims=True)


def k_first(iface_hbm, basis_hbm, outgoing, iface, basis, sems):
    copies = [
        pltpu.make_async_copy(iface_hbm, iface, sems.at[0]),
        pltpu.make_async_copy(basis_hbm, basis, sems.at[1]),
    ]
    for copy in copies:
        copy.start()
    for copy in copies:
        copy.wait()
    send_tiles(iface, outgoing, 0, basis)


def make_prep(count):
    def k_prep(part_hbm, slot_hbm, k_hbm, m_hbm, w_high, w_low, inv_d, cols, k, m, part_in, slot_in, sems):
        tiles, blocks, width, _ = k.shape
        pattern = [
            pltpu.make_async_copy(source, target, sems.at[which, tiles])
            for which, (source, target) in enumerate(((part_hbm, part_in), (slot_hbm, slot_in)))
        ]
        for copy in pattern:
            copy.start()
        copies = []
        for i in range(tiles):
            pair = [
                pltpu.make_async_copy(source.at[i], target.at[i], sems.at[which, i])
                for which, (source, target) in enumerate(((k_hbm, k), (m_hbm, m)))
            ]
            for copy in pair:
                copy.start()
            copies.append(pair)
        parts = lax.axis_size("parts")
        me = lax.axis_index("parts")
        for copy in pattern:
            copy.wait()
        part, slot = part_in[...], slot_in[...]
        remote = jnp.where(part == me ^ 1, 0, jnp.where(part == (me + parts // 2) % parts, count, 2 * count))
        cols[...] = jnp.where(part == me, slot, tiles + remote + slot)
        row = lax.broadcasted_iota(jnp.int32, (width, width), 0)
        lane = lax.broadcasted_iota(jnp.int32, (width, width), 1)
        for i in range(tiles):
            for which, source in enumerate((k, m)):
                copies[i][which].wait()
                for b in range(blocks):
                    high, low = split(source[i, b].T)
                    w_high[i, b * width : (b + 1) * width, which * width : (which + 1) * width] = high
                    w_low[i, b * width : (b + 1) * width, which * width : (which + 1) * width] = low
            diag = jnp.sum(jnp.where(row == lane, k[i, 0], 0.0), axis=0, keepdims=True)
            inv_d[:, i * width : (i + 1) * width] = 1.0 / diag

    return k_prep


def fill_blocks(out, value):
    for device in range(out.shape[0]):
        out[device] = value


def total(ref):
    value = ref[0]
    for device in range(1, ref.shape[0]):
        value = value + ref[device]
    return value


def fold(value):
    half = value.shape[0] // 2
    return value[:half] + pltpu.roll(value[half:], MAT // 2, 1)


def unfold(value):
    lane, _ = lane_row(value.shape)
    keep = lane < MAT // 2
    return rows([jnp.where(keep, value, 0.0), jnp.where(keep, pltpu.roll(value, MAT // 2, 1), 0.0)])


def pack_rows(value):
    lane, row = lane_row(value.shape)
    m = value.shape[0] // 2
    n = MAT // m
    shift = n
    while shift < MAT:
        value = value + pltpu.roll(value, shift, 1)
        shift *= 2
    value = jnp.where(lane // n == row % m, value, 0.0)
    return [jnp.sum(value[k * m : (k + 1) * m], axis=0, keepdims=True) for k in range(2)]


def unpack_rows(pair, m):
    value = rows([jnp.broadcast_to(part, (m, MAT)) for part in pair])
    lane, row = lane_row(value.shape)
    n = MAT // m
    value = jnp.where(lane // n == row % m, value, 0.0)
    shift = n
    while shift < MAT:
        value = value + pltpu.roll(value, shift, 1)
        shift *= 2
    return value


def make_kernels(n, scale):
    def put_small(ref, k, value):
        ref[k * n : (k + 1) * n] = jnp.broadcast_to(value, (n, MAT)) if value.shape[1] == 1 else lanes(
            [value, jnp.zeros((n, MAT - n), F32)]
        )

    def get_small(ref, k):
        return ref[k * n : (k + 1) * n, :n]

    def k_a(cols, iface, basis, h_a, h_f, h_b, w_high, w_low, inv_d, kb, mb, u, outgoing, grams, xs):
        put_sources(xs, 0, basis[...])
        put_sources(xs, basis.shape[1] // xs.shape[2], halo_lanes((h_a, h_f, h_b), 0, n))
        apply_pair(xs, cols, w_high, w_low, kb, mb)
        d = inv_d[...]
        u[:n] = kb[...] * d
        u[n:] = mb[...] * d
        send_tiles(iface, outgoing, 0, u)
        right = rows([basis[...], u[...], kb[...], mb[...], jnp.zeros((MAT - 5 * n, basis.shape[1]), F32)])
        both = nt3(*split(rows([basis[...], mb[...]])), right) * scale
        lane, row = lane_row((n, MAT))
        chosen = jnp.where(lane < 3 * n, both[:n], both[n:])
        mass = pltpu.roll(chosen, MAT - 4 * n, 1)
        packed = jnp.where((lane < n) & (lane > row), mass, jnp.where(lane < 4 * n, chosen, 0.0))
        mass_diag = jnp.sum(jnp.where((lane == row) & (lane < n), mass, 0.0), axis=0, keepdims=True)
        packed = fold(packed)
        for device in range(grams.shape[0]):
            grams[device, : n // 2, 0, :] = packed
            grams[device, n // 2] = mass_diag

    def k_b0(red, kb, mb, u, ko_out, mo_out, c0_out, words, small, theta_out):
        packed, mass_diag = red[0, : n // 2, 0, :], red[0, n // 2]
        for device in range(1, red.shape[0]):
            packed = packed + red[device, : n // 2, 0, :]
            mass_diag = mass_diag + red[device, n // 2]
        packed = unfold(packed)
        turned, g_u1b, g_u2b, g_km = blocks_of(packed, n)[:4]
        lane, row = lane_row((n, MAT))
        g_bb = jnp.where(lane < n, jnp.where(lane <= row, packed, turned), 0.0)
        g_mm = jnp.where(lane == row, mass_diag, jnp.where(lane > row, packed, turned))
        g_mm = jnp.where(lane < n, g_mm, 0.0)
        inv_v, inv_c = inverse_chols(g_bb, g_mm)
        lv, lc = inv_v[:, :n], inv_c[:, :n]
        left_cross = mm(lv, g_km[:, :n])
        cross = nt(left_cross, lc)
        cross_diag = jnp.sum(left_cross * lc, axis=1, keepdims=True)
        theta = cross_diag * (diagonal(inv_c) / diagonal(inv_v))
        g1 = mm3(lv, u[:n])
        both = mm3(rows([lv, lc]), u[n:])
        g2, f1 = both[:n], both[n:]
        for k, value in ((0, f1), (3, g1), (4, g2)):
            words[k * n : (k + 1) * n] = value
        c0_out[...] = -relax * (g1 - theta * g2)
        ko_out[...] = mm3(lv, kb[...])
        mo_out[...] = mm3(lv, mb[...])
        e1 = nt(mm(lv, g_u1b[:, :n]), lv)
        e2 = nt(mm(lv, g_u2b[:, :n]), lv)
        right = -relax * (e1 - theta * e2)
        for k, value in enumerate((cross, g_mm[:, :n], e1, e2, g_u2b[:, :n], theta, lv, lc, right)):
            put_small(small, k, value)
        theta_out[...] = jnp.sum(jnp.where(lane == row, theta, 0.0), axis=0, keepdims=True)[:, :n]

    def k_b1(
        cols, iface, h_a, h_f, h_b, w_high, w_low, inv_d, ko, mo, c0, words_in, small, words_halo, outgoing, xs
    ):
        lv, lc, right = (get_small(small, k) for k in (6, 7, 8))
        theta = small[5 * n : 6 * n, :1]
        g1 = mm3(lv, halo_lanes((h_a, h_f, h_b), 0, n))
        both = mm3(rows([lv, lc]), halo_lanes((h_a, h_f, h_b), n, 2 * n))
        g2, f1 = both[:n], both[n:]
        put_sources(xs, 0, rows([c0[...], words_in[:n]]))
        put_sources(xs, c0.shape[1] // xs.shape[2], rows([-relax * (g1 - theta * g2), f1]))
        for k, value in ((0, f1), (1, g1), (2, g2)):
            words_halo[k * n : (k + 1) * n] = value
        coef = lanes([right, -theta * right])
        for slot in range(outgoing.shape[0]):
            tile = iface[slot]
            at = lanes_of(tile, xs.shape[2])
            k_tile, m_tile = apply_iface(xs, cols, w_high, w_low, tile, n)
            image = k_tile - theta * m_tile - mm3(coef, rows([ko[:, at], mo[:, at]]))
            outgoing[slot] = 2.0 * c0[:, at] - relax * inv_d[:, at] * image

    def k_b2(
        cols, xs, w_high, w_low, inv_d, ko, mo, c0, words_in, small, p_out, image_out, words, kf_out, res
    ):
        right = get_small(small, 8)
        theta = small[5 * n : 6 * n, :1]
        apply_pair(xs, cols, w_high, w_low, res.at[0], res.at[1])
        d = inv_d[...]
        image = res[0, :n] - theta * res[1, :n] - mm3(lanes([right, -theta * right]), rows([ko[...], mo[...]]))
        image_out[...] = image
        kf_out[:n] = res[0, n:]
        kf_out[n:] = res[1, n:]
        words[:n] = words_in[:n]
        words[n : 2 * n] = res[0, n:] * d
        words[2 * n : 3 * n] = res[1, n:] * d
        words[3 * n :] = words_in[3 * n :]
        p_out[...] = 2.0 * c0[...] - relax * d * image

    def k_c0(small, basis, mb, image0, kf, p, words, v_out, tests_high, tests_low, small_b, part):
        lv, lc = get_small(small, 6), get_small(small, 7)
        v = mm3(lv, basis[...])
        v_out[...] = v
        high, low = split(rows([mm3(lc, mb[...]), v]))
        tests_high[...] = high
        tests_low[...] = low
        mass = nt(mm(lv, get_small(small, 1)), lc)
        ef = nt(mm(lc, get_small(small, 4)), lv)
        for k, value in enumerate((mass, ef, mm(ef, get_small(small, 0)), mm(ef, mass))):
            put_small(small_b, k, value)
        right = rows([image0[...], kf[...], p[...], words[n : 3 * n], jnp.zeros((2 * n, p.shape[1]), F32)])
        both = nt3(high, low, right) * scale
        lane, _ = lane_row((n, MAT))
        part[...] = jnp.where(lane < 3 * n, both[:n], both[n:])

    def half(cols, p, halo, small, c0, w_high, w_low, inv_d, tests_high, tests_low, xs, res):
        put_sources(xs, 0, p)
        put_sources(xs, p.shape[1] // xs.shape[2], halo)
        apply_pair(xs, cols, w_high, w_low, res.at[0], res.at[1])
        theta = small[5 * n : 6 * n, :1]
        image = res[0] - theta * res[1]
        fresh = p + c0[...] - relax * inv_d[...] * image
        both = nt3(tests_high[...], tests_low[...], rows([image, fresh])) * scale
        both = lanes([both, jnp.zeros((2 * n, MAT - 2 * n), F32)])
        lane, _ = lane_row((n, MAT))
        return fresh, jnp.where(lane < n, both[:n], both[n:])

    def k_c1(
        cols, iface, p, h_a, h_f, h_b, c0, words, small, part, pair, tests_high, tests_low, w_high, w_low, inv_d,
        p_out, outgoing, grams, xs, res,
    ):
        fresh, added = half(
            cols, p[...], halo_lanes((h_a, h_f, h_b), 0, n), small, c0, w_high, w_low, inv_d,
            tests_high, tests_low, xs, res,
        )
        p_out[...] = fresh
        send_tiles(iface, outgoing, 0, p_out)
        send_tiles(iface, outgoing, n, words.at[n : 3 * n])
        chip = part[...] + pair[...]
        chip = jnp.where(lax.axis_index("parts") % 2 == 0, chip, pltpu.roll(chip, MAT - 3 * n, 1))
        lane, _ = lane_row((n, MAT))
        first = jnp.where(lane < 3 * n, chip, pltpu.roll(added, 3 * n, 1))
        packed = fold(jnp.where(lane < 4 * n, first, 0.0))
        fifth = pack_rows(jnp.where(lane < n, pltpu.roll(added, MAT - n, 1), 0.0))
        for device in range(grams.shape[0]):
            grams[device, : n // 2, 0, :] = packed
            for k in range(2):
                grams[device, n // 2 + k] = fifth[k]

    def solve(small, small_b, kf_test, mf_test, g_left, g_p, g_a):
        cross, mass, ef = get_small(small, 0), get_small(small_b, 0), get_small(small_b, 1)
        theta = small[5 * n : 6 * n, :1]
        right = g_p + relax * mm(g_left, ef)
        left = g_a + mm(
            lanes([relax * g_left, -relax * theta * g_left, -g_p, theta * g_p]),
            rows([kf_test, mf_test, cross, mass]),
        )
        return lanes(
            [
                relax * (g_left + left),
                -relax * relax * g_left,
                relax * relax * theta * g_left,
                relax * right,
                -relax * theta * right,
            ]
        )

    def k_d0(red, p, words, small, small_b, c_out, tests_out, onto_v, coefs):
        half_n = n // 2
        sums = [red[device, :half_n, 0, :] for device in range(2)]
        fifth = [red[0, half_n + k] + red[1, half_n + k] for k in range(2)]
        for device in range(2, red.shape[0]):
            sums[device % 2] = sums[device % 2] + red[device, :half_n, 0, :]
            for k in range(2):
                fifth[k] = fifth[k] + red[device, half_n + k]
        lane, _ = lane_row((n, MAT))
        whole = jnp.where(lane < 4 * n, unfold(sums[0]), jnp.where(lane < 5 * n, unpack_rows(fifth, half_n), 0.0))
        g_left, g_kf, g_mf, g_a, g_fresh = (value[:, :n] for value in blocks_of(whole, n)[:5])
        g_p, g_h1, g_h2, g_a_odd = (value[:, :n] for value in blocks_of(unfold(sums[1]), n)[:4])
        g_a = g_a + g_a_odd
        kf_test, mf_test = g_kf - get_small(small_b, 2), g_mf - get_small(small_b, 3)
        coef = solve(small, small_b, kf_test, mf_test, g_left, g_p, g_a)
        c_out[...] = p[...] + mm3(coef, words[...])
        put_small(tests_out, 0, kf_test)
        put_small(tests_out, 1, mf_test)
        onto = (get_small(small_b, 1), g_h1, g_h2, get_small(small, 2), get_small(small, 3))
        for k, value in enumerate(onto):
            put_small(onto_v, k, value)
        coefs[:n] = lanes([coef, jnp.zeros((n, MAT - 5 * n), F32)])
        put_small(coefs, 1, g_fresh + mm(coef, rows(list(onto))))

    def k_d1(
        cols, iface, c_local, coefs, h_a, h_f, h_b, ko, mo, c0, words_halo, small,
        w_high, w_low, inv_d, outgoing, xs,
    ):
        coef, right = coefs[:n, : 5 * n], get_small(coefs, 1)
        theta = small[5 * n : 6 * n, :1]
        around = rows([words_halo[:n], halo_lanes((h_a, h_f, h_b), n, 3 * n), words_halo[n:]])
        c_halo = halo_lanes((h_a, h_f, h_b), 0, n) + mm3(coef, around)
        put_sources(xs, 0, c_local[...])
        put_sources(xs, c_local.shape[1] // xs.shape[2], c_halo)
        onto = lanes([right, -theta * right])
        for slot in range(outgoing.shape[0]):
            tile = iface[slot]
            at = lanes_of(tile, xs.shape[2])
            k_tile, m_tile = apply_iface(xs, cols, w_high, w_low, tile, n)
            image = k_tile - theta * m_tile - mm3(onto, rows([ko[:, at], mo[:, at]]))
            outgoing[slot] = c_local[:, at] + c0[:, at] - relax * inv_d[:, at] * image

    def k_d2(cols, xs, c_local, coefs, ko, mo, c0, small, w_high, w_low, inv_d, p_out, image_out, res):
        right = get_small(coefs, 1)
        theta = small[5 * n : 6 * n, :1]
        apply_pair(xs, cols, w_high, w_low, res.at[0], res.at[1])
        image = res[0] - theta * res[1] - mm3(lanes([right, -theta * right]), rows([ko[...], mo[...]]))
        image_out[...] = image
        p_out[...] = c_local[...] + c0[...] - relax * inv_d[...] * image

    def k_e0(image2, p, tests_high, tests_low, v, words, onto_v, part, last_high, last_low):
        right = rows([image2[...], p[...], jnp.zeros((MAT - 2 * n, p.shape[1]), F32)])
        both = nt3(tests_high[...], tests_low[...], right) * scale
        lane, _ = lane_row((n, MAT))
        part[...] = jnp.where(lane < n, both[:n], both[n:])
        free = words[...] - mm3(onto_v[:, :n], v[...])
        last_high[...], last_low[...] = split(rows([free, v[...]]))

    def k_e1(
        cols, p, h_a, h_f, h_b, c0, small, part, tests_high, tests_low, w_high, w_low, inv_d, p_out, grams, xs, res
    ):
        fresh, added = half(
            cols, p[...], halo_lanes((h_a, h_f, h_b), 0, n), small, c0, w_high, w_low, inv_d,
            tests_high, tests_low, xs, res,
        )
        p_out[...] = fresh
        lane, _ = lane_row((n, MAT))
        both = jnp.where(lane < 2 * n, part[...], pltpu.roll(added, 2 * n, 1))
        fill_blocks(grams, fold(jnp.where(lane < 4 * n, both, 0.0)))

    def k_f(red, p, small, small_b, tests_in, last_high, last_low, out):
        g_left, g_p, g_a, g_fresh = (value[:, :n] for value in blocks_of(unfold(total(red)), n)[:4])
        coef = solve(small, small_b, get_small(tests_in, 0), get_small(tests_in, 1), g_left, g_p, g_a)
        high, low = split(lanes([coef, -g_fresh]))
        both = jnp.dot(rows([high, low]), last_high[...], preferred_element_type=F32)
        low = jnp.dot(high, last_low[...], preferred_element_type=F32)
        out[...] = p[...] + both[:n] + both[n:] + low

    return k_a, k_b0, k_b1, k_b2, k_c0, k_c1, k_d0, k_d1, k_d2, k_e0, k_e1, k_f


def shards(basis, k_tiles, m_tiles, tile_part, tile_slot, iface):
    n, local = basis.shape
    tiles, blocks, width, _ = k_tiles.shape
    count = iface.shape[0]
    parts = lax.axis_size("parts")
    half_way = parts // 2
    scale = 1.0 / (local * parts)
    chip = [(source, source ^ 1) for source in range(parts)]
    other = [(source, (source + 1 if source % 2 else source - 1) % parts) for source in range(parts)]
    far = [(source, (source + half_way) % parts) for source in range(parts)]

    def halo(outgoing):
        got = []
        for pairs in (chip, far, other):
            got.append(lax.ppermute(outgoing, "parts", pairs))
        return got

    def reduced(blocks_out):
        return lax.all_to_all(blocks_out, "parts", 0, 0, tiled=True)

    k_a, k_b0, k_b1, k_b2, k_c0, k_c1, k_d0, k_d1, k_d2, k_e0, k_e1, k_f = make_kernels(n, scale)
    sources = tiles + 3 * count
    xs = lambda m: pltpu.VMEM((sources, 2 * m, width), BF16)
    vec = ((n, local), F32)
    vecs = lambda m: ((m * n, local), F32)
    mats = lambda m: ((m * n, MAT), F32)
    out = lambda m: ((count, m, width), F32)
    grams8 = ((parts, n // 2, MAT), F32)
    res = pltpu.VMEM((2, n, local), F32)

    (outgoing,) = call(
        k_first,
        [out(n)],
        [HBM, HBM],
        [pltpu.VMEM((count,), jnp.int32), pltpu.VMEM((n, local), F32), pltpu.SemaphoreType.DMA((2,))],
    )(in_hbm(iface), in_hbm(basis))
    h0 = halo(outgoing)
    w_high, w_low, inv_d, cols = call(
        make_prep(count),
        [((tiles, blocks * width, 2 * width), BF16)] * 2 + [((1, local), F32), ((tiles, blocks), jnp.int32)],
        [HBM] * 4,
        [pltpu.VMEM(k_tiles.shape, F32)] * 2
        + [pltpu.VMEM((tiles, blocks), jnp.int32)] * 2
        + [pltpu.SemaphoreType.DMA((2, tiles + 1))],
    )(*(in_hbm(value) for value in (tile_part, tile_slot, k_tiles, m_tiles)))
    w = (w_high, w_low, inv_d)
    packed = ((parts, n // 2 + 1, 1, MAT), F32)
    kb, mb, u, outgoing, grams = call(
        k_a, [vec, vec, vecs(2), out(2 * n), packed], [VM, VM] + [VM] * 7, [xs(n)]
    )(cols, iface, basis, *h0, *w)
    red = reduced(grams)
    h1 = halo(outgoing)
    ko, mo, c0, words, small, theta = call(
        k_b0, [vec] * 3 + [vecs(5), mats(9), ((1, n), F32)], [VM] * 4
    )(red, kb, mb, u)
    sources_of = lambda m: ((sources, 2 * m, width), BF16)
    words_halo, outgoing, source = call(
        k_b1, [((3 * n, 3 * count * width), F32), out(n), sources_of(2 * n)], [VM, VM] + [VM] * 11
    )(cols, iface, *h1, *w, ko, mo, c0, words, small)
    h2 = halo(outgoing)
    p1, image0, words, kf = call(
        k_b2, [vec, vec, vecs(5), vecs(2)], [VM] + [VM] * 9, [pltpu.VMEM((2, 2 * n, local), F32)]
    )(cols, source, *w, ko, mo, c0, words, small)
    v, tests_high, tests_low, small_b, part = call(
        k_c0, [vec] + [((2 * n, local), BF16)] * 2 + [mats(4), mats(1)], [VM] * 7
    )(small, basis, mb, image0, kf, p1, words)
    tests = (tests_high, tests_low)
    pair = lax.ppermute(part, "parts", chip)
    packed = ((parts, n // 2 + 2, 1, MAT), F32)
    p2, outgoing, grams = call(k_c1, [vec, out(3 * n), packed], [VM, VM] + [VM] * 14, [xs(n), res])(
        cols, iface, p1, *h2, c0, words, small, part, pair, *tests, *w
    )
    red = reduced(grams)
    h3 = halo(outgoing)
    c2, word_tests, onto_v, coefs = call(k_d0, [vec, mats(2), mats(5), mats(2)], [VM] * 5)(
        red, p2, words, small, small_b
    )
    outgoing, source = call(k_d1, [out(n), sources_of(n)], [VM, VM] + [VM] * 13)(
        cols, iface, c2, coefs, *h3, ko, mo, c0, words_halo, small, *w
    )
    h4 = halo(outgoing)
    p3, image2 = call(k_d2, [vec, vec], [VM] + [VM] * 10, [res])(cols, source, c2, coefs, ko, mo, c0, small, *w)
    part, *last = call(k_e0, [mats(1)] + [((6 * n, local), BF16)] * 2, [VM] * 7)(image2, p3, *tests, v, words, onto_v)
    p4, grams = call(k_e1, [vec, grams8], [VM] + [VM] * 12, [xs(n), res])(cols, p3, *h4, c0, small, part, *tests, *w)
    red = reduced(grams)
    (correct,) = call(k_f, [vec], [VM] * 7)(red, p4, small, small_b, word_tests, *last)
    return (correct, theta.reshape(-1))


def solution(mesh):
    placed = (
        P(None, "parts"),
        P("parts", None, None, None),
        P("parts", None, None, None),
        P("parts", None),
        P("parts", None),
        P("parts"),
    )
    return jax.shard_map(
        shards, mesh=mesh, in_specs=placed, out_specs=(P(None, "parts"), P()), check_vma=False
    )
```

```python
import jax
import jax.numpy as jnp
from jax import lax
from jax.experimental import pallas as pl
from jax.experimental.pallas import tpu as pltpu
from jax.sharding import PartitionSpec as P


relax = 0.4

F32 = jnp.float32
BF16 = jnp.bfloat16
VM = pl.BlockSpec(memory_space=pltpu.VMEM)
HBM = pl.BlockSpec(memory_space=pltpu.MemorySpace.HBM)
MAT = 128


def call(kernel, outs, specs, scratch=()):
    return pl.pallas_call(
        kernel,
        in_specs=specs,
        out_specs=[VM] * len(outs),
        out_shape=[jax.ShapeDtypeStruct(shape, dtype) for shape, dtype in outs],
        scratch_shapes=list(scratch),
        compiler_params=pltpu.CompilerParams(vmem_limit_bytes=24 << 20),
    )


def in_hbm(value):
    return pltpu.with_memory_space_constraint(value, pltpu.MemorySpace.HBM)


def mm(left, right):
    return jnp.dot(left, right, precision=lax.Precision.HIGHEST, preferred_element_type=F32)


def nt(left, right):
    return lax.dot_general(
        left, right, (((1,), (1,)), ((), ())), precision=lax.Precision.HIGHEST, preferred_element_type=F32
    )


def split(value):
    high = value.astype(BF16)
    return high, (value - high.astype(F32)).astype(BF16)


def mm3(left, right):
    lh, ll = split(left)
    rh, rl = split(right)
    n = left.shape[0]
    both = jnp.dot(jnp.concatenate([lh, ll], axis=0), rh, preferred_element_type=F32)
    return both[:n] + both[n:] + jnp.dot(lh, rl, preferred_element_type=F32)


def nt3(high, low, right):
    dims = (((1,), (1,)), ((), ()))
    n = high.shape[0]
    left = jnp.concatenate([high, low], axis=0)
    both = sum(lax.dot_general(left, part, dims, preferred_element_type=F32) for part in split(right))
    return both[:n] + both[n:]


def rows(parts):
    return jnp.concatenate(parts, axis=0)


def lanes(parts):
    return jnp.concatenate(parts, axis=1)


def halo_lanes(refs, first, last):
    return lanes([ref[slot, first:last] for ref in refs for slot in range(ref.shape[0])])


def put_sources(xs, at, value):
    n, width = value.shape[0], xs.shape[2]
    for t in range(value.shape[1] // width):
        high, low = split(value[:, t * width : (t + 1) * width])
        xs[at + t, :n] = high
        xs[at + t, n:] = low


def apply_pair(xs, cols, w_high, w_low, k_out, m_out):
    tiles, blocks = cols.shape
    width = xs.shape[2]
    n = xs.shape[1] // 2
    for i in range(tiles):
        lhs = lanes([xs[cols[i, b]] for b in range(blocks)])
        both = jnp.dot(lhs, w_high[i], preferred_element_type=F32)
        low = jnp.dot(lhs[:n], w_low[i], preferred_element_type=F32)
        result = both[:n] + both[n:] + low
        k_out[:, i * width : (i + 1) * width] = result[:, :width]
        m_out[:, i * width : (i + 1) * width] = result[:, width:]


def apply_iface(xs, cols, w_high, w_low, tile, n):
    low_at = xs.shape[1] // 2
    width = xs.shape[2]
    blocks = range(cols.shape[1])
    lhs = rows([lanes([xs[cols[tile, b], at : at + n] for b in blocks]) for at in (0, low_at)])
    both = jnp.dot(lhs, w_high[tile], preferred_element_type=F32)
    low = jnp.dot(lhs[:n], w_low[tile], preferred_element_type=F32)
    result = both[:n] + both[n:] + low
    return result[:, :width], result[:, width:]


def lanes_of(tile, width):
    return pl.ds(pl.multiple_of(tile * width, width), width)


def send_tiles(iface, outgoing, at, ref):
    width = outgoing.shape[2]
    n = ref.shape[0]
    for slot in range(outgoing.shape[0]):
        start = pl.multiple_of(iface[slot] * width, width)
        outgoing[slot, at : at + n] = ref[:, pl.ds(start, width)]


def lane_row(shape):
    return lax.broadcasted_iota(jnp.int32, shape, 1), lax.broadcasted_iota(jnp.int32, shape, 0)


def blocks_of(summed, n):
    square = rows([summed, jnp.zeros((MAT - n, MAT), F32)])
    turned = square.T
    return [turned[k * n : (k + 1) * n] for k in range(MAT // n)]


def inverse_chols(first, second):
    n = first.shape[0]
    shape = first.shape
    lane, row = lane_row(shape)
    half = MAT // 2
    columns = [
        jnp.where(
            lane < half,
            jnp.broadcast_to(first[:, j : j + 1], shape),
            jnp.broadcast_to(second[:, j : j + 1], shape),
        )
        for j in range(n)
    ]
    inverse = jnp.where(lane % half == row, 1.0, 0.0)
    pivots = jnp.ones(shape, F32)
    for k in range(n):
        pivot = columns[k][k : k + 1, :]
        pivots = jnp.where(row == k, pivot, pivots)
        if k == n - 1:
            break
        factor = jnp.where(row > k, columns[k], 0.0) * (1.0 / pivot)
        for j in range(k + 1, n):
            columns[j] = columns[j] - factor * columns[j][k : k + 1, :]
        inverse = inverse - factor * inverse[k : k + 1, :]
    inverse = inverse * lax.rsqrt(pivots)
    return [jnp.where(lane < n, value, 0.0) for value in (inverse, pltpu.roll(inverse, half, 1))]


def diagonal(a):
    lane, row = lane_row(a.shape)
    return jnp.sum(jnp.where(lane == row, a, 0.0), axis=1, keepdims=True)


def k_first(iface_hbm, basis_hbm, outgoing, iface, basis, sems):
    copies = [
        pltpu.make_async_copy(iface_hbm, iface, sems.at[0]),
        pltpu.make_async_copy(basis_hbm, basis, sems.at[1]),
    ]
    for copy in copies:
        copy.start()
    for copy in copies:
        copy.wait()
    send_tiles(iface, outgoing, 0, basis)


def make_prep(count):
    def k_prep(part_hbm, slot_hbm, k_hbm, m_hbm, w_high, w_low, inv_d, cols, k, m, part_in, slot_in, sems):
        tiles, blocks, width, _ = k.shape
        pattern = [
            pltpu.make_async_copy(source, target, sems.at[which, tiles])
            for which, (source, target) in enumerate(((part_hbm, part_in), (slot_hbm, slot_in)))
        ]
        for copy in pattern:
            copy.start()
        copies = []
        for i in range(tiles):
            pair = [
                pltpu.make_async_copy(source.at[i], target.at[i], sems.at[which, i])
                for which, (source, target) in enumerate(((k_hbm, k), (m_hbm, m)))
            ]
            for copy in pair:
                copy.start()
            copies.append(pair)
        parts = lax.axis_size("parts")
        me = lax.axis_index("parts")
        for copy in pattern:
            copy.wait()
        part, slot = part_in[...], slot_in[...]
        remote = jnp.where(part == me ^ 1, 0, jnp.where(part == (me + parts // 2) % parts, count, 2 * count))
        cols[...] = jnp.where(part == me, slot, tiles + remote + slot)
        row = lax.broadcasted_iota(jnp.int32, (width, width), 0)
        lane = lax.broadcasted_iota(jnp.int32, (width, width), 1)
        for i in range(tiles):
            for which, source in enumerate((k, m)):
                copies[i][which].wait()
                for b in range(blocks):
                    high, low = (part.T for part in split(source[i, b]))
                    w_high[i, b * width : (b + 1) * width, which * width : (which + 1) * width] = high
                    w_low[i, b * width : (b + 1) * width, which * width : (which + 1) * width] = low
            diag = jnp.sum(jnp.where(row == lane, k[i, 0], 0.0), axis=0, keepdims=True)
            inv_d[:, i * width : (i + 1) * width] = 1.0 / diag

    return k_prep


def fill_blocks(out, value):
    for device in range(out.shape[0]):
        out[device] = value


def total(ref):
    value = ref[0]
    for device in range(1, ref.shape[0]):
        value = value + ref[device]
    return value


def fold(value):
    half = value.shape[0] // 2
    return value[:half] + pltpu.roll(value[half:], MAT // 2, 1)


def unfold(value):
    lane, _ = lane_row(value.shape)
    keep = lane < MAT // 2
    return rows([jnp.where(keep, value, 0.0), jnp.where(keep, pltpu.roll(value, MAT // 2, 1), 0.0)])


def pack_rows(value):
    lane, row = lane_row(value.shape)
    m = value.shape[0] // 2
    n = MAT // m
    shift = n
    while shift < MAT:
        value = value + pltpu.roll(value, shift, 1)
        shift *= 2
    value = jnp.where(lane // n == row % m, value, 0.0)
    return [jnp.sum(value[k * m : (k + 1) * m], axis=0, keepdims=True) for k in range(2)]


def unpack_rows(pair, m):
    value = rows([jnp.broadcast_to(part, (m, MAT)) for part in pair])
    lane, row = lane_row(value.shape)
    n = MAT // m
    value = jnp.where(lane // n == row % m, value, 0.0)
    shift = n
    while shift < MAT:
        value = value + pltpu.roll(value, shift, 1)
        shift *= 2
    return value


def make_kernels(n, scale):
    def put_small(ref, k, value):
        ref[k * n : (k + 1) * n] = jnp.broadcast_to(value, (n, MAT)) if value.shape[1] == 1 else lanes(
            [value, jnp.zeros((n, MAT - n), F32)]
        )

    def get_small(ref, k):
        return ref[k * n : (k + 1) * n, :n]

    def k_a(cols, iface, basis, h_a, h_f, h_b, w_high, w_low, inv_d, kb, mb, u, outgoing, grams, xs):
        put_sources(xs, 0, basis[...])
        put_sources(xs, basis.shape[1] // xs.shape[2], halo_lanes((h_a, h_f, h_b), 0, n))
        apply_pair(xs, cols, w_high, w_low, kb, mb)
        d = inv_d[...]
        u[:n] = kb[...] * d
        u[n:] = mb[...] * d
        send_tiles(iface, outgoing, 0, u)
        right = rows([basis[...], u[...], kb[...], mb[...]])
        both = nt3(*split(rows([basis[...], mb[...]])), right) * scale
        both = lanes([both, jnp.zeros((2 * n, MAT - 5 * n), F32)])
        lane, row = lane_row((n, MAT))
        chosen = jnp.where(lane < 3 * n, both[:n], both[n:])
        mass = pltpu.roll(chosen, MAT - 4 * n, 1)
        packed = jnp.where((lane < n) & (lane > row), mass, jnp.where(lane < 4 * n, chosen, 0.0))
        mass_diag = jnp.sum(jnp.where((lane == row) & (lane < n), mass, 0.0), axis=0, keepdims=True)
        packed = fold(packed)
        for device in range(grams.shape[0]):
            grams[device, : n // 2, 0, :] = packed
            grams[device, n // 2] = mass_diag

    def k_b0(red, u, c0_out, words, small, theta_out):
        packed, mass_diag = red[0, : n // 2, 0, :], red[0, n // 2]
        for device in range(1, red.shape[0]):
            packed = packed + red[device, : n // 2, 0, :]
            mass_diag = mass_diag + red[device, n // 2]
        packed = unfold(packed)
        turned, g_u1b, g_u2b, g_km = blocks_of(packed, n)[:4]
        lane, row = lane_row((n, MAT))
        g_bb = jnp.where(lane < n, jnp.where(lane <= row, packed, turned), 0.0)
        g_mm = jnp.where(lane == row, mass_diag, jnp.where(lane > row, packed, turned))
        g_mm = jnp.where(lane < n, g_mm, 0.0)
        inv_v, inv_c = inverse_chols(g_bb, g_mm)
        lv, lc = inv_v[:, :n], inv_c[:, :n]
        left_cross = mm(lv, g_km[:, :n])
        cross = nt(left_cross, lc)
        cross_diag = jnp.sum(left_cross * lc, axis=1, keepdims=True)
        theta = cross_diag * (diagonal(inv_c) / diagonal(inv_v))
        g1 = mm3(lv, u[:n])
        both = mm3(rows([lv, lc]), u[n:])
        g2, f1 = both[:n], both[n:]
        for k, value in ((0, f1), (3, g1), (4, g2)):
            words[k * n : (k + 1) * n] = value
        c0_out[...] = -relax * (g1 - theta * g2)
        e1 = nt(mm(lv, g_u1b[:, :n]), lv)
        e2 = nt(mm(lv, g_u2b[:, :n]), lv)
        right = -relax * (e1 - theta * e2)
        for k, value in enumerate((cross, g_mm[:, :n], e1, e2, g_u2b[:, :n], theta, lv, lc, mm(right, lv))):
            put_small(small, k, value)
        theta_out[...] = jnp.sum(jnp.where(lane == row, theta, 0.0), axis=0, keepdims=True)[:, :n]

    def k_b1(
        cols, iface, h_a, h_f, h_b, w_high, w_low, inv_d, kb, mb, c0, words_in, small, words_halo, outgoing, xs
    ):
        lv, lc, right = (get_small(small, k) for k in (6, 7, 8))
        theta = small[5 * n : 6 * n, :1]
        g1 = mm3(lv, halo_lanes((h_a, h_f, h_b), 0, n))
        both = mm3(rows([lv, lc]), halo_lanes((h_a, h_f, h_b), n, 2 * n))
        g2, f1 = both[:n], both[n:]
        put_sources(xs, 0, rows([c0[...], words_in[:n]]))
        put_sources(xs, c0.shape[1] // xs.shape[2], rows([-relax * (g1 - theta * g2), f1]))
        for k, value in ((0, f1), (1, g1), (2, g2)):
            words_halo[k * n : (k + 1) * n] = value
        coef = lanes([right, -theta * right])
        for slot in range(outgoing.shape[0]):
            tile = iface[slot]
            at = lanes_of(tile, xs.shape[2])
            k_tile, m_tile = apply_iface(xs, cols, w_high, w_low, tile, n)
            image = k_tile - theta * m_tile - mm3(coef, rows([kb[:, at], mb[:, at]]))
            outgoing[slot] = 2.0 * c0[:, at] - relax * inv_d[:, at] * image

    def k_b2(
        cols, xs, w_high, w_low, inv_d, kb, mb, c0, words_in, small, p_out, image_out, words, kf_out, res
    ):
        right = get_small(small, 8)
        theta = small[5 * n : 6 * n, :1]
        apply_pair(xs, cols, w_high, w_low, res.at[0], res.at[1])
        d = inv_d[...]
        image = res[0, :n] - theta * res[1, :n] - mm3(lanes([right, -theta * right]), rows([kb[...], mb[...]]))
        image_out[...] = image
        kf_out[:n] = res[0, n:]
        kf_out[n:] = res[1, n:]
        words[:n] = words_in[:n]
        words[n : 2 * n] = res[0, n:] * d
        words[2 * n : 3 * n] = res[1, n:] * d
        words[3 * n :] = words_in[3 * n :]
        p_out[...] = 2.0 * c0[...] - relax * d * image

    def k_c0(small, basis, mb, image0, kf, p, words, v_out, tests_high, tests_low, small_b, part):
        lv, lc = get_small(small, 6), get_small(small, 7)
        v = mm3(lv, basis[...])
        v_out[...] = v
        high, low = split(rows([mm3(lc, mb[...]), v]))
        tests_high[...] = high
        tests_low[...] = low
        mass = nt(mm(lv, get_small(small, 1)), lc)
        ef = nt(mm(lc, get_small(small, 4)), lv)
        for k, value in enumerate((mass, ef, mm(ef, get_small(small, 0)), mm(ef, mass))):
            put_small(small_b, k, value)
        right = rows([image0[...], kf[...], p[...], words[n : 3 * n], jnp.zeros((2 * n, p.shape[1]), F32)])
        both = nt3(high, low, right) * scale
        lane, _ = lane_row((n, MAT))
        part[...] = jnp.where(lane < 3 * n, both[:n], both[n:])

    def half(cols, p, halo, small, c0, w_high, w_low, inv_d, tests_high, tests_low, xs, res):
        put_sources(xs, 0, p)
        put_sources(xs, p.shape[1] // xs.shape[2], halo)
        apply_pair(xs, cols, w_high, w_low, res.at[0], res.at[1])
        theta = small[5 * n : 6 * n, :1]
        image = res[0] - theta * res[1]
        fresh = p + c0[...] - relax * inv_d[...] * image
        both = nt3(tests_high[...], tests_low[...], rows([image, fresh])) * scale
        both = lanes([both, jnp.zeros((2 * n, MAT - 2 * n), F32)])
        lane, _ = lane_row((n, MAT))
        return fresh, jnp.where(lane < n, both[:n], both[n:])

    def k_c1(
        cols, iface, p, h_a, h_f, h_b, c0, words, small, part, pair, tests_high, tests_low, w_high, w_low, inv_d,
        p_out, outgoing, grams, xs, res,
    ):
        fresh, added = half(
            cols, p[...], halo_lanes((h_a, h_f, h_b), 0, n), small, c0, w_high, w_low, inv_d,
            tests_high, tests_low, xs, res,
        )
        p_out[...] = fresh
        send_tiles(iface, outgoing, 0, p_out)
        send_tiles(iface, outgoing, n, words.at[n : 3 * n])
        chip = part[...] + pair[...]
        chip = jnp.where(lax.axis_index("parts") % 2 == 0, chip, pltpu.roll(chip, MAT - 3 * n, 1))
        lane, _ = lane_row((n, MAT))
        first = jnp.where(lane < 3 * n, chip, pltpu.roll(added, 3 * n, 1))
        packed = fold(jnp.where(lane < 4 * n, first, 0.0))
        fifth = pack_rows(jnp.where(lane < n, pltpu.roll(added, MAT - n, 1), 0.0))
        for device in range(grams.shape[0]):
            grams[device, : n // 2, 0, :] = packed
            for k in range(2):
                grams[device, n // 2 + k] = fifth[k]

    def solve(small, small_b, kf_test, mf_test, g_left, g_p, g_a):
        cross, mass, ef = get_small(small, 0), get_small(small_b, 0), get_small(small_b, 1)
        theta = small[5 * n : 6 * n, :1]
        right = g_p + relax * mm(g_left, ef)
        left = g_a + mm(
            lanes([relax * g_left, -relax * theta * g_left, -g_p, theta * g_p]),
            rows([kf_test, mf_test, cross, mass]),
        )
        return lanes(
            [
                relax * (g_left + left),
                -relax * relax * g_left,
                relax * relax * theta * g_left,
                relax * right,
                -relax * theta * right,
            ]
        )

    def k_d0(red, p, words, small, small_b, c_out, tests_out, onto_v, coefs):
        half_n = n // 2
        sums = [red[device, :half_n, 0, :] for device in range(2)]
        fifth = [red[0, half_n + k] + red[1, half_n + k] for k in range(2)]
        for device in range(2, red.shape[0]):
            sums[device % 2] = sums[device % 2] + red[device, :half_n, 0, :]
            for k in range(2):
                fifth[k] = fifth[k] + red[device, half_n + k]
        lane, _ = lane_row((n, MAT))
        whole = jnp.where(lane < 4 * n, unfold(sums[0]), jnp.where(lane < 5 * n, unpack_rows(fifth, half_n), 0.0))
        g_left, g_kf, g_mf, g_a, g_fresh = (value[:, :n] for value in blocks_of(whole, n)[:5])
        g_p, g_h1, g_h2, g_a_odd = (value[:, :n] for value in blocks_of(unfold(sums[1]), n)[:4])
        g_a = g_a + g_a_odd
        kf_test, mf_test = g_kf - get_small(small_b, 2), g_mf - get_small(small_b, 3)
        coef = solve(small, small_b, kf_test, mf_test, g_left, g_p, g_a)
        c_out[...] = p[...] + mm3(coef, words[...])
        put_small(tests_out, 0, kf_test)
        put_small(tests_out, 1, mf_test)
        onto = (get_small(small_b, 1), g_h1, g_h2, get_small(small, 2), get_small(small, 3))
        for k, value in enumerate(onto):
            put_small(onto_v, k, value)
        coefs[:n] = lanes([coef, jnp.zeros((n, MAT - 5 * n), F32)])
        put_small(coefs, 1, mm(g_fresh, get_small(small, 6)) + mm(coef, mm(rows(list(onto)), get_small(small, 6))))

    def k_d1(
        cols, iface, c_local, coefs, h_a, h_f, h_b, kb, mb, c0, words_halo, small,
        w_high, w_low, inv_d, outgoing, xs,
    ):
        coef, right = coefs[:n, : 5 * n], get_small(coefs, 1)
        theta = small[5 * n : 6 * n, :1]
        around = rows([words_halo[:n], halo_lanes((h_a, h_f, h_b), n, 3 * n), words_halo[n:]])
        c_halo = halo_lanes((h_a, h_f, h_b), 0, n) + mm3(coef, around)
        put_sources(xs, 0, c_local[...])
        put_sources(xs, c_local.shape[1] // xs.shape[2], c_halo)
        onto = lanes([right, -theta * right])
        for slot in range(outgoing.shape[0]):
            tile = iface[slot]
            at = lanes_of(tile, xs.shape[2])
            k_tile, m_tile = apply_iface(xs, cols, w_high, w_low, tile, n)
            image = k_tile - theta * m_tile - mm3(onto, rows([kb[:, at], mb[:, at]]))
            outgoing[slot] = c_local[:, at] + c0[:, at] - relax * inv_d[:, at] * image

    def k_d2(cols, xs, c_local, coefs, kb, mb, c0, small, w_high, w_low, inv_d, p_out, image_out, res):
        right = get_small(coefs, 1)
        theta = small[5 * n : 6 * n, :1]
        apply_pair(xs, cols, w_high, w_low, res.at[0], res.at[1])
        image = res[0] - theta * res[1] - mm3(lanes([right, -theta * right]), rows([kb[...], mb[...]]))
        image_out[...] = image
        p_out[...] = c_local[...] + c0[...] - relax * inv_d[...] * image

    def k_e0(image2, p, tests_high, tests_low, v, words, onto_v, part, last_high, last_low):
        right = rows([image2[...], p[...], jnp.zeros((MAT - 2 * n, p.shape[1]), F32)])
        both = nt3(tests_high[...], tests_low[...], right) * scale
        lane, _ = lane_row((n, MAT))
        part[...] = jnp.where(lane < n, both[:n], both[n:])
        free = words[...] - mm3(onto_v[:, :n], v[...])
        last_high[...], last_low[...] = split(rows([free, v[...]]))

    def k_e1(
        cols, p, h_a, h_f, h_b, c0, small, part, tests_high, tests_low, w_high, w_low, inv_d, p_out, grams, xs, res
    ):
        fresh, added = half(
            cols, p[...], halo_lanes((h_a, h_f, h_b), 0, n), small, c0, w_high, w_low, inv_d,
            tests_high, tests_low, xs, res,
        )
        p_out[...] = fresh
        lane, _ = lane_row((n, MAT))
        both = jnp.where(lane < 2 * n, part[...], pltpu.roll(added, 2 * n, 1))
        fill_blocks(grams, fold(jnp.where(lane < 4 * n, both, 0.0)))

    def k_f(red, p, small, small_b, tests_in, last_high, last_low, out):
        g_left, g_p, g_a, g_fresh = (value[:, :n] for value in blocks_of(unfold(total(red)), n)[:4])
        coef = solve(small, small_b, get_small(tests_in, 0), get_small(tests_in, 1), g_left, g_p, g_a)
        high, low = split(lanes([coef, -g_fresh]))
        both = jnp.dot(rows([high, low]), last_high[...], preferred_element_type=F32)
        low = jnp.dot(high, last_low[...], preferred_element_type=F32)
        out[...] = p[...] + both[:n] + both[n:] + low

    return k_a, k_b0, k_b1, k_b2, k_c0, k_c1, k_d0, k_d1, k_d2, k_e0, k_e1, k_f


def shards(basis, k_tiles, m_tiles, tile_part, tile_slot, iface):
    n, local = basis.shape
    tiles, blocks, width, _ = k_tiles.shape
    count = iface.shape[0]
    parts = lax.axis_size("parts")
    half_way = parts // 2
    scale = 1.0 / (local * parts)
    chip = [(source, source ^ 1) for source in range(parts)]
    other = [(source, (source + 1 if source % 2 else source - 1) % parts) for source in range(parts)]
    far = [(source, (source + half_way) % parts) for source in range(parts)]

    def halo(outgoing):
        got = []
        for pairs in (chip, far, other):
            got.append(lax.ppermute(outgoing, "parts", pairs))
        return got

    def reduced(blocks_out):
        return lax.all_to_all(blocks_out, "parts", 0, 0, tiled=True)

    k_a, k_b0, k_b1, k_b2, k_c0, k_c1, k_d0, k_d1, k_d2, k_e0, k_e1, k_f = make_kernels(n, scale)
    sources = tiles + 3 * count
    xs = lambda m: pltpu.VMEM((sources, 2 * m, width), BF16)
    vec = ((n, local), F32)
    vecs = lambda m: ((m * n, local), F32)
    mats = lambda m: ((m * n, MAT), F32)
    out = lambda m: ((count, m, width), F32)
    grams8 = ((parts, n // 2, MAT), F32)
    res = pltpu.VMEM((2, n, local), F32)

    (outgoing,) = call(
        k_first,
        [out(n)],
        [HBM, HBM],
        [pltpu.VMEM((count,), jnp.int32), pltpu.VMEM((n, local), F32), pltpu.SemaphoreType.DMA((2,))],
    )(in_hbm(iface), in_hbm(basis))
    h0 = halo(outgoing)
    w_high, w_low, inv_d, cols = call(
        make_prep(count),
        [((tiles, blocks * width, 2 * width), BF16)] * 2 + [((1, local), F32), ((tiles, blocks), jnp.int32)],
        [HBM] * 4,
        [pltpu.VMEM(k_tiles.shape, F32)] * 2
        + [pltpu.VMEM((tiles, blocks), jnp.int32)] * 2
        + [pltpu.SemaphoreType.DMA((2, tiles + 1))],
    )(*(in_hbm(value) for value in (tile_part, tile_slot, k_tiles, m_tiles)))
    w = (w_high, w_low, inv_d)
    packed = ((parts, n // 2 + 1, 1, MAT), F32)
    kb, mb, u, outgoing, grams = call(
        k_a, [vec, vec, vecs(2), out(2 * n), packed], [VM, VM] + [VM] * 7, [xs(n)]
    )(cols, iface, basis, *h0, *w)
    red = reduced(grams)
    h1 = halo(outgoing)
    c0, words, small, theta = call(k_b0, [vec, vecs(5), mats(9), ((1, n), F32)], [VM] * 2)(red, u)
    sources_of = lambda m: ((sources, 2 * m, width), BF16)
    words_halo, outgoing, source = call(
        k_b1, [((3 * n, 3 * count * width), F32), out(n), sources_of(2 * n)], [VM, VM] + [VM] * 11
    )(cols, iface, *h1, *w, kb, mb, c0, words, small)
    h2 = halo(outgoing)
    p1, image0, words, kf = call(
        k_b2, [vec, vec, vecs(5), vecs(2)], [VM] + [VM] * 9, [pltpu.VMEM((2, 2 * n, local), F32)]
    )(cols, source, *w, kb, mb, c0, words, small)
    v, tests_high, tests_low, small_b, part = call(
        k_c0, [vec] + [((2 * n, local), BF16)] * 2 + [mats(4), mats(1)], [VM] * 7
    )(small, basis, mb, image0, kf, p1, words)
    tests = (tests_high, tests_low)
    pair = lax.ppermute(part, "parts", chip)
    packed = ((parts, n // 2 + 2, 1, MAT), F32)
    p2, outgoing, grams = call(k_c1, [vec, out(3 * n), packed], [VM, VM] + [VM] * 14, [xs(n), res])(
        cols, iface, p1, *h2, c0, words, small, part, pair, *tests, *w
    )
    red = reduced(grams)
    h3 = halo(outgoing)
    c2, word_tests, onto_v, coefs = call(k_d0, [vec, mats(2), mats(5), mats(2)], [VM] * 5)(
        red, p2, words, small, small_b
    )
    outgoing, source = call(k_d1, [out(n), sources_of(n)], [VM, VM] + [VM] * 13)(
        cols, iface, c2, coefs, *h3, kb, mb, c0, words_halo, small, *w
    )
    h4 = halo(outgoing)
    p3, image2 = call(k_d2, [vec, vec], [VM] + [VM] * 10, [res])(cols, source, c2, coefs, kb, mb, c0, small, *w)
    part, *last = call(k_e0, [mats(1)] + [((6 * n, local), BF16)] * 2, [VM] * 7)(image2, p3, *tests, v, words, onto_v)
    p4, grams = call(k_e1, [vec, grams8], [VM] + [VM] * 12, [xs(n), res])(cols, p3, *h4, c0, small, part, *tests, *w)
    red = reduced(grams)
    (correct,) = call(k_f, [vec], [VM] * 7)(red, p4, small, small_b, word_tests, *last)
    return (correct, theta.reshape(-1))


def solution(mesh):
    placed = (
        P(None, "parts"),
        P("parts", None, None, None),
        P("parts", None, None, None),
        P("parts", None),
        P("parts", None),
        P("parts"),
    )
    return jax.shard_map(
        shards, mesh=mesh, in_specs=placed, out_specs=(P(None, "parts"), P()), check_vma=False
    )
```

```python
import jax
import jax.numpy as jnp
from jax import lax
from jax.experimental import pallas as pl
from jax.experimental.pallas import tpu as pltpu
from jax.sharding import PartitionSpec as P


relax = 0.4

F32 = jnp.float32
BF16 = jnp.bfloat16
VM = pl.BlockSpec(memory_space=pltpu.VMEM)
HBM = pl.BlockSpec(memory_space=pltpu.MemorySpace.HBM)
MAT = 128


def call(kernel, outs, specs, scratch=()):
    return pl.pallas_call(
        kernel,
        in_specs=specs,
        out_specs=[VM] * len(outs),
        out_shape=[jax.ShapeDtypeStruct(shape, dtype) for shape, dtype in outs],
        scratch_shapes=list(scratch),
        compiler_params=pltpu.CompilerParams(vmem_limit_bytes=24 << 20),
    )


def in_hbm(value):
    return pltpu.with_memory_space_constraint(value, pltpu.MemorySpace.HBM)


def mm(left, right):
    return jnp.dot(left, right, precision=lax.Precision.HIGHEST, preferred_element_type=F32)


def nt(left, right):
    return lax.dot_general(
        left, right, (((1,), (1,)), ((), ())), precision=lax.Precision.HIGHEST, preferred_element_type=F32
    )


def split(value):
    high = value.astype(BF16)
    return high, (value - high.astype(F32)).astype(BF16)


def mm3(left, right):
    lh, ll = split(left)
    rh, rl = split(right)
    n = left.shape[0]
    both = jnp.dot(jnp.concatenate([lh, ll], axis=0), rh, preferred_element_type=F32)
    return both[:n] + both[n:] + jnp.dot(lh, rl, preferred_element_type=F32)


def nt3(high, low, right):
    dims = (((1,), (1,)), ((), ()))
    n = high.shape[0]
    left = jnp.concatenate([high, low], axis=0)
    both = sum(lax.dot_general(left, part, dims, preferred_element_type=F32) for part in split(right))
    return both[:n] + both[n:]


def rows(parts):
    return jnp.concatenate(parts, axis=0)


def lanes(parts):
    return jnp.concatenate(parts, axis=1)


def halo_lanes(refs, first, last):
    return lanes([ref[slot, first:last] for ref in refs for slot in range(ref.shape[0])])


def put_sources(xs, at, value):
    n, width = value.shape[0], xs.shape[2]
    for t in range(value.shape[1] // width):
        high, low = split(value[:, t * width : (t + 1) * width])
        xs[at + t, :n] = high
        xs[at + t, n:] = low


def apply_pair(xs, cols, w_high, w_low, k_out, m_out):
    tiles, blocks = cols.shape
    width = xs.shape[2]
    n = xs.shape[1] // 2
    for i in range(tiles):
        lhs = lanes([xs[cols[i, b]] for b in range(blocks)])
        both = jnp.dot(lhs, w_high[i], preferred_element_type=F32)
        low = jnp.dot(lhs[:n], w_low[i], preferred_element_type=F32)
        result = both[:n] + both[n:] + low
        k_out[:, i * width : (i + 1) * width] = result[:, :width]
        m_out[:, i * width : (i + 1) * width] = result[:, width:]


def apply_iface(xs, cols, w_high, w_low, tile, n):
    low_at = xs.shape[1] // 2
    width = xs.shape[2]
    blocks = range(cols.shape[1])
    lhs = rows([lanes([xs[cols[tile, b], at : at + n] for b in blocks]) for at in (0, low_at)])
    both = jnp.dot(lhs, w_high[tile], preferred_element_type=F32)
    low = jnp.dot(lhs[:n], w_low[tile], preferred_element_type=F32)
    result = both[:n] + both[n:] + low
    return result[:, :width], result[:, width:]


def lanes_of(tile, width):
    return pl.ds(pl.multiple_of(tile * width, width), width)


def send_tiles(iface, outgoing, at, ref):
    width = outgoing.shape[2]
    n = ref.shape[0]
    for slot in range(outgoing.shape[0]):
        start = pl.multiple_of(iface[slot] * width, width)
        outgoing[slot, at : at + n] = ref[:, pl.ds(start, width)]


def lane_row(shape):
    return lax.broadcasted_iota(jnp.int32, shape, 1), lax.broadcasted_iota(jnp.int32, shape, 0)


def blocks_of(summed, n):
    square = rows([summed, jnp.zeros((MAT - n, MAT), F32)])
    turned = square.T
    return [turned[k * n : (k + 1) * n] for k in range(MAT // n)]


def inverse_chols(first, second):
    n = first.shape[0]
    shape = first.shape
    lane, row = lane_row(shape)
    half = MAT // 2
    columns = [
        jnp.where(
            lane < half,
            jnp.broadcast_to(first[:, j : j + 1], shape),
            jnp.broadcast_to(second[:, j : j + 1], shape),
        )
        for j in range(n)
    ]
    inverse = jnp.where(lane % half == row, 1.0, 0.0)
    pivots = jnp.ones(shape, F32)
    for k in range(n):
        pivot = columns[k][k : k + 1, :]
        pivots = jnp.where(row == k, pivot, pivots)
        if k == n - 1:
            break
        factor = jnp.where(row > k, columns[k], 0.0) * (1.0 / pivot)
        for j in range(k + 1, n):
            columns[j] = columns[j] - factor * columns[j][k : k + 1, :]
        inverse = inverse - factor * inverse[k : k + 1, :]
    inverse = inverse * lax.rsqrt(pivots)
    return [jnp.where(lane < n, value, 0.0) for value in (inverse, pltpu.roll(inverse, half, 1))]


def diagonal(a):
    lane, row = lane_row(a.shape)
    return jnp.sum(jnp.where(lane == row, a, 0.0), axis=1, keepdims=True)


def k_first(iface_hbm, basis_hbm, outgoing, iface, basis, sems):
    copies = [
        pltpu.make_async_copy(iface_hbm, iface, sems.at[0]),
        pltpu.make_async_copy(basis_hbm, basis, sems.at[1]),
    ]
    for copy in copies:
        copy.start()
    for copy in copies:
        copy.wait()
    send_tiles(iface, outgoing, 0, basis)


def make_prep(count):
    def k_prep(part_hbm, slot_hbm, k_hbm, m_hbm, w_high, w_low, inv_d, cols, k, m, part_in, slot_in, sems):
        tiles, blocks, width, _ = k.shape
        pattern = [
            pltpu.make_async_copy(source, target, sems.at[which, tiles])
            for which, (source, target) in enumerate(((part_hbm, part_in), (slot_hbm, slot_in)))
        ]
        for copy in pattern:
            copy.start()
        copies = []
        for i in range(tiles):
            pair = [
                pltpu.make_async_copy(source.at[i], target.at[i], sems.at[which, i])
                for which, (source, target) in enumerate(((k_hbm, k), (m_hbm, m)))
            ]
            for copy in pair:
                copy.start()
            copies.append(pair)
        parts = lax.axis_size("parts")
        me = lax.axis_index("parts")
        for copy in pattern:
            copy.wait()
        part, slot = part_in[...], slot_in[...]
        remote = jnp.where(part == me ^ 1, 0, jnp.where(part == (me + parts // 2) % parts, count, 2 * count))
        cols[...] = jnp.where(part == me, slot, tiles + remote + slot)
        row = lax.broadcasted_iota(jnp.int32, (width, width), 0)
        lane = lax.broadcasted_iota(jnp.int32, (width, width), 1)
        for i in range(tiles):
            for which, source in enumerate((k, m)):
                copies[i][which].wait()
                for b in range(blocks):
                    high, low = (part.T for part in split(source[i, b]))
                    w_high[i, b * width : (b + 1) * width, which * width : (which + 1) * width] = high
                    w_low[i, b * width : (b + 1) * width, which * width : (which + 1) * width] = low
            diag = jnp.sum(jnp.where(row == lane, k[i, 0], 0.0), axis=0, keepdims=True)
            inv_d[:, i * width : (i + 1) * width] = 1.0 / diag

    return k_prep


def fill_blocks(out, value):
    for device in range(out.shape[0]):
        out[device] = value


def total(ref):
    value = ref[0]
    for device in range(1, ref.shape[0]):
        value = value + ref[device]
    return value


def fold(value):
    half = value.shape[0] // 2
    return value[:half] + pltpu.roll(value[half:], MAT // 2, 1)


def unfold(value):
    lane, _ = lane_row(value.shape)
    keep = lane < MAT // 2
    return rows([jnp.where(keep, value, 0.0), jnp.where(keep, pltpu.roll(value, MAT // 2, 1), 0.0)])


def pack_rows(value):
    lane, row = lane_row(value.shape)
    m = value.shape[0] // 2
    n = MAT // m
    shift = n
    while shift < MAT:
        value = value + pltpu.roll(value, shift, 1)
        shift *= 2
    value = jnp.where(lane // n == row % m, value, 0.0)
    return [jnp.sum(value[k * m : (k + 1) * m], axis=0, keepdims=True) for k in range(2)]


def unpack_rows(pair, m):
    value = rows([jnp.broadcast_to(part, (m, MAT)) for part in pair])
    lane, row = lane_row(value.shape)
    n = MAT // m
    value = jnp.where(lane // n == row % m, value, 0.0)
    shift = n
    while shift < MAT:
        value = value + pltpu.roll(value, shift, 1)
        shift *= 2
    return value


def make_kernels(n, scale):
    def put_small(ref, k, value):
        ref[k * n : (k + 1) * n] = jnp.broadcast_to(value, (n, MAT)) if value.shape[1] == 1 else lanes(
            [value, jnp.zeros((n, MAT - n), F32)]
        )

    def get_small(ref, k):
        return ref[k * n : (k + 1) * n, :n]

    def k_a(cols, iface, basis, h_a, h_f, h_b, w_high, w_low, inv_d, kb, mb, u, outgoing, grams, xs):
        put_sources(xs, 0, basis[...])
        put_sources(xs, basis.shape[1] // xs.shape[2], halo_lanes((h_a, h_f, h_b), 0, n))
        apply_pair(xs, cols, w_high, w_low, kb, mb)
        d = inv_d[...]
        u[:n] = kb[...] * d
        u[n:] = mb[...] * d
        send_tiles(iface, outgoing, 0, u)
        right = rows([basis[...], u[...], kb[...], mb[...]])
        both = nt3(*split(rows([basis[...], mb[...]])), right) * scale
        both = lanes([both, jnp.zeros((2 * n, MAT - 5 * n), F32)])
        lane, row = lane_row((n, MAT))
        chosen = jnp.where(lane < 3 * n, both[:n], both[n:])
        mass = pltpu.roll(chosen, MAT - 4 * n, 1)
        packed = jnp.where((lane < n) & (lane > row), mass, jnp.where(lane < 4 * n, chosen, 0.0))
        mass_diag = jnp.sum(jnp.where((lane == row) & (lane < n), mass, 0.0), axis=0, keepdims=True)
        packed = fold(packed)
        for device in range(grams.shape[0]):
            grams[device, : n // 2, 0, :] = packed
            grams[device, n // 2] = mass_diag

    def k_b0(red, u, c0_out, words, small, theta_out):
        packed, mass_diag = red[0, : n // 2, 0, :], red[0, n // 2]
        for device in range(1, red.shape[0]):
            packed = packed + red[device, : n // 2, 0, :]
            mass_diag = mass_diag + red[device, n // 2]
        packed = unfold(packed)
        turned, g_u1b, g_u2b, g_km = blocks_of(packed, n)[:4]
        lane, row = lane_row((n, MAT))
        g_bb = jnp.where(lane < n, jnp.where(lane <= row, packed, turned), 0.0)
        g_mm = jnp.where(lane == row, mass_diag, jnp.where(lane > row, packed, turned))
        g_mm = jnp.where(lane < n, g_mm, 0.0)
        inv_v, inv_c = inverse_chols(g_bb, g_mm)
        lv, lc = inv_v[:, :n], inv_c[:, :n]
        left_cross = mm(lv, g_km[:, :n])
        cross = nt(left_cross, lc)
        cross_diag = jnp.sum(left_cross * lc, axis=1, keepdims=True)
        theta = cross_diag * (diagonal(inv_c) / diagonal(inv_v))
        g1 = mm3(lv, u[:n])
        both = mm3(rows([lv, lc]), u[n:])
        g2, f1 = both[:n], both[n:]
        for k, value in ((0, f1), (3, g1), (4, g2)):
            words[k * n : (k + 1) * n] = value
        c0_out[...] = -relax * (g1 - theta * g2)
        e1 = nt(mm(lv, g_u1b[:, :n]), lv)
        e2 = nt(mm(lv, g_u2b[:, :n]), lv)
        right = -relax * (e1 - theta * e2)
        for k, value in enumerate((cross, g_mm[:, :n], e1, e2, g_u2b[:, :n], theta, lv, lc, mm(right, lv))):
            put_small(small, k, value)
        theta_out[...] = jnp.sum(jnp.where(lane == row, theta, 0.0), axis=0, keepdims=True)[:, :n]

    def k_b1(
        cols, iface, h_a, h_f, h_b, w_high, w_low, inv_d, kb, mb, c0, words_in, small, words_halo, outgoing, xs
    ):
        lv, lc, right = (get_small(small, k) for k in (6, 7, 8))
        theta = small[5 * n : 6 * n, :1]
        g1 = mm3(lv, halo_lanes((h_a, h_f, h_b), 0, n))
        both = mm3(rows([lv, lc]), halo_lanes((h_a, h_f, h_b), n, 2 * n))
        g2, f1 = both[:n], both[n:]
        put_sources(xs, 0, rows([c0[...], words_in[:n]]))
        put_sources(xs, c0.shape[1] // xs.shape[2], rows([-relax * (g1 - theta * g2), f1]))
        for k, value in ((0, f1), (1, g1), (2, g2)):
            words_halo[k * n : (k + 1) * n] = value
        coef = lanes([right, -theta * right])
        for slot in range(outgoing.shape[0]):
            tile = iface[slot]
            at = lanes_of(tile, xs.shape[2])
            k_tile, m_tile = apply_iface(xs, cols, w_high, w_low, tile, n)
            image = k_tile - theta * m_tile - mm3(coef, rows([kb[:, at], mb[:, at]]))
            outgoing[slot] = 2.0 * c0[:, at] - relax * inv_d[:, at] * image

    def k_b2(
        cols, xs, w_high, w_low, inv_d, kb, mb, c0, words_in, small, p_out, image_out, words, kf_out, res
    ):
        right = get_small(small, 8)
        theta = small[5 * n : 6 * n, :1]
        apply_pair(xs, cols, w_high, w_low, res.at[0], res.at[1])
        d = inv_d[...]
        image = res[0, :n] - theta * res[1, :n] - mm3(lanes([right, -theta * right]), rows([kb[...], mb[...]]))
        image_out[...] = image
        kf_out[:n] = res[0, n:]
        kf_out[n:] = res[1, n:]
        words[:n] = words_in[:n]
        words[n : 2 * n] = res[0, n:] * d
        words[2 * n : 3 * n] = res[1, n:] * d
        words[3 * n :] = words_in[3 * n :]
        p_out[...] = 2.0 * c0[...] - relax * d * image

    def k_c0(small, basis, mb, image0, kf, p, words, v_out, tests_high, tests_low, small_b, part):
        lv, lc = get_small(small, 6), get_small(small, 7)
        v = mm3(lv, basis[...])
        v_out[...] = v
        high, low = split(rows([mm3(lc, mb[...]), v]))
        tests_high[...] = high
        tests_low[...] = low
        mass = nt(mm(lv, get_small(small, 1)), lc)
        ef = nt(mm(lc, get_small(small, 4)), lv)
        for k, value in enumerate((mass, ef, mm(ef, get_small(small, 0)), mm(ef, mass))):
            put_small(small_b, k, value)
        right = rows([image0[...], kf[...], p[...], words[n : 3 * n], jnp.zeros((2 * n, p.shape[1]), F32)])
        both = nt3(high, low, right) * scale
        lane, _ = lane_row((n, MAT))
        part[...] = jnp.where(lane < 3 * n, both[:n], both[n:])

    def half(cols, p, halo, small, c0, w_high, w_low, inv_d, tests_high, tests_low, xs, res):
        put_sources(xs, 0, p)
        put_sources(xs, p.shape[1] // xs.shape[2], halo)
        apply_pair(xs, cols, w_high, w_low, res.at[0], res.at[1])
        theta = small[5 * n : 6 * n, :1]
        image = res[0] - theta * res[1]
        fresh = p + c0[...] - relax * inv_d[...] * image
        both = nt3(tests_high[...], tests_low[...], rows([image, fresh])) * scale
        both = lanes([both, jnp.zeros((2 * n, MAT - 2 * n), F32)])
        lane, _ = lane_row((n, MAT))
        return fresh, jnp.where(lane < n, both[:n], both[n:])

    def k_c1(
        cols, iface, p, h_a, h_f, h_b, c0, words, small, part, pair, tests_high, tests_low, w_high, w_low, inv_d,
        p_out, outgoing, grams, xs, res,
    ):
        fresh, added = half(
            cols, p[...], halo_lanes((h_a, h_f, h_b), 0, n), small, c0, w_high, w_low, inv_d,
            tests_high, tests_low, xs, res,
        )
        p_out[...] = fresh
        send_tiles(iface, outgoing, 0, p_out)
        send_tiles(iface, outgoing, n, words.at[n : 3 * n])
        chip = part[...] + pair[...]
        chip = jnp.where(lax.axis_index("parts") % 2 == 0, chip, pltpu.roll(chip, MAT - 3 * n, 1))
        lane, _ = lane_row((n, MAT))
        first = jnp.where(lane < 3 * n, chip, pltpu.roll(added, 3 * n, 1))
        packed = fold(jnp.where(lane < 4 * n, first, 0.0))
        fifth = pack_rows(jnp.where(lane < n, pltpu.roll(added, MAT - n, 1), 0.0))
        for device in range(grams.shape[0]):
            grams[device, : n // 2, 0, :] = packed
            for k in range(2):
                grams[device, n // 2 + k] = fifth[k]

    def solve(small, small_b, kf_test, mf_test, g_left, g_p, g_a):
        cross, mass, ef = get_small(small, 0), get_small(small_b, 0), get_small(small_b, 1)
        theta = small[5 * n : 6 * n, :1]
        right = g_p + relax * mm(g_left, ef)
        left = (
            g_a
            + relax * (mm(g_left, kf_test) - theta * mm(g_left, mf_test))
            - (mm(g_p, cross) - theta * mm(g_p, mass))
        )
        return lanes(
            [
                relax * (g_left + left),
                -relax * relax * g_left,
                relax * relax * theta * g_left,
                relax * right,
                -relax * theta * right,
            ]
        )

    def k_d0(red, p, words, small, small_b, c_out, tests_out, onto_v, coefs):
        half_n = n // 2
        sums = [red[device, :half_n, 0, :] for device in range(2)]
        fifth = [red[0, half_n + k] + red[1, half_n + k] for k in range(2)]
        for device in range(2, red.shape[0]):
            sums[device % 2] = sums[device % 2] + red[device, :half_n, 0, :]
            for k in range(2):
                fifth[k] = fifth[k] + red[device, half_n + k]
        lane, _ = lane_row((n, MAT))
        whole = jnp.where(lane < 4 * n, unfold(sums[0]), jnp.where(lane < 5 * n, unpack_rows(fifth, half_n), 0.0))
        g_left, g_kf, g_mf, g_a, g_fresh = (value[:, :n] for value in blocks_of(whole, n)[:5])
        g_p, g_h1, g_h2, g_a_odd = (value[:, :n] for value in blocks_of(unfold(sums[1]), n)[:4])
        g_a = g_a + g_a_odd
        kf_test, mf_test = g_kf - get_small(small_b, 2), g_mf - get_small(small_b, 3)
        coef = solve(small, small_b, kf_test, mf_test, g_left, g_p, g_a)
        c_out[...] = p[...] + mm3(coef, words[...])
        put_small(tests_out, 0, kf_test)
        put_small(tests_out, 1, mf_test)
        onto = (get_small(small_b, 1), g_h1, g_h2, get_small(small, 2), get_small(small, 3))
        for k, value in enumerate(onto):
            put_small(onto_v, k, value)
        coefs[:n] = lanes([coef, jnp.zeros((n, MAT - 5 * n), F32)])
        put_small(coefs, 1, mm(g_fresh, get_small(small, 6)) + mm(coef, mm(rows(list(onto)), get_small(small, 6))))

    def k_d1(
        cols, iface, c_local, coefs, h_a, h_f, h_b, kb, mb, c0, words_halo, small,
        w_high, w_low, inv_d, outgoing, xs,
    ):
        coef, right = coefs[:n, : 5 * n], get_small(coefs, 1)
        theta = small[5 * n : 6 * n, :1]
        around = rows([words_halo[:n], halo_lanes((h_a, h_f, h_b), n, 3 * n), words_halo[n:]])
        c_halo = halo_lanes((h_a, h_f, h_b), 0, n) + mm3(coef, around)
        put_sources(xs, 0, c_local[...])
        put_sources(xs, c_local.shape[1] // xs.shape[2], c_halo)
        onto = lanes([right, -theta * right])
        for slot in range(outgoing.shape[0]):
            tile = iface[slot]
            at = lanes_of(tile, xs.shape[2])
            k_tile, m_tile = apply_iface(xs, cols, w_high, w_low, tile, n)
            image = k_tile - theta * m_tile - mm3(onto, rows([kb[:, at], mb[:, at]]))
            outgoing[slot] = c_local[:, at] + c0[:, at] - relax * inv_d[:, at] * image

    def k_d2(cols, xs, c_local, coefs, kb, mb, c0, small, w_high, w_low, inv_d, p_out, image_out, res):
        right = get_small(coefs, 1)
        theta = small[5 * n : 6 * n, :1]
        apply_pair(xs, cols, w_high, w_low, res.at[0], res.at[1])
        image = res[0] - theta * res[1] - mm3(lanes([right, -theta * right]), rows([kb[...], mb[...]]))
        image_out[...] = image
        p_out[...] = c_local[...] + c0[...] - relax * inv_d[...] * image

    def k_e0(image2, p, tests_high, tests_low, v, words, onto_v, part, last_high, last_low):
        right = rows([image2[...], p[...], jnp.zeros((MAT - 2 * n, p.shape[1]), F32)])
        both = nt3(tests_high[...], tests_low[...], right) * scale
        lane, _ = lane_row((n, MAT))
        part[...] = jnp.where(lane < n, both[:n], both[n:])
        free = words[...] - mm3(onto_v[:, :n], v[...])
        last_high[...], last_low[...] = split(rows([free, v[...]]))

    def k_e1(
        cols, p, h_a, h_f, h_b, c0, small, part, tests_high, tests_low, w_high, w_low, inv_d, p_out, grams, xs, res
    ):
        fresh, added = half(
            cols, p[...], halo_lanes((h_a, h_f, h_b), 0, n), small, c0, w_high, w_low, inv_d,
            tests_high, tests_low, xs, res,
        )
        p_out[...] = fresh
        lane, _ = lane_row((n, MAT))
        both = jnp.where(lane < 2 * n, part[...], pltpu.roll(added, 2 * n, 1))
        fill_blocks(grams, fold(jnp.where(lane < 4 * n, both, 0.0)))

    def k_f(red, p, small, small_b, tests_in, last_high, last_low, out):
        g_left, g_p, g_a, g_fresh = (value[:, :n] for value in blocks_of(unfold(total(red)), n)[:4])
        coef = solve(small, small_b, get_small(tests_in, 0), get_small(tests_in, 1), g_left, g_p, g_a)
        high, low = split(lanes([coef, -g_fresh]))
        both = jnp.dot(rows([high, low]), last_high[...], preferred_element_type=F32)
        low = jnp.dot(high, last_low[...], preferred_element_type=F32)
        out[...] = p[...] + both[:n] + both[n:] + low

    return k_a, k_b0, k_b1, k_b2, k_c0, k_c1, k_d0, k_d1, k_d2, k_e0, k_e1, k_f


def shards(basis, k_tiles, m_tiles, tile_part, tile_slot, iface):
    n, local = basis.shape
    tiles, blocks, width, _ = k_tiles.shape
    count = iface.shape[0]
    parts = lax.axis_size("parts")
    half_way = parts // 2
    scale = 1.0 / (local * parts)
    chip = [(source, source ^ 1) for source in range(parts)]
    other = [(source, (source + 1 if source % 2 else source - 1) % parts) for source in range(parts)]
    far = [(source, (source + half_way) % parts) for source in range(parts)]

    def halo(outgoing):
        got = []
        for pairs in (chip, far, other):
            got.append(lax.ppermute(outgoing, "parts", pairs))
        return got

    def reduced(blocks_out):
        return lax.all_to_all(blocks_out, "parts", 0, 0, tiled=True)

    k_a, k_b0, k_b1, k_b2, k_c0, k_c1, k_d0, k_d1, k_d2, k_e0, k_e1, k_f = make_kernels(n, scale)
    sources = tiles + 3 * count
    xs = lambda m: pltpu.VMEM((sources, 2 * m, width), BF16)
    vec = ((n, local), F32)
    vecs = lambda m: ((m * n, local), F32)
    mats = lambda m: ((m * n, MAT), F32)
    out = lambda m: ((count, m, width), F32)
    grams8 = ((parts, n // 2, MAT), F32)
    res = pltpu.VMEM((2, n, local), F32)

    (outgoing,) = call(
        k_first,
        [out(n)],
        [HBM, HBM],
        [pltpu.VMEM((count,), jnp.int32), pltpu.VMEM((n, local), F32), pltpu.SemaphoreType.DMA((2,))],
    )(in_hbm(iface), in_hbm(basis))
    h0 = halo(outgoing)
    w_high, w_low, inv_d, cols = call(
        make_prep(count),
        [((tiles, blocks * width, 2 * width), BF16)] * 2 + [((1, local), F32), ((tiles, blocks), jnp.int32)],
        [HBM] * 4,
        [pltpu.VMEM(k_tiles.shape, F32)] * 2
        + [pltpu.VMEM((tiles, blocks), jnp.int32)] * 2
        + [pltpu.SemaphoreType.DMA((2, tiles + 1))],
    )(*(in_hbm(value) for value in (tile_part, tile_slot, k_tiles, m_tiles)))
    w = (w_high, w_low, inv_d)
    packed = ((parts, n // 2 + 1, 1, MAT), F32)
    kb, mb, u, outgoing, grams = call(
        k_a, [vec, vec, vecs(2), out(2 * n), packed], [VM, VM] + [VM] * 7, [xs(n)]
    )(cols, iface, basis, *h0, *w)
    red = reduced(grams)
    h1 = halo(outgoing)
    c0, words, small, theta = call(k_b0, [vec, vecs(5), mats(9), ((1, n), F32)], [VM] * 2)(red, u)
    sources_of = lambda m: ((sources, 2 * m, width), BF16)
    words_halo, outgoing, source = call(
        k_b1, [((3 * n, 3 * count * width), F32), out(n), sources_of(2 * n)], [VM, VM] + [VM] * 11
    )(cols, iface, *h1, *w, kb, mb, c0, words, small)
    h2 = halo(outgoing)
    p1, image0, words, kf = call(
        k_b2, [vec, vec, vecs(5), vecs(2)], [VM] + [VM] * 9, [pltpu.VMEM((2, 2 * n, local), F32)]
    )(cols, source, *w, kb, mb, c0, words, small)
    v, tests_high, tests_low, small_b, part = call(
        k_c0, [vec] + [((2 * n, local), BF16)] * 2 + [mats(4), mats(1)], [VM] * 7
    )(small, basis, mb, image0, kf, p1, words)
    tests = (tests_high, tests_low)
    pair = lax.ppermute(part, "parts", chip)
    packed = ((parts, n // 2 + 2, 1, MAT), F32)
    p2, outgoing, grams = call(k_c1, [vec, out(3 * n), packed], [VM, VM] + [VM] * 14, [xs(n), res])(
        cols, iface, p1, *h2, c0, words, small, part, pair, *tests, *w
    )
    red = reduced(grams)
    h3 = halo(outgoing)
    c2, word_tests, onto_v, coefs = call(k_d0, [vec, mats(2), mats(5), mats(2)], [VM] * 5)(
        red, p2, words, small, small_b
    )
    outgoing, source = call(k_d1, [out(n), sources_of(n)], [VM, VM] + [VM] * 13)(
        cols, iface, c2, coefs, *h3, kb, mb, c0, words_halo, small, *w
    )
    h4 = halo(outgoing)
    p3, image2 = call(k_d2, [vec, vec], [VM] + [VM] * 10, [res])(cols, source, c2, coefs, kb, mb, c0, small, *w)
    part, *last = call(k_e0, [mats(1)] + [((6 * n, local), BF16)] * 2, [VM] * 7)(image2, p3, *tests, v, words, onto_v)
    p4, grams = call(k_e1, [vec, grams8], [VM] + [VM] * 12, [xs(n), res])(cols, p3, *h4, c0, small, part, *tests, *w)
    red = reduced(grams)
    (correct,) = call(k_f, [vec], [VM] * 7)(red, p4, small, small_b, word_tests, *last)
    return (correct, theta.reshape(-1))


def solution(mesh):
    placed = (
        P(None, "parts"),
        P("parts", None, None, None),
        P("parts", None, None, None),
        P("parts", None),
        P("parts", None),
        P("parts"),
    )
    return jax.shard_map(
        shards, mesh=mesh, in_specs=placed, out_specs=(P(None, "parts"), P()), check_vma=False
    )
```
